32 devices in a mesh: dp: 8 (over y, x, core), mp: 4 (over z).
Axes of the slice: x: 2, y: 2, z: 4, core: 2. Of those that a mesh axis runs over, the one named last changes fastest.
Arguments:
- tokens: bfloat16 [16384, 1024], P(('dp', 'mp')), may hold values from -6 to 6
- segment_ids: int32 [8, 2048], P('dp'), may hold values from 0 to 5, never falling along the last dimension, each value on 1 to 768 neighbouring positions
- norm1_gain: float32 [1024], replicated, may hold values from 0.5 to 1.5
- norm1_shift: float32 [1024], replicated, may hold values from -3 to 3
- qkv_weight: bfloat16 [1024, 3, 1024], P(None, None, 'mp'), may hold values from -0.1875 to 0.1875
- qv_bias: float32 [2, 1024], P(None, 'mp'), may hold values from -3 to 3
- out_weight: bfloat16 [1024, 1024], P('mp'), may hold values from -0.375 to 0.375
- out_bias: float32 [1024], replicated, may hold values from -3 to 3
- norm2_gain: float32 [1024], replicated, may hold values from 0.5 to 1.5
- norm2_shift: float32 [1024], replicated, may hold values from -3 to 3
- fc1_weight: bfloat16 [1024, 4096], P(None, 'mp'), may hold values from -0.1875 to 0.1875
- fc1_bias: float32 [4096], P('mp'), may hold values from -3 to 3
- fc2_weight: bfloat16 [4096, 1024], P('mp'), may hold values from -0.09375 to 0.09375
- fc2_bias: float32 [1024], replicated, may hold values from -3 to 3
- out_grad: bfloat16 [16384, 1024], P(('dp', 'mp')), may hold values from -6 to 6
Outputs:
- out_tokens: bfloat16 [16384, 1024], P(('dp', 'mp'))
- in_grad: float32 [16384, 1024], P(('dp', 'mp'))
- norm1_gain_grad: float32 [1024], P('mp')
- norm1_shift_grad: float32 [1024], P('mp')
- qkv_weight_grad: float32 [1024, 3, 1024], P(None, None, 'mp')
- qv_bias_grad: float32 [2, 1024], P(None, 'mp')
- out_weight_grad: float32 [1024, 1024], P('mp')
- out_bias_grad: float32 [1024], P('mp')
- norm2_gain_grad: float32 [1024], P('mp')
- norm2_shift_grad: float32 [1024], P('mp')
- fc1_weight_grad: float32 [1024, 4096], P(None, 'mp')
- fc1_bias_grad: float32 [4096], P('mp')
- fc2_weight_grad: float32 [4096, 1024], P('mp')
- fc2_bias_grad: float32 [1024], P('mp')
The draws below stay inside these ranges and needn't reach their ends.
Inputs may be any that keep to these rules, and one draw needn't show every extreme that they name: `segment_ids`: ids never fall along a sequence; a document has 1 to 768 tokens.
All inputs are finite; a program needn't handle non-finite values.
Results may differ from the reference program's by a relative error of at most 0.015.
Values may be sent and summed in bfloat16 or wider, within the bound.
No kernel may reach another device: no remote copies, remote signals or barrier semaphores. Data moves between devices by JAX's collectives and lax.ppermute only.
A program may use at most 320 MiB of HBM per device.

```python
import math
import jax
import jax.numpy as jnp
import numpy as np
from jax import lax

D = 1024
HEADS = 16
HD = 64
FF = 4096
SEQ = 2048
SEQS = 1
DOCS = 6
DOC_MOST = 768
ROWS = 8
TOKENS = 16384
N_DP = 8


def level_of(rng, dims, cuts, least, top_value):
    def one(position, blocks):
        draws = jax.random.uniform(jax.random.fold_in(jax.random.fold_in(rng, 6), position), (blocks,), jnp.float32, least / len(cuts), top_value / len(cuts))
        return jnp.repeat(jnp.exp(draws), dims[position] // blocks).reshape((-1,) + (1,) * (len(dims) - position - 1))

    factor_of = one(*cuts[0])
    for cut in cuts[1:]:
        factor_of = factor_of * one(*cut)
    return factor_of


def profile(number_of, total, bound, skew):
    portions = [(1 << 20) // math.isqrt(standing ** skew) + 1 for standing in range(2, number_of + 1)]
    surplus, given = total - bound - (number_of - 1), [1] * (number_of - 1)
    while surplus > 0:
        movable = [i for i in range(number_of - 1) if given[i] < bound]
        mass, remaining = sum([portions[i] for i in movable]), surplus
        for i in movable:
            more = min(bound - given[i], max(1, remaining * portions[i] // mass), surplus)
            given[i] = given[i] + more
            surplus = surplus - more
    return np.array([bound] + given)


def ragged_sizes(rng, number_of, total, most, slope):
    if number_of == 2:
        one = jax.random.randint(rng, (), max(1, total - most), min(most, total - 1) + 1)
        return jnp.stack([one, total - one])
    sizes = jnp.asarray(profile(number_of, total, most, slope), jnp.int32)
    twos = (number_of - 1) // 2
    source_of, receiver = sizes[1:1 + 2 * twos:2], sizes[2:2 + 2 * twos:2]
    slack = jnp.minimum(source_of - 1, most - receiver)
    moved = jax.random.randint(jax.random.fold_in(rng, 1), (twos,), 0, 1 << 20) % (slack + 1)
    sizes = sizes.at[1:1 + 2 * twos:2].set(source_of - moved).at[2:2 + 2 * twos:2].set(receiver + moved)
    return sizes[jax.random.permutation(jax.random.fold_in(rng, 2), number_of)]


def scatter_about(key, shape, width, bound, shards=(), dtype=jnp.bfloat16):
    array = width * jax.random.normal(key, shape, jnp.float32)
    if shards:
        array = array * level_of(key, shape, shards, -0.22, 0.18)
    return jnp.clip(array, -bound, bound).astype(dtype)


def setup_inputs(seed: int = 0) -> dict:
    key_list = jax.random.split(jax.random.key(seed), 16)
    return {
        "tokens": scatter_about(key_list[0], (TOKENS, D), 1.0, 6.0, ((0, 32),)),
        "segment_ids": jax.vmap(lambda own: jnp.searchsorted(jnp.cumsum(ragged_sizes(own, DOCS, SEQ, DOC_MOST, 0)), jnp.arange(SEQ), side="right"))(jax.random.split(key_list[1], ROWS)).reshape((ROWS, SEQ)).astype(jnp.int32),
        "norm1_gain": jnp.clip(1.0 + 0.1 * jax.random.normal(key_list[2], (D,), jnp.float32), 0.5, 1.5),
        "norm1_shift": scatter_about(key_list[3], (D,), 0.5, 3.0, (), jnp.float32),
        "qkv_weight": scatter_about(key_list[4], (D, 3, D), D ** -0.5, 0.1875, ((2, 4),)),
        "qv_bias": scatter_about(key_list[5], (2, D), 0.5, 3.0, ((1, 4),), jnp.float32),
        "out_weight": scatter_about(key_list[6], (D, D), (D // 4) ** -0.5, 0.375, ((0, 4),)),
        "out_bias": scatter_about(key_list[7], (D,), 0.5, 3.0, (), jnp.float32),
        "norm2_gain": jnp.clip(1.0 + 0.1 * jax.random.normal(key_list[8], (D,), jnp.float32), 0.5, 1.5),
        "norm2_shift": scatter_about(key_list[9], (D,), 0.5, 3.0, (), jnp.float32),
        "fc1_weight": scatter_about(key_list[10], (D, FF), D ** -0.5, 0.1875, ((1, 4),)),
        "fc1_bias": scatter_about(key_list[11], (FF,), 0.5, 3.0, ((0, 4),), jnp.float32),
        "fc2_weight": scatter_about(key_list[12], (FF, D), FF ** -0.5, 0.09375, ((0, 4),)),
        "fc2_bias": scatter_about(key_list[13], (D,), 0.5, 3.0, (), jnp.float32),
        "out_grad": scatter_about(key_list[14], (TOKENS, D), 1.0, 6.0, ((0, 32),)),
    }


@jax.custom_vjp
def low(v):
    return lax.optimization_barrier(v.astype(jnp.bfloat16)).astype(jnp.float32)

@jax.custom_vjp
def low_back(v):
    return v

def low_keep(v):
    return (low(v), None)

def low_pass(kept, grad):
    return (grad,)

def back_keep(v):
    return (v, None)

def back_low(kept, grad):
    return (low(grad),)
low.defvjp(low_keep, low_pass)
low_back.defvjp(back_keep, back_low)
eps = 1e-05
highest = lax.Precision.HIGHEST

def layer_norm(values_in, gain_vec, shift_vec):
    row_mean = lax.optimization_barrier(jnp.mean(values_in, axis=-1, keepdims=True))
    centred = values_in - row_mean
    row_var = lax.optimization_barrier(jnp.mean(centred * centred, axis=-1, keepdims=True))
    return centred * lax.rsqrt(row_var + eps) * gain_vec + shift_vec

def gelu_tanh(values_in):
    return 0.5 * values_in * (1.0 + jnp.tanh(0.7978845608028654 * (values_in + 0.044715 * values_in * values_in * values_in)))

def attend(query, key_rows, value_rows, segment):
    block_rows = min(512, SEQ)
    slopes = jnp.exp2(-8.0 * (jnp.arange(HEADS) + 1).astype(jnp.float32) / HEADS)
    key_at = jnp.arange(SEQ).astype(jnp.int32)

    def one_block(member):
        query_block, offset = member
        query_at = offset + jnp.arange(block_rows).astype(jnp.int32)
        raw_scores = jnp.einsum('qhd,khd->hqk', query_block, key_rows, precision=highest) * HD ** (-0.5)
        distance = (query_at[:, None] - key_at[None, :]).astype(jnp.float32)
        raw_scores = raw_scores - slopes[:, None, None] * distance[None]
        here_seg = lax.dynamic_slice_in_dim(segment, offset, block_rows)
        allowed = (key_at[None, :] <= query_at[:, None]) & (here_seg[:, None] == segment[None, :])
        scores = low_back(jnp.where(allowed[None], raw_scores, -1000000000.0))
        row_top = lax.optimization_barrier(jnp.max(scores, axis=-1, keepdims=True))
        exponent = jnp.exp(scores - row_top)
        weights = low(exponent / lax.optimization_barrier(jnp.sum(exponent, axis=-1, keepdims=True)))
        return jnp.einsum('hqk,khd->qhd', weights, value_rows, precision=highest)
    offsets = (jnp.arange(SEQ // block_rows) * block_rows).astype(jnp.int32)
    blocks = lax.map(jax.checkpoint(one_block), (query.reshape(SEQ // block_rows, block_rows, HEADS, HD), offsets))
    return blocks.reshape(SEQ, HEADS, HD)

def forward(tokens_in, norm1_gain, norm1_shift, qkv_weight, qv_bias, out_weight, out_bias, norm2_gain, norm2_shift, fc1_weight, fc1_bias, fc2_weight, fc2_bias, segments):
    rows_here = tokens_in.shape[0]
    seq_count = rows_here // SEQ
    normed = low(layer_norm(tokens_in, norm1_gain, norm1_shift))
    bias_rows = jnp.stack([qv_bias[0], jnp.zeros_like(qv_bias[0]), qv_bias[1]])
    mixed_qkv = jnp.einsum('td,dcf->tcf', normed, qkv_weight, precision=highest) + bias_rows
    mixed_qkv = low(low_back(mixed_qkv)).reshape(seq_count, SEQ, 3, HEADS, HD)
    context = lax.map(lambda member: attend(*member), (mixed_qkv[:, :, 0], mixed_qkv[:, :, 1], mixed_qkv[:, :, 2], segments))
    context = low(low_back(context.reshape(rows_here, D)))
    attention = low_back(jnp.dot(context, out_weight, precision=highest))
    resid = attention + out_bias + tokens_in
    normed_two = low(layer_norm(resid, norm2_gain, norm2_shift))
    hidden_pre = low_back(jnp.dot(normed_two, fc1_weight, precision=highest) + fc1_bias)
    hidden = low(gelu_tanh(hidden_pre))
    return jnp.dot(hidden, fc2_weight, precision=highest) + fc2_bias + resid

def reference(tokens, segment_ids, norm1_gain, norm1_shift, qkv_weight, qv_bias, out_weight, out_bias, norm2_gain, norm2_shift, fc1_weight, fc1_bias, fc2_weight, fc2_bias, out_grad):
    params = tuple((param.astype(jnp.float32) for param in (norm1_gain, norm1_shift, qkv_weight, qv_bias, out_weight, out_bias, norm2_gain, norm2_shift, fc1_weight, fc1_bias, fc2_weight, fc2_bias)))
    seq_total = SEQS * N_DP
    per_step = math.gcd(seq_total, max(1, 4096 // SEQ))
    step_count = seq_total // per_step
    tok_steps = tokens.reshape(step_count, per_step * SEQ, D)
    grad_steps = out_grad.reshape(step_count, per_step * SEQ, D)
    seg_steps = segment_ids.reshape(step_count, per_step, SEQ)

    def scan_step(running, member):
        tok_block, seg_block, grad_block = member

        def apply_layer(tok_rows, *weights):
            return forward(tok_rows, *weights, seg_block)
        outputs, pull_back = jax.vjp(apply_layer, tok_block.astype(jnp.float32), *params)
        gradients = pull_back(grad_block.astype(jnp.float32))
        running = tuple((earlier + fresh for earlier, fresh in zip(running, gradients[1:])))
        return (running, (outputs.astype(jnp.bfloat16), gradients[0]))
    zero_grads = tuple((jnp.zeros_like(param) for param in params))
    running, (out_rows, in_grads) = lax.scan(scan_step, zero_grads, (tok_steps, seg_steps, grad_steps))
    return (out_rows.reshape(TOKENS, D), in_grads.reshape(TOKENS, D), running[0], running[1], running[2], running[3], running[4], running[5], running[6], running[7], running[8], running[9], running[10], running[11])
```

```python
import functools

import jax
import jax.numpy as jnp
from jax import lax
from jax.experimental import pallas as pl
from jax.experimental.pallas import tpu as pltpu
from jax.sharding import PartitionSpec as P

HEADS = 16
HD = 64
DOC_MOST = 768
QB = 256
MASKED = -1e12
eps = 1e-05
f32 = jnp.float32
bf16 = jnp.bfloat16


def dot(a, b, ca, cb):
    return lax.dot_general(a, b, (((ca,), (cb,)), ((), ())), preferred_element_type=f32)


def fill_mask(segq_ref, segk_ref, mask_ref, window, halo):
    for i in range(mask_ref.shape[0]):
        key_at = lax.broadcasted_iota(jnp.int32, (window, QB), 0) + i * QB
        query_at = lax.broadcasted_iota(jnp.int32, (window, QB), 1) + (i * QB + halo)
        same = segk_ref[i * QB : i * QB + window, :] == segq_ref[:, i * QB : (i + 1) * QB]
        allowed = same & (key_at <= query_at)
        mask_ref[i] = jnp.where(allowed, (key_at - query_at).astype(f32), MASKED)


def halves(rows):
    lane = lax.broadcasted_iota(jnp.int32, (rows, 2 * HD), 1)
    return [lane < HD, lane >= HD]


def attend_kernel(halo, slopes, segq, segk, q_ref, k_ref, v_ref, o_ref, lse_ref, mask_ref):
    window = halo + QB
    pair = pl.program_id(0)

    @pl.when(pair == 0)
    def _():
        fill_mask(segq, segk, mask_ref, window, halo)

    v_t = v_ref[...].T
    pick = halves(QB)
    for i in range(mask_ref.shape[0]):
        rows = slice(i * QB, (i + 1) * QB)
        keys = slice(i * QB, i * QB + window)
        query = q_ref[rows, :] * jnp.asarray(HD**-0.5, bf16)
        key_rows = k_ref[keys, :]
        out = []
        for h in range(2):
            q_h = jnp.where(pick[h], query, jnp.zeros_like(query))
            scores = dot(key_rows, q_h, 1, 1) + slopes[2 * pair + h] * mask_ref[i]
            top = jnp.max(scores, axis=0, keepdims=True)
            expo = jnp.exp(scores - top)
            total = jnp.sum(expo, axis=0, keepdims=True)
            o_t = dot(v_t[:, keys], expo.astype(bf16), 1, 0)
            out.append(o_t[h * HD : (h + 1) * HD, :] * (1.0 / total))
            lse_ref[0, h : h + 1, rows] = top + jnp.log(total)
        o_ref[rows, :] = jnp.concatenate(out, axis=0).T.astype(bf16)


def attend_back_kernel(
    halo, slopes, segq, segk, q_ref, k_ref, v_ref, g_ref, lse_ref, dq_ref, dk_ref, dv_ref,
    mask_ref, dk_acc, dv_acc,
):
    window = halo + QB
    pair = pl.program_id(0)

    @pl.when(pair == 0)
    def _():
        fill_mask(segq, segk, mask_ref, window, halo)

    k_t = k_ref[...].T
    pick = halves(QB)
    dk_acc[...] = jnp.zeros_like(dk_acc)
    dv_acc[...] = jnp.zeros_like(dv_acc)
    for i in range(mask_ref.shape[0]):
        rows = slice(i * QB, (i + 1) * QB)
        keys = slice(i * QB, i * QB + window)
        query = q_ref[rows, :] * jnp.asarray(HD**-0.5, bf16)
        grad = g_ref[rows, :]
        key_rows = k_ref[keys, :]
        value_rows = v_ref[keys, :]
        out = []
        for h in range(2):
            q_h = jnp.where(pick[h], query, jnp.zeros_like(query))
            g_h = jnp.where(pick[h], grad, jnp.zeros_like(grad))
            scores = dot(key_rows, q_h, 1, 1) + slopes[2 * pair + h] * mask_ref[i]
            probs = jnp.exp(scores - lse_ref[0, h : h + 1, rows])
            grad_probs = dot(value_rows, g_h, 1, 1)
            delta = jnp.sum(probs * grad_probs, axis=0, keepdims=True)
            grad_scores = (probs * (grad_probs - delta)).astype(bf16)
            dv_acc[keys, :] += dot(probs.astype(bf16), g_h, 1, 0)
            dk_acc[keys, :] += dot(grad_scores, q_h, 1, 0)
            dq_t = dot(k_t[:, keys], grad_scores, 1, 0)
            out.append(dq_t[h * HD : (h + 1) * HD, :])
        dq_ref[rows, :] = (jnp.concatenate(out, axis=0).T * HD**-0.5).astype(bf16)
    dk_ref[...] = dk_acc[...].astype(bf16)
    dv_ref[...] = dv_acc[...].astype(bf16)


def attend(slopes, segq, segk, q, k, v):
    rows, wide = q.shape
    ext = k.shape[0]
    halo = ext - rows
    pairs = wide // (2 * HD)
    blocks = rows // QB
    col = lambda n: pl.BlockSpec((n, 2 * HD), lambda p: (0, p))
    work = pairs * 2 * blocks * (halo + QB) * QB
    return pl.pallas_call(
        functools.partial(attend_kernel, halo),
        grid=(pairs,),
        in_specs=[
            pl.BlockSpec(memory_space=pltpu.SMEM),
            pl.BlockSpec((1, rows), lambda p: (0, 0)),
            pl.BlockSpec((ext, 1), lambda p: (0, 0)),
            col(rows),
            col(ext),
            col(ext),
        ],
        out_specs=[col(rows), pl.BlockSpec((1, 2, rows), lambda p: (p, 0, 0))],
        out_shape=[
            jax.ShapeDtypeStruct((rows, wide), bf16),
            jax.ShapeDtypeStruct((pairs, 2, rows), f32),
        ],
        scratch_shapes=[pltpu.VMEM((blocks, halo + QB, QB), f32)],
        compiler_params=pltpu.CompilerParams(vmem_limit_bytes=40 << 20),
        cost_estimate=pl.CostEstimate(
            flops=work * 256 * 4, bytes_accessed=2 * wide * (2 * rows + 2 * ext), transcendentals=work
        ),
    )(slopes, segq, segk, q, k, v)


def attend_back(slopes, segq, segk, q, k, v, grad, lse):
    rows, wide = q.shape
    ext = k.shape[0]
    halo = ext - rows
    pairs = wide // (2 * HD)
    blocks = rows // QB
    col = lambda n: pl.BlockSpec((n, 2 * HD), lambda p: (0, p))
    work = pairs * 2 * blocks * (halo + QB) * QB
    return pl.pallas_call(
        functools.partial(attend_back_kernel, halo),
        grid=(pairs,),
        in_specs=[
            pl.BlockSpec(memory_space=pltpu.SMEM),
            pl.BlockSpec((1, rows), lambda p: (0, 0)),
            pl.BlockSpec((ext, 1), lambda p: (0, 0)),
            col(rows),
            col(ext),
            col(ext),
            col(rows),
            pl.BlockSpec((1, 2, rows), lambda p: (p, 0, 0)),
        ],
        out_specs=[col(rows), col(ext), col(ext)],
        out_shape=[
            jax.ShapeDtypeStruct((rows, wide), bf16),
            jax.ShapeDtypeStruct((ext, wide), bf16),
            jax.ShapeDtypeStruct((ext, wide), bf16),
        ],
        scratch_shapes=[
            pltpu.VMEM((blocks, halo + QB, QB), f32),
            pltpu.VMEM((ext, 2 * HD), f32),
            pltpu.VMEM((ext, 2 * HD), f32),
        ],
        compiler_params=pltpu.CompilerParams(vmem_limit_bytes=48 << 20),
        cost_estimate=pl.CostEstimate(
            flops=work * 256 * 10, bytes_accessed=2 * wide * (3 * rows + 4 * ext), transcendentals=work
        ),
    )(slopes, segq, segk, q, k, v, grad, lse)


def swap(value, b):
    n = lax.axis_size("dp")
    return lax.ppermute(value, "dp", [(i, i ^ (1 << b)) for i in range(n)])


def shift(value, s):
    n = lax.axis_size("mp")
    return lax.ppermute(value, "mp", [(i, (i + s) % n) for i in range(n)])


def add(a, b):
    return (a.astype(f32) + b.astype(f32)).astype(bf16)


def spread(a, b):
    x_a, y_b = swap(a, 1), swap(b, 2)
    a2, b2 = jnp.stack([a, x_a], 1), jnp.stack([b, y_b], 1)
    y_a2, x_b2 = swap(a2, 2), swap(b2, 1)
    return jnp.stack([a2, y_a2], 1), jnp.stack([b2, x_b2], 2)


def gather_blocks(a, b):
    n = lax.axis_size("mp")
    both = [shift(jnp.concatenate([a, b], 0), s) for s in range(1, n)]
    cut = a.shape[0]
    return spread(jnp.stack([r[:cut] for r in both]), jnp.stack([r[cut:] for r in both]))


def scatter_blocks(a, b):
    n = lax.axis_size("mp")
    a, b = add(a[:, 0], swap(a[:, 1], 2)), add(b[:, :, 0], swap(b[:, :, 1], 1))
    a, b = add(a[:, 0], swap(a[:, 1], 1)), add(b[:, 0], swap(b[:, 1], 2))
    both = jnp.concatenate([a, b], 1)
    total = both[0].astype(f32)
    for s in range(1, n):
        total = total + shift(both[s], n - s).astype(f32)
    for b_hi in range(3, lax.axis_size("dp").bit_length() - 1):
        total = total + swap(total, b_hi)
    cut = a.shape[1]
    total = total.astype(bf16)
    a4, b4 = spread(total[None, :cut], total[None, cut:])
    return a4[0], b4[0]


def norm_parts(rows):
    mean = jnp.mean(rows, axis=-1, keepdims=True)
    centred = rows - mean
    rstd = lax.rsqrt(jnp.mean(centred * centred, axis=-1, keepdims=True) + eps)
    return centred * rstd, rstd


def norm_back(grad, gain, xhat, rstd):
    scaled = grad * gain
    return rstd * (
        scaled
        - jnp.mean(scaled, axis=-1, keepdims=True)
        - xhat * jnp.mean(scaled * xhat, axis=-1, keepdims=True)
    )


def gelu_both(v):
    c, k = 0.7978845608028654, 0.044715
    t = jnp.tanh(c * (v + k * v * v * v))
    value = 0.5 * v * (1.0 + t)
    slope = 0.5 * (1.0 + t) + 0.5 * v * (1.0 - t * t) * (c * (1.0 + 3.0 * k * v * v))
    return value, slope


def body(
    tokens,
    segment_ids,
    norm1_gain,
    norm1_shift,
    qkv_weight,
    qv_bias,
    out_weight,
    out_bias,
    norm2_gain,
    norm2_shift,
    fc1_weight,
    fc1_bias,
    fc2_weight,
    fc2_bias,
    out_grad,
):
    rows, wide = tokens.shape
    half = wide // 2
    mp = lax.axis_size("mp")
    m = lax.axis_index("mp")
    d = lax.axis_index("dp")
    bits = (d & 1, (d >> 1) & 1, (d >> 2) & 1)
    places = [(ey, ex) for ey in range(2) for ex in range(2)]
    ff_here = fc1_weight.shape[1]
    piece = ff_here // 8
    heads_here = qkv_weight.shape[2] // HD

    def rel(ec, ey, ex):
        return (bits[0] ^ ec), (bits[2] ^ ey) * 2 + (bits[1] ^ ex)

    halo, parts = 0, [tokens]
    t = 1
    while halo < DOC_MOST:
        n = min(rows, DOC_MOST - halo)
        parts.insert(
            0, lax.ppermute(tokens[rows - n :], "mp", [(i, i + t) for i in range(mp - t)])
        )
        halo += n
        t += 1
    halo_parts = [(p.shape[0], i) for p, i in zip(parts[:-1], range(len(parts) - 1, 0, -1))]

    loc = jnp.concatenate(
        [
            jnp.transpose(qkv_weight, (1, 2, 0)),
            out_weight[None],
        ],
        0,
    ).reshape(4, heads_here, HD, wide)
    loc = jnp.stack([loc[0], loc[3], loc[1], loc[2]], 1)

    def loc_half(ec):
        out = []
        for ey, ex in places:
            c_at, head = rel(ec, ey, ex)
            out.append(lax.dynamic_slice(loc, (head, 0, 0, c_at * half), (1, 4, HD, half))[0])
        return jnp.stack(out)

    att_loc = [loc_half(0), loc_half(1)]
    fc1_t = fc1_weight.T

    def loc_rows(weight, ec):
        out = []
        for ey, ex in places:
            c_at, place = rel(ec, ey, ex)
            out.append(lax.dynamic_slice_in_dim(weight, (place * 2 + c_at) * piece, piece, 0))
        return jnp.stack(out)

    fc1_loc = [loc_rows(fc1_t, 0), loc_rows(fc1_t, 1)]
    fc2_loc = [loc_rows(fc2_weight, 0), loc_rows(fc2_weight, 1)]

    bias_own = jnp.concatenate([fc1_bias, qv_bias.reshape(-1)])
    bias_all = jnp.stack([bias_own] + [shift(bias_own, s) for s in range(1, mp)])
    fc1_b = bias_all[:, :ff_here]
    qv_b = bias_all[:, ff_here:].reshape(mp, 2, heads_here, HD)

    def rel_rows(table, ec):
        out = []
        for ey, ex in places:
            c_at, place = rel(ec, ey, ex)
            at = place if ec is None else place * 2 + c_at
            out.append(lax.dynamic_slice_in_dim(table, at, 1, 1))
        return jnp.concatenate(out, 1)

    def rel_heads(table):
        out = []
        for ey, ex in places:
            place = rel(0, ey, ex)[1]
            out.append(lax.dynamic_slice_in_dim(table, place, 1, 1))
        return jnp.concatenate(out, 1)

    q_bias = rel_heads(qv_b[:, 0]).reshape(-1)
    v_bias = rel_heads(qv_b[:, 1]).reshape(-1)
    fc1_bs = [rel_rows(fc1_b.reshape(mp, 8, piece), ec).reshape(-1) for ec in range(2)]

    def gather_att():
        own = att_loc[0][0]
        a4, b4 = gather_blocks(own[:2].reshape(2 * HD, half), own[2:].reshape(2 * HD, half))
        a4 = a4.reshape(mp - 1, 4, 2, HD, half)
        b4 = b4.reshape(mp - 1, 4, 2, HD, half)
        mine = jnp.concatenate(
            [att_loc[0][None], jnp.concatenate([a4, b4], 2)], 0
        )
        mine = jnp.transpose(mine, (2, 0, 1, 3, 4)).reshape(4, HEADS * HD, half)
        return mine, swap(mine, 0)

    def gather_ff(local):
        own = local[0][0]
        a4, b4 = gather_blocks(own[: piece // 2], own[piece // 2 :])
        rest = jnp.stack([a4, b4], 3).reshape(mp - 1, 4, piece, wide)
        mine = jnp.concatenate([local[0][None], rest], 0).reshape(-1, wide)
        return mine, swap(mine, 0)

    w_att = gather_att()
    w_fc1 = gather_ff(fc1_loc)
    w_fc2 = gather_ff(fc2_loc)

    ext = jnp.concatenate(parts, 0).astype(f32)
    xhat_ext, rstd_ext = norm_parts(ext)
    norm1 = (xhat_ext * norm1_gain + norm1_shift).astype(bf16)
    col = [bits[0] * half, (1 - bits[0]) * half]

    def cols(value):
        return [lax.dynamic_slice_in_dim(value, at, half, 1) for at in col]

    def join(own, other):
        first = bits[0] == 0
        return jnp.concatenate([jnp.where(first, own, other), jnp.where(first, other, own)], 1)

    n1 = cols(norm1)

    def project(t, lhs):
        return dot(lhs[0], w_att[0][t], 1, 1) + dot(lhs[1], w_att[1][t], 1, 1)

    q = (project(0, [v[halo:] for v in n1]) + q_bias).astype(bf16)
    k = project(2, n1).astype(bf16)
    v = (project(3, n1) + v_bias).astype(bf16)

    seg_row = jnp.concatenate([jnp.full((1, halo), -1, jnp.int32), segment_ids], 1)
    segk = lax.dynamic_slice_in_dim(seg_row, m * rows, halo + rows, 1)
    segq = segk[:, halo:]
    segk = segk.reshape(halo + rows, 1)
    block = (m + mp - jnp.arange(mp)) % mp
    place = jnp.stack([rel(0, ey, ex)[1] for ey, ex in places])
    head = (block[:, None] * heads_here + place[None]).reshape(-1)
    slopes = jnp.exp2(-8.0 * (head + 1).astype(f32) / HEADS)

    context, lse = attend(slopes, segq, segk, q, k, v)
    attention = join(dot(context, w_att[0][1], 1, 0), dot(context, w_att[1][1], 1, 0))
    tokens_wide = tokens.astype(f32)
    resid = attention + out_bias + tokens_wide
    xhat2, rstd2 = norm_parts(resid)
    norm2 = (xhat2 * norm2_gain + norm2_shift).astype(bf16)
    pre = [dot(norm2, w_fc1[i], 1, 1) + fc1_bs[i] for i in range(2)]
    hidden = [gelu_both(p)[0].astype(bf16) for p in pre]
    mlp = dot(hidden[0], w_fc2[0], 1, 0) + dot(hidden[1], w_fc2[1], 1, 0)
    result = (mlp + fc2_bias + resid).astype(bf16)

    def reduce_ff(lhs, rhs):
        theirs = swap(dot(lhs[1], rhs, 0, 0).astype(bf16), 0)
        mine = (dot(lhs[0], rhs, 0, 0) + theirs.astype(f32)).astype(bf16)
        mine = mine.reshape(mp, 2, 2, 2, piece // 2, wide)
        a4, b4 = scatter_blocks(mine[:, :, :, 0], mine[:, :, :, 1])
        mine = jnp.stack([a4, b4], 2).reshape(4, piece, wide)
        both = jnp.stack([mine, swap(mine, 0)])
        out = []
        for i in range(8):
            at = d ^ i
            at_c, at_p = at & 1, (at >> 1) & 3
            out.append(lax.dynamic_slice(both, (at_c, at_p, 0, 0), (1, 1, piece, wide))[0, 0])
        return jnp.concatenate(out, 0).astype(f32)

    grad_fc2 = reduce_ff(hidden, out_grad)
    grad_pre = [
        (dot(out_grad, w_fc2[i], 1, 1) * gelu_both(pre[i])[1]).astype(bf16) for i in range(2)
    ]
    grad_fc1 = reduce_ff(grad_pre, norm2).T
    grad_norm2 = dot(grad_pre[0], w_fc1[0], 1, 0) + dot(grad_pre[1], w_fc1[1], 1, 0)
    out_grad_wide = out_grad.astype(f32)
    grad_resid = out_grad_wide + norm_back(grad_norm2, norm2_gain, xhat2, rstd2)
    grad_att = cols(grad_resid.astype(bf16))
    grad_context = (
        dot(grad_att[0], w_att[0][1], 1, 1) + dot(grad_att[1], w_att[1][1], 1, 1)
    ).astype(bf16)
    dq, dk, dv = attend_back(slopes, segq, segk, q, k, v, grad_context, lse)

    def back_half(i):
        tail = dot(dk, w_att[i][2], 1, 0) + dot(dv, w_att[i][3], 1, 0)
        return tail[:halo], tail[halo:] + dot(dq, w_att[i][0], 1, 0)

    back = [back_half(0), back_half(1)]
    grad_halo = join(back[0][0], back[1][0]).astype(bf16)
    grad_norm1 = join(back[0][1], back[1][1])

    def weights_half(i):
        return jnp.stack(
            [
                dot(dq, n1[i][halo:], 0, 0).astype(bf16),
                dot(context, grad_att[i], 0, 0).astype(bf16),
                dot(dk, n1[i], 0, 0).astype(bf16),
                dot(dv, n1[i], 0, 0).astype(bf16),
            ]
        )

    theirs = swap(weights_half(1), 0)
    mine = add(weights_half(0), theirs).reshape(4, mp, 2, 2, HD, half)
    mine = jnp.transpose(mine, (1, 2, 3, 0, 4, 5))
    a4, b4 = scatter_blocks(
        mine[:, :, :, :2].reshape(mp, 2, 2, 2 * HD, half),
        mine[:, :, :, 2:].reshape(mp, 2, 2, 2 * HD, half),
    )
    mine = jnp.stack([a4, b4], 2).reshape(4, 4, HD, half)
    both = jnp.stack([mine, swap(mine, 0)])
    out = []
    for p in range(4):
        at_p = ((d >> 1) & 3) ^ p
        pair = lax.dynamic_slice_in_dim(both, at_p, 1, 1)[:, 0]
        first = bits[0] == 0
        out.append(
            jnp.concatenate(
                [jnp.where(first, pair[0], pair[1]), jnp.where(first, pair[1], pair[0])], -1
            )
        )
    grad_att_w = jnp.stack(out, 1).reshape(4, heads_here * HD, wide).astype(f32)
    grad_out = grad_att_w[1]
    grad_qkv = jnp.transpose(
        jnp.stack([grad_att_w[0], grad_att_w[2], grad_att_w[3]]), (2, 0, 1)
    )

    at = 0
    for n, t in halo_parts:
        moved = lax.ppermute(
            grad_halo[at : at + n], "mp", [(i, i - t) for i in range(t, mp)]
        ).astype(f32)
        grad_norm1 = grad_norm1 + jnp.pad(moved, ((rows - n, 0), (0, 0)))
        at += n
    xhat1, rstd1 = xhat_ext[halo:], rstd_ext[halo:]
    in_grad = grad_resid + norm_back(grad_norm1, norm1_gain, xhat1, rstd1)

    def in_order(pieces, n):
        table = jnp.stack(
            [lax.dynamic_index_in_dim(pieces, (m + mp - j) % mp, 0, False) for j in range(mp)]
        )
        table = jnp.where(bits[2] == 0, table, table[:, ::-1])
        table = jnp.where(bits[1] == 0, table, table[:, :, ::-1])
        if table.shape[3] == 2:
            table = jnp.where(bits[0] == 0, table, table[:, :, :, ::-1])
        return table.reshape(mp, -1)

    ff_sums = jnp.stack(
        [jnp.sum(g.astype(f32), axis=0).reshape(mp, 2, 2, piece) for g in grad_pre], 3
    )
    q_sums = jnp.sum(dq.astype(f32), axis=0).reshape(mp, 2, 2, 1, HD)
    v_sums = jnp.sum(dv.astype(f32), axis=0).reshape(mp, 2, 2, 1, HD)
    small = jnp.stack(
        [
            jnp.sum(grad_resid, axis=0),
            jnp.sum(grad_norm1 * xhat1, axis=0),
            jnp.sum(grad_norm1, axis=0),
            jnp.sum(grad_norm2 * xhat2, axis=0),
            jnp.sum(grad_norm2, axis=0),
            jnp.sum(out_grad_wide, axis=0),
        ]
    )
    n_small = wide // mp
    vectors = jnp.concatenate(
        [
            jnp.transpose(small.reshape(6, mp, n_small), (1, 0, 2)).reshape(mp, -1),
            in_order(q_sums, HD),
            in_order(v_sums, HD),
            in_order(ff_sums, piece),
        ],
        1,
    )
    for b in range(lax.axis_size("dp").bit_length() - 1):
        vectors = vectors + swap(vectors, b)
    mine = lax.dynamic_index_in_dim(vectors, m, 0, False)
    for s in range(1, mp):
        sent = lax.dynamic_index_in_dim(vectors, (m + mp - s) % mp, 0, False)
        mine = mine + shift(sent, mp - s)
    six = mine[: 6 * n_small].reshape(6, n_small)
    rest = mine[6 * n_small :]
    n_qv = heads_here * HD
    grad_qv = rest[: 2 * n_qv].reshape(2, n_qv)
    grad_fc1_bias = rest[2 * n_qv :]
    return (
        result,
        in_grad,
        six[1],
        six[2],
        grad_qkv,
        grad_qv,
        grad_out,
        six[0],
        six[3],
        six[4],
        grad_fc1,
        grad_fc1_bias,
        grad_fc2,
        six[5],
    )


def solution(mesh):
    placed = (
        P(("dp", "mp"), None),
        P("dp", None),
        P(),
        P(),
        P(None, None, "mp"),
        P(None, "mp"),
        P("mp", None),
        P(),
        P(),
        P(),
        P(None, "mp"),
        P("mp"),
        P("mp", None),
        P(),
        P(("dp", "mp"), None),
    )
    return jax.shard_map(
        body,
        mesh=mesh,
        in_specs=placed,
        out_specs=(
            P(("dp", "mp"), None),
            P(("dp", "mp"), None),
            P("mp"),
            P("mp"),
            P(None, None, "mp"),
            P(None, "mp"),
            P("mp", None),
            P("mp"),
            P("mp"),
            P("mp"),
            P(None, "mp"),
            P("mp"),
            P("mp", None),
            P("mp"),
        ),
        check_vma=False,
    )
```

```python
import functools

import jax
import jax.numpy as jnp
from jax import lax
from jax.experimental import pallas as pl
from jax.experimental.pallas import tpu as pltpu
from jax.sharding import PartitionSpec as P

HEADS = 16
HD = 64
DOC_MOST = 768
QB = 256
MASKED = -1e12
eps = 1e-05
f32 = jnp.float32
bf16 = jnp.bfloat16


def dot(a, b, ca, cb):
    return lax.dot_general(a, b, (((ca,), (cb,)), ((), ())), preferred_element_type=f32)


def fill_mask(segq_ref, segk_ref, mask_ref, window, halo):
    for i in range(mask_ref.shape[0]):
        key_at = lax.broadcasted_iota(jnp.int32, (window, QB), 0) + i * QB
        query_at = lax.broadcasted_iota(jnp.int32, (window, QB), 1) + (i * QB + halo)
        same = segk_ref[i * QB : i * QB + window, :] == segq_ref[:, i * QB : (i + 1) * QB]
        allowed = same & (key_at <= query_at)
        mask_ref[i] = jnp.where(allowed, (key_at - query_at).astype(f32), MASKED)


def halves(rows):
    lane = lax.broadcasted_iota(jnp.int32, (rows, 2 * HD), 1)
    return [lane < HD, lane >= HD]


def attend_kernel(halo, slopes, segq, segk, q_ref, k_ref, v_ref, o_ref, lse_ref, mask_ref):
    window = halo + QB
    pair = pl.program_id(0)

    @pl.when(pair == 0)
    def _():
        fill_mask(segq, segk, mask_ref, window, halo)

    v_t = v_ref[...].T
    pick = halves(QB)
    for i in range(mask_ref.shape[0]):
        rows = slice(i * QB, (i + 1) * QB)
        keys = slice(i * QB, i * QB + window)
        query = q_ref[rows, :] * jnp.asarray(HD**-0.5, bf16)
        key_rows = k_ref[keys, :]
        out = []
        for h in range(2):
            q_h = jnp.where(pick[h], query, jnp.zeros_like(query))
            scores = dot(key_rows, q_h, 1, 1) + slopes[2 * pair + h] * mask_ref[i]
            top = jnp.max(scores, axis=0, keepdims=True)
            expo = jnp.exp(scores - top)
            total = jnp.sum(expo, axis=0, keepdims=True)
            o_t = dot(v_t[:, keys], expo.astype(bf16), 1, 0)
            out.append(o_t[h * HD : (h + 1) * HD, :] * (1.0 / total))
            lse_ref[0, h : h + 1, rows] = top + jnp.log(total)
        o_ref[rows, :] = jnp.concatenate(out, axis=0).T.astype(bf16)


def attend_back_kernel(
    halo, slopes, segq, segk, q_ref, k_ref, v_ref, g_ref, lse_ref, dq_ref, dk_ref, dv_ref,
    mask_ref, dk_acc, dv_acc,
):
    window = halo + QB
    pair = pl.program_id(0)

    @pl.when(pair == 0)
    def _():
        fill_mask(segq, segk, mask_ref, window, halo)

    k_t = k_ref[...].T
    pick = halves(QB)
    dk_acc[...] = jnp.zeros_like(dk_acc)
    dv_acc[...] = jnp.zeros_like(dv_acc)
    for i in range(mask_ref.shape[0]):
        rows = slice(i * QB, (i + 1) * QB)
        keys = slice(i * QB, i * QB + window)
        query = q_ref[rows, :] * jnp.asarray(HD**-0.5, bf16)
        grad = g_ref[rows, :]
        key_rows = k_ref[keys, :]
        value_rows = v_ref[keys, :]
        out = []
        for h in range(2):
            q_h = jnp.where(pick[h], query, jnp.zeros_like(query))
            g_h = jnp.where(pick[h], grad, jnp.zeros_like(grad))
            scores = dot(key_rows, q_h, 1, 1) + slopes[2 * pair + h] * mask_ref[i]
            probs = jnp.exp(scores - lse_ref[0, h : h + 1, rows])
            grad_probs = dot(value_rows, g_h, 1, 1)
            delta = jnp.sum(probs * grad_probs, axis=0, keepdims=True)
            grad_scores = (probs * (grad_probs - delta)).astype(bf16)
            dv_acc[keys, :] += dot(probs.astype(bf16), g_h, 1, 0)
            dk_acc[keys, :] += dot(grad_scores, q_h, 1, 0)
            dq_t = dot(k_t[:, keys], grad_scores, 1, 0)
            out.append(dq_t[h * HD : (h + 1) * HD, :])
        dq_ref[rows, :] = (jnp.concatenate(out, axis=0).T * HD**-0.5).astype(bf16)
    dk_ref[...] = dk_acc[...].astype(bf16)
    dv_ref[...] = dv_acc[...].astype(bf16)


def attend(slopes, segq, segk, q, k, v):
    rows, wide = q.shape
    ext = k.shape[0]
    halo = ext - rows
    pairs = wide // (2 * HD)
    blocks = rows // QB
    col = lambda n: pl.BlockSpec((n, 2 * HD), lambda p: (0, p))
    work = pairs * 2 * blocks * (halo + QB) * QB
    return pl.pallas_call(
        functools.partial(attend_kernel, halo),
        grid=(pairs,),
        in_specs=[
            pl.BlockSpec(memory_space=pltpu.SMEM),
            pl.BlockSpec((1, rows), lambda p: (0, 0)),
            pl.BlockSpec((ext, 1), lambda p: (0, 0)),
            col(rows),
            col(ext),
            col(ext),
        ],
        out_specs=[col(rows), pl.BlockSpec((1, 2, rows), lambda p: (p, 0, 0))],
        out_shape=[
            jax.ShapeDtypeStruct((rows, wide), bf16),
            jax.ShapeDtypeStruct((pairs, 2, rows), f32),
        ],
        scratch_shapes=[pltpu.VMEM((blocks, halo + QB, QB), f32)],
        compiler_params=pltpu.CompilerParams(vmem_limit_bytes=40 << 20),
        cost_estimate=pl.CostEstimate(
            flops=work * 256 * 4, bytes_accessed=2 * wide * (2 * rows + 2 * ext), transcendentals=work
        ),
    )(slopes, segq, segk, q, k, v)


def attend_back(slopes, segq, segk, q, k, v, grad, lse):
    rows, wide = q.shape
    ext = k.shape[0]
    halo = ext - rows
    pairs = wide // (2 * HD)
    blocks = rows // QB
    col = lambda n: pl.BlockSpec((n, 2 * HD), lambda p: (0, p))
    work = pairs * 2 * blocks * (halo + QB) * QB
    return pl.pallas_call(
        functools.partial(attend_back_kernel, halo),
        grid=(pairs,),
        in_specs=[
            pl.BlockSpec(memory_space=pltpu.SMEM),
            pl.BlockSpec((1, rows), lambda p: (0, 0)),
            pl.BlockSpec((ext, 1), lambda p: (0, 0)),
            col(rows),
            col(ext),
            col(ext),
            col(rows),
            pl.BlockSpec((1, 2, rows), lambda p: (p, 0, 0)),
        ],
        out_specs=[col(rows), col(ext), col(ext)],
        out_shape=[
            jax.ShapeDtypeStruct((rows, wide), bf16),
            jax.ShapeDtypeStruct((ext, wide), bf16),
            jax.ShapeDtypeStruct((ext, wide), bf16),
        ],
        scratch_shapes=[
            pltpu.VMEM((blocks, halo + QB, QB), f32),
            pltpu.VMEM((ext, 2 * HD), f32),
            pltpu.VMEM((ext, 2 * HD), f32),
        ],
        compiler_params=pltpu.CompilerParams(vmem_limit_bytes=48 << 20),
        cost_estimate=pl.CostEstimate(
            flops=work * 256 * 10, bytes_accessed=2 * wide * (3 * rows + 4 * ext), transcendentals=work
        ),
    )(slopes, segq, segk, q, k, v, grad, lse)


def own_att_kernel(at, qkv_ref, out_ref, own_ref):
    for t, rows in enumerate((qkv_ref[0], out_ref[...], qkv_ref[1], qkv_ref[2])):
        half = rows.shape[1] // 2
        left, right = rows[:, :half], rows[:, half:]
        own_ref[0, t, 0] = jnp.where(at[0] == 0, left, right)
        own_ref[1, t, 0] = jnp.where(at[0] == 0, right, left)


def own_att(at, qkv_t, out_weight):
    wide = out_weight.shape[1]
    return pl.pallas_call(
        own_att_kernel,
        grid_spec=pltpu.PrefetchScalarGridSpec(
            num_scalar_prefetch=1,
            grid=(4,),
            in_specs=[
                pl.BlockSpec((3, HD, wide), lambda p, at: (0, at[1 + p], 0)),
                pl.BlockSpec((HD, wide), lambda p, at: (at[1 + p], 0)),
            ],
            out_specs=pl.BlockSpec((2, 4, 1, HD, wide // 2), lambda p, at: (0, 0, p, 0, 0)),
        ),
        out_shape=jax.ShapeDtypeStruct((2, 4, 4, HD, wide // 2), bf16),
    )(at, qkv_t, out_weight)


def own_ff_kernel(at, fc1_ref, fc2_ref, o1_ref, o2_ref):
    o1_ref[...] = fc1_ref[...].T
    o2_ref[...] = fc2_ref[...]


def own_ff(at, fc1_weight, fc2_weight):
    hidden, wide = fc2_weight.shape
    piece = hidden // 8
    return pl.pallas_call(
        own_ff_kernel,
        grid_spec=pltpu.PrefetchScalarGridSpec(
            num_scalar_prefetch=1,
            grid=(8,),
            in_specs=[
                pl.BlockSpec((wide, piece), lambda i, at: (0, at[i])),
                pl.BlockSpec((piece, wide), lambda i, at: (at[i], 0)),
            ],
            out_specs=[pl.BlockSpec((piece, wide), lambda i, at: (i, 0))] * 2,
        ),
        out_shape=[jax.ShapeDtypeStruct((hidden, wide), bf16)] * 2,
    )(at, fc1_weight, fc2_weight)


def join_att_kernel(core, own_ref, x0_ref, x1_ref, y_ref, out_ref):
    p1, p2 = x1_ref[:, 0], y_ref[0, :, 0]
    first = core[0] == 0
    out_ref[0, :, 0] = own_ref[0]
    out_ref[0, 0, 1:] = x0_ref[:, 0]
    out_ref[0, 1, 1:] = jnp.where(first, p1, p2)
    out_ref[0, 2, 1:] = jnp.where(first, p2, p1)
    out_ref[0, 3, 1:] = y_ref[1, :, 0]


def join_att(core, own, x0, x1, y):
    rest, _, hd, half = x0.shape
    one = pl.BlockSpec((rest, 1, hd, half), lambda t: (0, t, 0, 0))
    return pl.pallas_call(
        join_att_kernel,
        grid=(4,),
        in_specs=[
            pl.BlockSpec(memory_space=pltpu.SMEM),
            pl.BlockSpec((1, 4, hd, half), lambda t: (t, 0, 0, 0)),
            one,
            one,
            pl.BlockSpec((2, rest, 1, hd, half), lambda t: (0, 0, t, 0, 0)),
        ],
        out_specs=pl.BlockSpec((1, 4, rest + 1, hd, half), lambda t: (t, 0, 0, 0, 0)),
        out_shape=jax.ShapeDtypeStruct((4, 4, rest + 1, hd, half), bf16),
    )(core, own, x0, x1, y)


def add_att_kernel(at, *refs):
    mine, theirs, (hi_ref, lo_ref) = refs[:4], refs[4:8], refs[8:]
    i = pl.program_id(0)
    for t in range(4):
        total = (mine[t][...].astype(f32) + theirs[t][...].astype(f32)).astype(bf16)

        @pl.when(i < 2)
        def _():
            hi_ref[0, t] = total

        @pl.when(i >= 2)
        def _():
            lo_ref[0, t] = total


def add_att(at, mine, theirs):
    rows, half = mine[0].shape
    block = pl.BlockSpec((rows // 4, half), lambda i, at: (at[i], 0))
    shape = jax.ShapeDtypeStruct((2, 4, rows // 4, half), bf16)
    return pl.pallas_call(
        add_att_kernel,
        grid_spec=pltpu.PrefetchScalarGridSpec(
            num_scalar_prefetch=1,
            grid=(4,),
            in_specs=[block] * 8,
            out_specs=[
                pl.BlockSpec((1, 4, rows // 4, half), lambda i, at: (jnp.minimum(i, 1), 0, 0, 0)),
                pl.BlockSpec((1, 4, rows // 4, half), lambda i, at: (jnp.maximum(i - 2, 0), 0, 0, 0)),
            ],
        ),
        out_shape=[shape, shape],
    )(at, *mine, *theirs)


def swap(value, b):
    n = lax.axis_size("dp")
    return lax.ppermute(value, "dp", [(i, i ^ (1 << b)) for i in range(n)])


def hop(value, stage):
    n = lax.axis_size("dp")
    return lax.ppermute(
        value, "dp", [(i, i ^ (2 if (i & 1) == stage - 1 else 4)) for i in range(n)]
    )


def move(value, pairs):
    return lax.ppermute(value, "mp", pairs)


def shift(value, s):
    n = lax.axis_size("mp")
    return move(value, [(i, (i + s) % n) for i in range(n)])


def all_eight(value):
    n = lax.axis_size("dp")
    groups = None if n == 8 else [list(range(g, g + 8)) for g in range(0, n, 8)]
    return lax.all_gather(value, "dp", axis=0, axis_index_groups=groups)


def beyond(value):
    for b in range(3, lax.axis_size("dp").bit_length() - 1):
        value = value + swap(value, b)
    return value


def add(a, b):
    return (a.astype(f32) + b.astype(f32)).astype(bf16)


tie = lax.optimization_barrier
NEAR = [(0, 1), (1, 0), (2, 3), (3, 2)]
MIDDLE = [(1, 2), (2, 1)]
OUTWARD = [(1, 0), (2, 3)]
INWARD = [(0, 1), (3, 2)]


def norm_parts(rows):
    mean = jnp.mean(rows, axis=-1, keepdims=True)
    centred = rows - mean
    rstd = lax.rsqrt(jnp.mean(centred * centred, axis=-1, keepdims=True) + eps)
    return centred * rstd, rstd


def norm_back(grad, gain, xhat, rstd):
    scaled = grad * gain
    return rstd * (
        scaled
        - jnp.mean(scaled, axis=-1, keepdims=True)
        - xhat * jnp.mean(scaled * xhat, axis=-1, keepdims=True)
    )


def gelu_both(v):
    c, k = 0.7978845608028654, 0.044715
    t = jnp.tanh(c * (v + k * v * v * v))
    value = 0.5 * v * (1.0 + t)
    slope = 0.5 * (1.0 + t) + 0.5 * v * (1.0 - t * t) * (c * (1.0 + 3.0 * k * v * v))
    return value, slope


def body(
    tokens,
    segment_ids,
    norm1_gain,
    norm1_shift,
    qkv_weight,
    qv_bias,
    out_weight,
    out_bias,
    norm2_gain,
    norm2_shift,
    fc1_weight,
    fc1_bias,
    fc2_weight,
    fc2_bias,
    out_grad,
):
    rows, wide = tokens.shape
    half = wide // 2
    mp = lax.axis_size("mp")
    m = lax.axis_index("mp")
    d = lax.axis_index("dp") & 7
    core = d & 1
    ff_here = fc1_weight.shape[1]
    piece = ff_here // 8
    heads_here = qkv_weight.shape[2] // HD
    rest = mp - 1

    b1 = jnp.where(core == 0, 2, 4)
    b2 = 6 - b1
    zero = jnp.zeros_like(b1)
    mine_masks = jnp.stack([zero, b1, b2, zero + 6])
    their_masks = jnp.stack([zero + 1, 1 + b2, 1 + b1, zero + 7])
    slices = d ^ jnp.concatenate([mine_masks, their_masks])
    place = (d >> 1) ^ jnp.arange(4)
    far = jnp.where(m < 2, 2, 1)
    ff_blocks = jnp.stack([m ^ 1, far, far ^ 1])
    ff_rows = jnp.concatenate(
        [m * 8 + slices]
        + [(ff_blocks[None, :] * 8 + slices[i : i + 2, None]).reshape(-1) for i in range(0, 8, 2)]
    )
    att_blocks = (m + mp - jnp.arange(mp)) % mp
    heads = (att_blocks[None, :] * heads_here + place[:, None]).reshape(-1)
    slopes = jnp.exp2(-8.0 * (heads + 1).astype(f32) / HEADS)

    qkv_t = jnp.transpose(qkv_weight, (1, 2, 0))
    own = own_att(jnp.concatenate([core[None], place]), qkv_t, out_weight)
    att_me = own[0, :, 0]
    att_z = [shift(att_me, s) for s in range(1, mp)]

    near_rows = DOC_MOST - rows
    tokens_late, _ = tie((tokens, att_me))
    halo1 = move(tokens_late, [(i, i + 1) for i in range(mp - 1)])
    halo2 = move(halo1[rows - near_rows :], [(i, i + 1) for i in range(mp - 1)])
    halo = DOC_MOST

    own1, own2 = own_ff(slices, fc1_weight, fc2_weight)
    ff_me = jnp.concatenate([own1[:piece], own2[:piece]])
    ff_near = move(ff_me, NEAR)
    ff_mid = move(jnp.concatenate([ff_me, ff_near]), MIDDLE)
    ff_out = move(ff_mid, OUTWARD)
    ff_far = jnp.where((m == 1) | (m == 2), ff_mid, ff_out)
    ff_x0 = jnp.concatenate(
        [
            ff_near[:piece],
            ff_far[:piece],
            ff_far[2 * piece : 3 * piece],
            ff_near[piece:],
            ff_far[piece : 2 * piece],
            ff_far[3 * piece :],
        ]
    )

    bias_all = lax.all_gather(jnp.concatenate([fc1_bias, qv_bias.reshape(-1)]), "mp", axis=0)
    fc1_b = bias_all[:, :ff_here].reshape(mp * 8, piece)[ff_rows].reshape(-1)
    qv_b = bias_all[:, ff_here:].reshape(mp, 2, heads_here, HD)
    qv_b = jnp.transpose(qv_b, (0, 2, 1, 3)).reshape(mp * heads_here, 2 * HD)[heads]
    q_bias, v_bias = qv_b[:, :HD].reshape(-1), qv_b[:, HD:].reshape(-1)

    att_x0 = jnp.stack(att_z)
    att_x1 = hop(att_x0, 1)
    att_y = hop(jnp.stack([att_x0, att_x1]), 2)
    att_mine = join_att(core[None], own[0], att_x0, att_x1, att_y)
    att_mine = att_mine.reshape(4, HEADS * HD, half)
    w_att = [att_mine, swap(att_mine, 0)]

    ext = jnp.concatenate([halo2, halo1, tokens], 0).astype(f32)
    xhat_ext, rstd_ext = norm_parts(ext)
    norm1 = (xhat_ext * norm1_gain + norm1_shift).astype(bf16)
    col = [core * half, (1 - core) * half]

    def cols(value):
        return [lax.dynamic_slice_in_dim(value, at, half, 1) for at in col]

    def join(own, other):
        first = core == 0
        return jnp.concatenate([jnp.where(first, own, other), jnp.where(first, other, own)], 1)

    n1 = cols(norm1)

    def project(t, lhs):
        return dot(lhs[0], w_att[0][t], 1, 1) + dot(lhs[1], w_att[1][t], 1, 1)

    q = (project(0, [v[halo:] for v in n1]) + q_bias).astype(bf16)
    k = project(2, n1).astype(bf16)
    v = (project(3, n1) + v_bias).astype(bf16)

    seg_row = jnp.concatenate([jnp.full((1, halo), -1, jnp.int32), segment_ids], 1)
    segk = lax.dynamic_slice_in_dim(seg_row, m * rows, halo + rows, 1)
    segq = segk[:, halo:]
    segk = segk.reshape(halo + rows, 1)

    q, ff_x0 = tie((q, ff_x0))
    ff_x1 = hop(ff_x0, 1)
    cut = rest * piece
    z1 = jnp.concatenate([ff_x0[:cut], ff_x1[:cut]])
    z2 = jnp.concatenate([ff_x0[cut:], ff_x1[cut:]])
    y1, y2 = hop(z1, 2), hop(z2, 2)
    w1 = [own1, z1, y1, swap(z1, 0), swap(y1, 0)]
    w2 = [own2, z2, y2, swap(z2, 0), swap(y2, 0)]

    context, lse = attend(slopes, segq, segk, q, k, v)
    attention = join(dot(context, w_att[0][1], 1, 0), dot(context, w_att[1][1], 1, 0))
    tokens_wide = tokens.astype(f32)
    resid = attention + out_bias + tokens_wide
    xhat2, rstd2 = norm_parts(resid)
    norm2 = (xhat2 * norm2_gain + norm2_shift).astype(bf16)

    pre, at = [], 0
    for w in w1:
        pre.append(dot(norm2, w, 1, 1) + fc1_b[at : at + w.shape[0]])
        at += w.shape[0]
    hidden = [gelu_both(p)[0].astype(bf16) for p in pre]

    def partials(lhs, rhs):
        send = [lhs[3], lhs[4], lhs[0][:, 4 * piece :]]
        return [dot(v, rhs, 0, 0).astype(bf16) for v in send]

    def after_core(lhs, rhs, got):
        hi = jnp.concatenate(
            [
                (dot(lhs[2], rhs, 0, 0) + got[1].astype(f32)).astype(bf16),
                (dot(lhs[0][:, 2 * piece : 4 * piece], rhs, 0, 0) + got[2][2 * piece :].astype(f32)).astype(bf16),
            ]
        )
        lo = [
            (dot(lhs[1], rhs, 0, 0) + got[0].astype(f32)).astype(bf16),
            (dot(lhs[0][:, : 2 * piece], rhs, 0, 0) + got[2][: 2 * piece].astype(f32)).astype(bf16),
        ]
        return hi, lo

    def after_hop2(lo, got):
        send = jnp.concatenate([add(lo[0][cut:], got[cut : 2 * cut]), add(lo[1][piece:], got[2 * cut + piece :])])
        keep = [add(lo[0][:cut], got[:cut]), add(lo[1][:piece], got[2 * cut : 2 * cut + piece])]
        return send, keep

    def along_mp(keep, got):
        near = add(keep[0][:piece], got[:piece])
        far = add(keep[0][piece:], got[piece:cut])
        mine = keep[1].astype(f32) + got[cut:].astype(f32)
        far = add(far, move(far, INWARD))
        back = move(far, MIDDLE)
        mine = mine + back[:piece].astype(f32)
        near = add(near, back[piece:])
        return beyond(mine + move(near, NEAR).astype(f32)).astype(bf16)

    send2 = partials(hidden, out_grad)
    got2 = [swap(v, 0) for v in send2]
    mlp = sum(dot(h, w, 1, 0) for h, w in zip(hidden, w2))
    result = (mlp + fc2_bias + resid).astype(bf16)
    grad_pre = [
        (dot(out_grad, w, 1, 1) * gelu_both(p)[1]).astype(bf16) for w, p in zip(w2, pre)
    ]
    send1 = partials(grad_pre, norm2)
    got1 = [swap(v, 0) for v in send1]
    hi2, lo2 = after_core(hidden, out_grad, got2)
    hop2_2 = hop(hi2, 2)

    grad_norm2 = sum(dot(g, w, 1, 0) for g, w in zip(grad_pre, w1))
    out_grad_wide = out_grad.astype(f32)
    grad_resid = out_grad_wide + norm_back(grad_norm2, norm2_gain, xhat2, rstd2)
    hi1, lo1 = after_core(grad_pre, norm2, got1)
    grad_att = cols(grad_resid.astype(bf16))
    grad_context = (
        dot(grad_att[0], w_att[0][1], 1, 1) + dot(grad_att[1], w_att[1][1], 1, 1)
    ).astype(bf16)

    grad_context, hi1, hop2_2 = tie((grad_context, hi1, hop2_2))
    hop2_1 = hop(hi1, 2)
    send2, keep2 = after_hop2(lo2, hop2_2)
    hop1_2 = hop(send2, 1)
    dq, dk, dv = attend_back(slopes, segq, segk, q, k, v, grad_context, lse)
    dq, hop2_1, hop1_2 = tie((dq, hop2_1, hop1_2))
    send1, keep1 = after_hop2(lo1, hop2_1)
    hop1_1 = hop(send1, 1)
    sum2 = along_mp(keep2, hop1_2)

    def weights_half(i):
        return [
            dot(dq, n1[i][halo:], 0, 0).astype(bf16),
            dot(context, grad_att[i], 0, 0).astype(bf16),
            dot(dk, n1[i], 0, 0).astype(bf16),
            dot(dv, n1[i], 0, 0).astype(bf16),
        ]

    theirs = [swap(v, 0) for v in weights_half(1)]
    mine = weights_half(0)
    slots = jnp.where(core == 0, jnp.asarray([2, 3, 0, 1]), jnp.asarray([1, 3, 0, 2]))
    att_hi, att_lo = add_att(slots, mine, theirs)
    att_got = hop(att_hi, 2)
    sum1 = along_mp(keep1, hop1_1)
    ff_sums = all_eight(jnp.stack([sum1, sum2]))
    att_keep = add(att_lo[0], att_got[0]), add(att_lo[1], att_got[1])
    att_keep = add(att_keep[0], hop(att_keep[1], 1)).reshape(4, mp, HD, half)
    att_sum = att_keep[:, 0].astype(f32)
    for s in range(1, mp):
        att_sum = att_sum + shift(att_keep[:, s], mp - s).astype(f32)
    att_sum = all_eight(beyond(att_sum).astype(bf16))
    att_sum = att_sum.reshape(4, 2, 4, HD, half)
    grad_out = jnp.transpose(att_sum[:, :, 1], (0, 2, 1, 3)).reshape(4 * HD, wide).astype(f32)
    grad_qkv = jnp.transpose(
        jnp.stack([att_sum[:, :, 0], att_sum[:, :, 2], att_sum[:, :, 3]]), (2, 4, 0, 1, 3)
    ).reshape(wide, 3, 4 * HD).astype(f32)
    grad_fc1 = ff_sums[:, 0].reshape(ff_here, wide).T.astype(f32)
    grad_fc2 = ff_sums[:, 1].reshape(ff_here, wide).astype(f32)

    def back_half(i):
        tail = dot(dk, w_att[i][2], 1, 0) + dot(dv, w_att[i][3], 1, 0)
        return tail[:halo], tail[halo:] + dot(dq, w_att[i][0], 1, 0)

    back = [back_half(0), back_half(1)]
    grad_halo = join(back[0][0], back[1][0])
    grad_norm1 = join(back[0][1], back[1][1])
    down = [(i, i - 1) for i in range(1, mp)]
    passed = move(grad_halo[:near_rows].astype(bf16), down).astype(f32)
    near = grad_halo[near_rows:]
    near = jnp.concatenate([near[: rows - near_rows], near[rows - near_rows :] + passed])
    grad_norm1 = grad_norm1 + move(near.astype(bf16), down).astype(f32)
    xhat1, rstd1 = xhat_ext[halo:], rstd_ext[halo:]
    in_grad = grad_resid + norm_back(grad_norm1, norm1_gain, xhat1, rstd1)

    ff_bias = jnp.concatenate([jnp.sum(g.astype(f32), axis=0) for g in grad_pre])
    ff_bias = ff_bias.reshape(mp * 8, piece)
    qv_sums = jnp.concatenate(
        [jnp.sum(g.astype(f32), axis=0).reshape(mp * heads_here, HD) for g in (dq, dv[:, :])], 1
    )

    def in_order(table, at):
        n = table.shape[0]
        pick = (at[None, :] == jnp.arange(n)[:, None]).astype(f32)
        return lax.dot(pick, table, precision=lax.Precision.HIGHEST)

    small = jnp.stack(
        [
            jnp.sum(grad_resid, axis=0),
            jnp.sum(grad_norm1 * xhat1, axis=0),
            jnp.sum(grad_norm1, axis=0),
            jnp.sum(grad_norm2 * xhat2, axis=0),
            jnp.sum(grad_norm2, axis=0),
            jnp.sum(out_grad_wide, axis=0),
        ]
    )
    n_small = wide // mp
    vectors = jnp.concatenate(
        [
            jnp.transpose(small.reshape(6, mp, n_small), (1, 0, 2)).reshape(mp, -1),
            in_order(qv_sums, heads).reshape(mp, -1),
            in_order(ff_bias, ff_rows).reshape(mp, -1),
        ],
        1,
    )
    vectors = lax.psum(vectors, ("dp", "mp"))
    total = lax.dynamic_index_in_dim(vectors, m, 0, False)
    six = total[: 6 * n_small].reshape(6, n_small)
    n_qv = heads_here * HD
    grad_qv = total[6 * n_small : 6 * n_small + 2 * n_qv].reshape(heads_here, 2, HD)
    grad_qv = jnp.transpose(grad_qv, (1, 0, 2)).reshape(2, n_qv)
    grad_fc1_bias = total[6 * n_small + 2 * n_qv :]
    return (
        result,
        in_grad,
        six[1],
        six[2],
        grad_qkv,
        grad_qv,
        grad_out,
        six[0],
        six[3],
        six[4],
        grad_fc1,
        grad_fc1_bias,
        grad_fc2,
        six[5],
    )


def solution(mesh):
    placed = (
        P(("dp", "mp"), None),
        P("dp", None),
        P(),
        P(),
        P(None, None, "mp"),
        P(None, "mp"),
        P("mp", None),
        P(),
        P(),
        P(),
        P(None, "mp"),
        P("mp"),
        P("mp", None),
        P(),
        P(("dp", "mp"), None),
    )
    return jax.shard_map(
        body,
        mesh=mesh,
        in_specs=placed,
        out_specs=(
            P(("dp", "mp"), None),
            P(("dp", "mp"), None),
            P("mp"),
            P("mp"),
            P(None, None, "mp"),
            P(None, "mp"),
            P("mp", None),
            P("mp"),
            P("mp"),
            P("mp"),
            P(None, "mp"),
            P("mp"),
            P("mp", None),
            P("mp"),
        ),
        check_vma=False,
    )
```

```python
import functools

import jax
import jax.numpy as jnp
from jax import lax
from jax.experimental import pallas as pl
from jax.experimental.pallas import tpu as pltpu
from jax.sharding import PartitionSpec as P

HEADS = 16
HD = 64
DOC_MOST = 768
QB = 256
MASKED = -1e12
SMALL = pl.CostEstimate(flops=1, bytes_accessed=1, transcendentals=1)
eps = 1e-05
f32 = jnp.float32
bf16 = jnp.bfloat16


def dot(a, b, ca, cb):
    return lax.dot_general(a, b, (((ca,), (cb,)), ((), ())), preferred_element_type=f32)


def fill_mask(segq_ref, segk_ref, mask_ref, window, halo):
    for i in range(mask_ref.shape[0]):
        key_at = lax.broadcasted_iota(jnp.int32, (window, QB), 0) + i * QB
        query_at = lax.broadcasted_iota(jnp.int32, (window, QB), 1) + (i * QB + halo)
        same = segk_ref[i * QB : i * QB + window, :] == segq_ref[:, i * QB : (i + 1) * QB]
        allowed = same & (key_at <= query_at)
        mask_ref[i] = jnp.where(allowed, (key_at - query_at).astype(f32), MASKED)


def halves(rows):
    lane = lax.broadcasted_iota(jnp.int32, (rows, 2 * HD), 1)
    return [lane < HD, lane >= HD]


def attend_kernel(halo, start, slopes, segq, segk, q_ref, k_ref, v_ref, *refs):
    o_ref, lse_ref, mask_ref = refs[-3:]
    window = halo + QB
    pair = start + pl.program_id(0)

    @pl.when(pair == start)
    def _():
        fill_mask(segq, segk, mask_ref, window, halo)

    v_t = v_ref[...].T
    pick = halves(QB)
    for i in range(mask_ref.shape[0]):
        rows = slice(i * QB, (i + 1) * QB)
        keys = slice(i * QB, i * QB + window)
        query = q_ref[rows, :] * jnp.asarray(HD**-0.5, bf16)
        key_rows = k_ref[keys, :]
        out = []
        for h in range(2):
            q_h = jnp.where(pick[h], query, jnp.zeros_like(query))
            scores = dot(key_rows, q_h, 1, 1) + slopes[2 * pair + h] * mask_ref[i]
            top = jnp.max(scores, axis=0, keepdims=True)
            expo = jnp.exp(scores - top)
            total = jnp.sum(expo, axis=0, keepdims=True)
            o_t = dot(v_t[:, keys], expo.astype(bf16), 1, 0)
            out.append(o_t[h * HD : (h + 1) * HD, :] * (1.0 / total))
            lse_ref[0, h : h + 1, rows] = top + jnp.log(total)
        o_ref[rows, :] = jnp.concatenate(out, axis=0).T.astype(bf16)


def attend_back_kernel(halo, start, slopes, segq, segk, q_ref, k_ref, v_ref, g_ref, lse_ref, *refs):
    dq_ref, dk_ref, dv_ref, mask_ref, dk_acc, dv_acc = refs[-6:]
    window = halo + QB
    pair = start + pl.program_id(0)

    @pl.when(pair == start)
    def _():
        fill_mask(segq, segk, mask_ref, window, halo)

    k_t = k_ref[...].T
    pick = halves(QB)
    dk_acc[...] = jnp.zeros_like(dk_acc)
    dv_acc[...] = jnp.zeros_like(dv_acc)
    for i in range(mask_ref.shape[0]):
        rows = slice(i * QB, (i + 1) * QB)
        keys = slice(i * QB, i * QB + window)
        query = q_ref[rows, :] * jnp.asarray(HD**-0.5, bf16)
        grad = g_ref[rows, :]
        key_rows = k_ref[keys, :]
        value_rows = v_ref[keys, :]
        out = []
        for h in range(2):
            q_h = jnp.where(pick[h], query, jnp.zeros_like(query))
            g_h = jnp.where(pick[h], grad, jnp.zeros_like(grad))
            scores = dot(key_rows, q_h, 1, 1) + slopes[2 * pair + h] * mask_ref[i]
            probs = jnp.exp(scores - lse_ref[0, h : h + 1, rows])
            grad_probs = dot(value_rows, g_h, 1, 1)
            delta = jnp.sum(probs * grad_probs, axis=0, keepdims=True)
            grad_scores = (probs * (grad_probs - delta)).astype(bf16)
            dv_acc[keys, :] += dot(probs.astype(bf16), g_h, 1, 0)
            dk_acc[keys, :] += dot(grad_scores, q_h, 1, 0)
            dq_t = dot(k_t[:, keys], grad_scores, 1, 0)
            out.append(dq_t[h * HD : (h + 1) * HD, :])
        dq_ref[rows, :] = (jnp.concatenate(out, axis=0).T * HD**-0.5).astype(bf16)
    dk_ref[...] = dk_acc[...].astype(bf16)
    dv_ref[...] = dv_acc[...].astype(bf16)


def attend(part, slopes, segq, segk, q, k, v, before=()):
    rows, wide = q.shape
    ext = k.shape[0]
    halo = ext - rows
    pairs = wide // (2 * HD)
    blocks = rows // QB
    start = part * (pairs // 2)
    col = lambda n: pl.BlockSpec((n, 2 * HD), lambda p: (0, p + start))
    return pl.pallas_call(
        functools.partial(attend_kernel, halo, start),
        grid=(pairs // 2,),
        in_specs=[
            pl.BlockSpec(memory_space=pltpu.SMEM),
            pl.BlockSpec((1, rows), lambda p: (0, 0)),
            pl.BlockSpec((ext, 1), lambda p: (0, 0)),
            col(rows),
            col(ext),
            col(ext),
        ]
        + [pl.BlockSpec(memory_space=pl.ANY)] * len(before),
        out_specs=[col(rows), pl.BlockSpec((1, 2, rows), lambda p: (p + start, 0, 0))],
        out_shape=[
            jax.ShapeDtypeStruct((rows, wide), bf16),
            jax.ShapeDtypeStruct((pairs, 2, rows), f32),
        ],
        input_output_aliases={6 + i: i for i in range(len(before))},
        scratch_shapes=[pltpu.VMEM((blocks, halo + QB, QB), f32)],
        compiler_params=pltpu.CompilerParams(vmem_limit_bytes=40 << 20),
        cost_estimate=SMALL,
    )(slopes, segq, segk, q, k, v, *before)


def attend_back(part, slopes, segq, segk, q, k, v, grad, lse, before=()):
    rows, wide = q.shape
    ext = k.shape[0]
    halo = ext - rows
    pairs = wide // (2 * HD)
    blocks = rows // QB
    start, stop = [pairs * i // 8 for i in (0, 3, 6, 8)][part : part + 2]
    col = lambda n: pl.BlockSpec((n, 2 * HD), lambda p: (0, p + start))
    return pl.pallas_call(
        functools.partial(attend_back_kernel, halo, start),
        grid=(stop - start,),
        in_specs=[
            pl.BlockSpec(memory_space=pltpu.SMEM),
            pl.BlockSpec((1, rows), lambda p: (0, 0)),
            pl.BlockSpec((ext, 1), lambda p: (0, 0)),
            col(rows),
            col(ext),
            col(ext),
            col(rows),
            pl.BlockSpec((1, 2, rows), lambda p: (p + start, 0, 0)),
        ]
        + [pl.BlockSpec(memory_space=pl.ANY)] * len(before),
        out_specs=[col(rows), col(ext), col(ext)],
        out_shape=[
            jax.ShapeDtypeStruct((rows, wide), bf16),
            jax.ShapeDtypeStruct((ext, wide), bf16),
            jax.ShapeDtypeStruct((ext, wide), bf16),
        ],
        input_output_aliases={8 + i: i for i in range(len(before))},
        scratch_shapes=[
            pltpu.VMEM((blocks, halo + QB, QB), f32),
            pltpu.VMEM((ext, 2 * HD), f32),
            pltpu.VMEM((ext, 2 * HD), f32),
        ],
        compiler_params=pltpu.CompilerParams(vmem_limit_bytes=48 << 20),
        cost_estimate=SMALL,
    )(slopes, segq, segk, q, k, v, grad, lse, *before)


def own_att_kernel(at, qkv_ref, out_ref, *own_refs):
    for t, rows in enumerate((qkv_ref[0], out_ref[...], qkv_ref[1], qkv_ref[2])):
        half = rows.shape[1] // 2
        left, right = rows[:, :half], rows[:, half:]
        own_refs[0][t, 0] = jnp.where(at[0] == 0, left, right)
        if len(own_refs) == 2:
            own_refs[1][t, 0] = jnp.where(at[0] == 0, right, left)


def own_att(halves, at, qkv_t, out_weight):
    wide = out_weight.shape[1]
    places = 4 if halves == 2 else 1
    return pl.pallas_call(
        own_att_kernel,
        grid_spec=pltpu.PrefetchScalarGridSpec(
            num_scalar_prefetch=1,
            grid=(places,),
            in_specs=[
                pl.BlockSpec((3, HD, wide), lambda p, at: (0, at[1 + p], 0)),
                pl.BlockSpec((HD, wide), lambda p, at: (at[1 + p], 0)),
            ],
            out_specs=[pl.BlockSpec((4, 1, HD, wide // 2), lambda p, at: (0, p, 0, 0))] * halves,
        ),
        cost_estimate=SMALL,
        out_shape=[jax.ShapeDtypeStruct((4, places, HD, wide // 2), bf16)] * halves,
    )(at, qkv_t, out_weight)


def me_ff_kernel(at, fc1_ref, fc2_ref, me1_ref, me2_ref):
    me1_ref[...] = fc1_ref[...].T
    me2_ref[...] = fc2_ref[...]


def me_ff(at, fc1_weight, fc2_weight):
    hidden, wide = fc2_weight.shape
    piece = hidden // 8
    return pl.pallas_call(
        me_ff_kernel,
        grid_spec=pltpu.PrefetchScalarGridSpec(
            num_scalar_prefetch=1,
            grid=(1,),
            in_specs=[
                pl.BlockSpec((wide, piece), lambda i, at: (0, at[0])),
                pl.BlockSpec((piece, wide), lambda i, at: (at[0], 0)),
            ],
            out_specs=[pl.BlockSpec((piece, wide), lambda i, at: (0, 0))] * 2,
        ),
        cost_estimate=SMALL,
        out_shape=[jax.ShapeDtypeStruct((piece, wide), bf16)] * 2,
    )(at, fc1_weight, fc2_weight)


def own_ff_kernel(at, fc1_ref, fc2_ref, o1_ref, o2_ref):
    o1_ref[...] = fc1_ref[...]
    o2_ref[...] = fc2_ref[...]


def own_ff(at, fc1_weight, fc2_weight):
    hidden, wide = fc2_weight.shape
    piece = hidden // 8
    return pl.pallas_call(
        own_ff_kernel,
        grid_spec=pltpu.PrefetchScalarGridSpec(
            num_scalar_prefetch=1,
            grid=(8,),
            in_specs=[
                pl.BlockSpec((wide, piece), lambda i, at: (0, at[i])),
                pl.BlockSpec((piece, wide), lambda i, at: (at[i], 0)),
            ],
            out_specs=[
                pl.BlockSpec((wide, piece), lambda i, at: (0, i)),
                pl.BlockSpec((piece, wide), lambda i, at: (i, 0)),
            ],
        ),
        cost_estimate=SMALL,
        out_shape=[
            jax.ShapeDtypeStruct((wide, hidden), bf16),
            jax.ShapeDtypeStruct((hidden, wide), bf16),
        ],
    )(at, fc1_weight, fc2_weight)


def join_att_kernel(exchanged, own_ref, x0_ref, x1_ref, y_ref, *out_refs):
    hops = (y_ref[0], x1_ref[...]) if exchanged else (x1_ref[...], y_ref[0])
    for t, out_ref in enumerate(out_refs):
        out_ref[:, 0] = own_ref[t]
        for place, rest in enumerate((x0_ref[...], *hops, y_ref[1])):
            out_ref[place, 1:] = rest[:, t]


def join_att(own, x0, x1, y, exchanged=False):
    rest, _, hd, half = x0.shape
    step = hd // 4
    one = pl.BlockSpec((rest, 4, step, half), lambda i: (0, 0, i, 0))
    return pl.pallas_call(
        functools.partial(join_att_kernel, exchanged),
        grid=(4,),
        in_specs=[
            pl.BlockSpec((4, 4, step, half), lambda i: (0, 0, i, 0)),
            one,
            one,
            pl.BlockSpec((2, rest, 4, step, half), lambda i: (0, 0, 0, i, 0)),
        ],
        out_specs=[pl.BlockSpec((4, rest + 1, step, half), lambda i: (0, 0, i, 0))] * 4,
        cost_estimate=SMALL,
        out_shape=[jax.ShapeDtypeStruct((4, rest + 1, hd, half), bf16)] * 4,
    )(own, x0, x1, y)


def add_att_kernel(*refs):
    mine, theirs, (hi_ref, lo_ref) = refs[:4], refs[4:8], refs[8:]
    i = pl.program_id(0)
    for t in range(4):
        total = (mine[t][...].astype(f32) + theirs[t][...].astype(f32)).astype(bf16)

        @pl.when(i < 2)
        def _():
            hi_ref[0, t] = total

        @pl.when(i >= 2)
        def _():
            lo_ref[0, t] = total


def add_att(mine, theirs):
    rows, half = mine[0].shape
    ours = pl.BlockSpec((rows // 4, half), lambda i: ((i + 2) % 4, 0))
    got = pl.BlockSpec((rows // 4, half), lambda i: ((2 * i + 1) % 4 - i // 2, 0))
    shape = jax.ShapeDtypeStruct((2, 4, rows // 4, half), bf16)
    return pl.pallas_call(
        add_att_kernel,
        grid=(4,),
        in_specs=[ours] * 4 + [got] * 4,
        out_specs=[
            pl.BlockSpec((1, 4, rows // 4, half), lambda i: (jnp.minimum(i, 1), 0, 0, 0)),
            pl.BlockSpec((1, 4, rows // 4, half), lambda i: (jnp.maximum(i - 2, 0), 0, 0, 0)),
        ],
        cost_estimate=SMALL,
        out_shape=[shape, shape],
    )(*mine, *theirs)


def last_att_kernel(at, left_ref, right_ref, out_ref, qkv_ref):
    rows = jnp.concatenate([left_ref[0], right_ref[0]], axis=-1).astype(f32)
    out_ref[...] = rows[1]
    qkv_ref[0], qkv_ref[1], qkv_ref[2] = rows[0], rows[2], rows[3]


def last_att(at, pieces):
    _, _, hd, half = pieces.shape
    block = lambda c: pl.BlockSpec((1, 4, hd, half), lambda p, at: (at[2 * p + c], 0, 0, 0))
    return pl.pallas_call(
        last_att_kernel,
        grid_spec=pltpu.PrefetchScalarGridSpec(
            num_scalar_prefetch=1,
            grid=(4,),
            in_specs=[block(0), block(1)],
            out_specs=[
                pl.BlockSpec((hd, 2 * half), lambda p, at: (p, 0)),
                pl.BlockSpec((3, hd, 2 * half), lambda p, at: (0, p, 0)),
            ],
        ),
        cost_estimate=SMALL,
        out_shape=[
            jax.ShapeDtypeStruct((4 * hd, 2 * half), f32),
            jax.ShapeDtypeStruct((3, 4 * hd, 2 * half), f32),
        ],
    )(at, pieces, pieces)


def swap(value, b):
    n = lax.axis_size("dp")
    return lax.ppermute(value, "dp", [(i, i ^ (1 << b)) for i in range(n)])


def hop(value, stage):
    n = lax.axis_size("dp")
    return lax.ppermute(
        value, "dp", [(i, i ^ (2 if (i & 1) == stage - 1 else 4)) for i in range(n)]
    )


def move(value, pairs):
    return lax.ppermute(value, "mp", pairs)


def shift(value, s):
    n = lax.axis_size("mp")
    return move(value, [(i, (i + s) % n) for i in range(n)])


def all_eight(value):
    n = lax.axis_size("dp")
    groups = None if n == 8 else [list(range(g, g + 8)) for g in range(0, n, 8)]
    return lax.all_gather(value, "dp", axis=0, axis_index_groups=groups)


def beyond(value):
    for b in range(3, lax.axis_size("dp").bit_length() - 1):
        value = value + swap(value, b)
    return value


def add(a, b):
    return (a.astype(f32) + b.astype(f32)).astype(bf16)


tie = lax.optimization_barrier


def norm_parts(rows):
    mean = jnp.mean(rows, axis=-1, keepdims=True)
    centred = rows - mean
    rstd = lax.rsqrt(jnp.mean(centred * centred, axis=-1, keepdims=True) + eps)
    return centred * rstd, rstd


def norm_back(grad, gain, xhat, rstd):
    scaled = grad * gain
    return rstd * (
        scaled
        - jnp.mean(scaled, axis=-1, keepdims=True)
        - xhat * jnp.mean(scaled * xhat, axis=-1, keepdims=True)
    )


def gelu_both(v):
    c, k = 0.7978845608028654, 0.044715
    t = jnp.tanh(c * (v + k * v * v * v))
    value = 0.5 * v * (1.0 + t)
    slope = 0.5 * (1.0 + t) + 0.5 * v * (1.0 - t * t) * (c * (1.0 + 3.0 * k * v * v))
    return value, slope


def body(
    tokens,
    segment_ids,
    norm1_gain,
    norm1_shift,
    qkv_weight,
    qv_bias,
    out_weight,
    out_bias,
    norm2_gain,
    norm2_shift,
    fc1_weight,
    fc1_bias,
    fc2_weight,
    fc2_bias,
    out_grad,
):
    rows, wide = tokens.shape
    half = wide // 2
    mp = lax.axis_size("mp")
    m = lax.axis_index("mp")
    d = lax.axis_index("dp") & 7
    core = d & 1
    ff_here = fc1_weight.shape[1]
    piece = ff_here // 8
    heads_here = qkv_weight.shape[2] // HD
    rest = mp - 1

    def slice_at(k):
        first = jnp.where((core ^ (k >> 2)) == 0, 2, 4)
        return d ^ ((k >> 2) + (k & 1) * first + ((k >> 1) & 1) * (6 - first))

    slices = slice_at(jnp.arange(8))
    place = slice_at(jnp.arange(4)) >> 1
    row = jnp.arange(mp * 8)
    other = jnp.maximum(row - 8, 0)
    shifts = jnp.where(row < 8, 0, other % rest + 1)
    lies_at = slice_at(jnp.where(row < 8, row, other // rest))
    ff_rows = (m + mp - shifts) % mp * 8 + lies_at
    ff_from = shifts * 8 + lies_at
    head = jnp.arange(mp * heads_here)
    head_place = slice_at(head // mp) >> 1
    heads = (m + mp - head % mp) % mp * heads_here + head_place
    heads_from = head % mp * heads_here + head_place
    slopes = jnp.exp2(-8.0 * (heads + 1).astype(f32) / HEADS)

    def pick(table, at):
        n = table.shape[0]
        chosen = (at[:, None] == jnp.arange(n)[None, :]).astype(f32)
        return lax.dot(chosen, table, precision=lax.Precision.HIGHEST)

    near_rows = DOC_MOST - rows
    halo = DOC_MOST
    qv_own = jnp.transpose(qv_bias.reshape(2, heads_here, HD), (1, 0, 2))
    bias_own = jnp.concatenate([fc1_bias.reshape(8, piece), qv_own.reshape(heads_here, 2 * HD)])
    bias_all = [bias_own] + [shift(bias_own, s) for s in range(1, mp)]
    qkv_t = jnp.transpose(qkv_weight, (1, 2, 0))
    att_places = jnp.concatenate([core[None], place])
    (att_me,) = own_att(1, att_places, qkv_t, out_weight)
    att_me = att_me.reshape(4, HD, half)
    att_z = [shift(att_me, s) for s in range(1, mp)]
    halo1 = move(tokens, [(i, i + 1) for i in range(mp - 1)])
    fc1_b = pick(jnp.concatenate([v[:8] for v in bias_all]), ff_from).reshape(-1)
    qv_b = pick(jnp.concatenate([v[8:] for v in bias_all]), heads_from)
    q_bias, v_bias = qv_b[:, :HD].reshape(-1), qv_b[:, HD:].reshape(-1)
    seg_row = jnp.concatenate([jnp.full((1, halo), -1, jnp.int32), segment_ids], 1)
    segk = lax.dynamic_slice_in_dim(seg_row, m * rows, halo + rows, 1)
    segq = segk[:, halo:]
    segk = segk.reshape(halo + rows, 1)

    small_ones = (fc1_b, q_bias, v_bias, segk, segq, slopes)
    att_z, halo1, small_ones, slices, att_places = tie(
        (att_z, halo1, small_ones, slices, att_places)
    )
    fc1_b, q_bias, v_bias, segk, segq, slopes = small_ones
    halo2 = move(halo1[rows - near_rows :], [(i, i + 1) for i in range(mp - 1)])
    att_x0 = jnp.stack(att_z)
    att_x1 = hop(att_x0, 1)
    me1, me2 = me_ff(slices, fc1_weight, fc2_weight)
    own = own_att(2, att_places, qkv_t, out_weight)
    own1, own2 = own_ff(slices, fc1_weight, fc2_weight)
    att_x1, halo2, me1, me2, own, own1, own2 = tie((att_x1, halo2, me1, me2, own, own1, own2))
    z1 = [shift(me1, s) for s in range(1, mp)]
    part0 = swap(att_x0, 0)
    att_y = hop(jnp.stack([att_x0, att_x1]), 2)
    part1 = swap(att_x1, 0)
    ext = jnp.concatenate([halo2, halo1, tokens], 0).astype(f32)
    xhat_ext, rstd_ext = norm_parts(ext)
    norm1 = (xhat_ext * norm1_gain + norm1_shift).astype(bf16)
    col = [core * half, (1 - core) * half]

    def cols(value):
        return [lax.dynamic_slice_in_dim(value, at, half, 1) for at in col]

    def join(own, other):
        first = core == 0
        return jnp.concatenate([jnp.where(first, own, other), jnp.where(first, other, own)], 1)

    n1 = cols(norm1)
    att_y, part0, part1, z1, n1 = tie((att_y, part0, part1, z1, n1))
    z2 = [shift(me2, s) for s in range(1, mp)]
    part_y = swap(att_y, 0)
    w_att = [
        join_att(own[0], att_x0, att_x1, att_y),
        join_att(own[1], part0, part1, part_y, True),
    ]
    w_att = [[w.reshape(HEADS * HD, half) for w in four] for four in w_att]

    def project(t, lhs):
        return dot(lhs[0], w_att[0][t], 1, 1) + dot(lhs[1], w_att[1][t], 1, 1)

    q = (project(0, [v[halo:] for v in n1]) + q_bias).astype(bf16)
    k = project(2, n1).astype(bf16)
    v = (project(3, n1) + v_bias).astype(bf16)

    cut = rest * piece

    x0_1 = jnp.concatenate(z1)
    q, x0_1, z2 = tie((q, x0_1, z2))
    x1_1 = hop(x0_1, 1)
    first = attend(0, slopes, segq, segk, q, k, v)
    first, x1_1, z2 = tie((first, x1_1, z2))
    x0_2 = jnp.concatenate(z2)
    z1 = jnp.concatenate([x0_1, x1_1])
    y1 = hop(z1, 2)
    x1_2 = hop(x0_2, 1)
    context, lse = attend(1, slopes, segq, segk, q, k, v, first)
    context, y1, x1_2 = tie((context, y1, x1_2))
    z2 = jnp.concatenate([x0_2, x1_2])
    y2 = hop(z2, 2)
    w1 = [z1, y1, swap(z1, 0), swap(y1, 0)]
    w2 = [z2, y2, swap(z2, 0), swap(y2, 0)]
    attention = join(dot(context, w_att[0][1], 1, 0), dot(context, w_att[1][1], 1, 0))
    tokens_wide = tokens.astype(f32)
    resid = attention + out_bias + tokens_wide
    xhat2, rstd2 = norm_parts(resid)
    norm2 = (xhat2 * norm2_gain + norm2_shift).astype(bf16)

    pre, at = [dot(norm2, own1, 1, 0) + fc1_b[:ff_here]], ff_here
    for w in w1:
        pre.append(dot(norm2, w, 1, 1) + fc1_b[at : at + w.shape[0]])
        at += w.shape[0]
    hidden = [gelu_both(p)[0].astype(bf16) for p in pre]

    def partials(lhs, rhs):
        send = [lhs[3], lhs[4], lhs[0][:, 4 * piece :]]
        return [dot(v, rhs, 0, 0).astype(bf16) for v in send]

    def after_core(lhs, rhs, got):
        hi = jnp.concatenate(
            [
                (dot(lhs[2], rhs, 0, 0) + got[1].astype(f32)).astype(bf16),
                (dot(lhs[0][:, 2 * piece : 4 * piece], rhs, 0, 0) + got[2][2 * piece :].astype(f32)).astype(bf16),
            ]
        )
        lo = [
            (dot(lhs[1], rhs, 0, 0) + got[0].astype(f32)).astype(bf16),
            (dot(lhs[0][:, : 2 * piece], rhs, 0, 0) + got[2][: 2 * piece].astype(f32)).astype(bf16),
        ]
        return hi, lo

    def after_hop2(lo, got):
        send = jnp.concatenate([add(lo[0][cut:], got[cut : 2 * cut]), add(lo[1][piece:], got[2 * cut + piece :])])
        keep = [add(lo[0][:cut], got[:cut]), add(lo[1][:piece], got[2 * cut : 2 * cut + piece])]
        return send, keep

    def to_mp(keep, got):
        sent = [
            shift(add(keep[0][at : at + piece], got[at : at + piece]), mp - 1 - at // piece)
            for at in range(0, cut, piece)
        ]
        return sent, keep[1].astype(f32) + got[cut:].astype(f32)

    def all_mp(sent, mine):
        for got in sent:
            mine = mine + got.astype(f32)
        return beyond(mine).astype(bf16)

    send2 = partials(hidden, out_grad)
    got2 = [swap(v, 0) for v in send2]
    mlp = sum(dot(h, w, 1, 0) for h, w in zip(hidden, [own2] + w2))
    result = (mlp + fc2_bias + resid).astype(bf16)
    grad_pre = [
        (dot(out_grad, w, 1, 1) * gelu_both(p)[1]).astype(bf16) for w, p in zip([own2] + w2, pre)
    ]
    send1 = partials(grad_pre, norm2)
    got1 = [swap(v, 0) for v in send1]
    hi2, lo2 = after_core(hidden, out_grad, got2)
    hop2_2 = hop(hi2, 2)

    grad_norm2 = dot(grad_pre[0], own1, 1, 1)
    grad_norm2 = grad_norm2 + sum(dot(g, w, 1, 0) for g, w in zip(grad_pre[1:], w1))
    out_grad_wide = out_grad.astype(f32)
    grad_resid = out_grad_wide + norm_back(grad_norm2, norm2_gain, xhat2, rstd2)
    hi1, lo1 = after_core(grad_pre, norm2, got1)
    grad_att = cols(grad_resid.astype(bf16))
    grad_context = (
        dot(grad_att[0], w_att[0][1], 1, 1) + dot(grad_att[1], w_att[1][1], 1, 1)
    ).astype(bf16)

    grad_context, hi1, hi2 = tie((grad_context, hi1, hi2))
    hop2_1 = hop(hi1, 2)
    first = attend_back(0, slopes, segq, segk, q, k, v, grad_context, lse)
    first, hop2_2 = tie((first, hop2_2))
    send2, keep2 = after_hop2(lo2, hop2_2)
    hop1_2 = hop(send2, 1)
    second = attend_back(1, slopes, segq, segk, q, k, v, grad_context, lse, first)
    second, hop2_1, hop1_2 = tie((second, hop2_1, hop1_2))
    send1, keep1 = after_hop2(lo1, hop2_1)
    hop1_1 = hop(send1, 1)
    z2, mine2 = to_mp(keep2, hop1_2)
    grads = attend_back(2, slopes, segq, segk, q, k, v, grad_context, lse, second)
    (dq, dk, dv), hop1_1, z2 = tie((grads, hop1_1, z2))
    z1, mine1 = to_mp(keep1, hop1_1)
    sum2 = all_mp(z2, mine2)

    def weights_half(i):
        return [
            dot(dq, n1[i][halo:], 0, 0).astype(bf16),
            dot(context, grad_att[i], 0, 0).astype(bf16),
            dot(dk, n1[i], 0, 0).astype(bf16),
            dot(dv, n1[i], 0, 0).astype(bf16),
        ]

    def back_half(i):
        tail = dot(dk, w_att[i][2], 1, 0) + dot(dv, w_att[i][3], 1, 0)
        return tail[:halo], tail[halo:] + dot(dq, w_att[i][0], 1, 0)

    theirs = weights_half(1)
    theirs, dk = tie((theirs, dk))
    theirs = [swap(v, 0) for v in theirs]
    back = [back_half(0), back_half(1)]
    grad_halo = join(back[0][0], back[1][0]).astype(bf16)
    grad_halo, dv, theirs, z1 = tie((grad_halo, dv, theirs, z1))
    ff_sums = all_eight(jnp.stack([all_mp(z1, mine1), sum2]))
    near = move(grad_halo[near_rows:], [(i, i - 1) for i in range(1, mp)])
    passed = move(grad_halo[:near_rows], [(i, i - 2) for i in range(2, mp)])
    mine = weights_half(0)
    att_hi, att_lo = add_att(mine, theirs)
    att_got = hop(att_hi, 2)
    grad_norm1 = join(back[0][1], back[1][1])
    att_got, near, passed, grad_norm1 = tie((att_got, near, passed, grad_norm1))
    att_hop1 = hop(add(att_lo[1], att_got[1]), 1)
    att_keep = add(att_lo[0], att_got[0])
    grad_fc1 = ff_sums[:, 0].reshape(ff_here, wide).T.astype(f32)
    grad_fc2 = ff_sums[:, 1].reshape(ff_here, wide).astype(f32)
    near = jnp.pad(passed.astype(f32), ((rows - near_rows, 0), (0, 0))) + near.astype(f32)
    grad_norm1 = grad_norm1 + near
    xhat1, rstd1 = xhat_ext[halo:], rstd_ext[halo:]
    in_grad = grad_resid + norm_back(grad_norm1, norm1_gain, xhat1, rstd1)
    att_hop1, in_grad = tie((att_hop1, in_grad))
    att_keep = add(att_keep, att_hop1).reshape(4, mp, HD, half)
    att_z = [shift(att_keep[:, s], mp - s) for s in range(1, mp)]
    ff_bias = jnp.concatenate([jnp.sum(g.astype(f32), axis=0) for g in grad_pre])
    ff_bias = ff_bias.reshape(mp * 8, piece)
    qv_sums = jnp.concatenate(
        [jnp.sum(g.astype(f32), axis=0).reshape(mp * heads_here, HD) for g in (dq, dv[:, :])], 1
    )

    def in_order(table, at):
        n = table.shape[0]
        chosen = (at[None, :] == jnp.arange(n)[:, None]).astype(f32)
        return lax.dot(chosen, table, precision=lax.Precision.HIGHEST)

    small = jnp.stack(
        [
            jnp.sum(grad_resid, axis=0),
            jnp.sum(grad_norm1 * xhat1, axis=0),
            jnp.sum(grad_norm1, axis=0),
            jnp.sum(grad_norm2 * xhat2, axis=0),
            jnp.sum(grad_norm2, axis=0),
            jnp.sum(out_grad_wide, axis=0),
        ]
    )
    n_small = wide // mp
    vectors = jnp.concatenate(
        [
            jnp.transpose(small.reshape(6, mp, n_small), (1, 0, 2)).reshape(mp, -1),
            in_order(qv_sums, heads).reshape(mp, -1),
            in_order(ff_bias, ff_rows).reshape(mp, -1),
        ],
        1,
    )
    for bit in range(lax.axis_size("dp").bit_length() - 1):
        vectors = vectors + swap(vectors, bit)
    att_z, vectors, grad_fc1, grad_fc2 = tie((att_z, vectors, grad_fc1, grad_fc2))
    att_sum = att_keep[:, 0].astype(f32)
    for got in att_z:
        att_sum = att_sum + got.astype(f32)
    att_sum = beyond(att_sum).astype(bf16)
    att_sum = jnp.stack([att_sum, hop(att_sum, 2)])
    att_sum = jnp.stack([att_sum, hop(att_sum, 1)])
    att_sum = att_sum.reshape(4, 4, HD, half)
    att_sum = jnp.stack([att_sum, swap(att_sum, 0)]).reshape(8, 4, HD, half)
    from_slice = slice_at((row[:8] & 4) + ((row[:8] & 1) << 1) + ((row[:8] >> 1) & 1))
    at = jnp.sum(jnp.where(from_slice[None] == row[:8, None], row[None, :8], 0), axis=1)
    grad_out, grad_qkv = last_att(at, att_sum)
    grad_qkv = jnp.transpose(grad_qkv, (2, 0, 1))
    for bit in range(mp.bit_length() - 1):
        vectors = vectors + move(vectors, [(i, i ^ (1 << bit)) for i in range(mp)])
    total = lax.dynamic_index_in_dim(vectors, m, 0, False)
    six = total[: 6 * n_small].reshape(6, n_small)
    n_qv = heads_here * HD
    grad_qv = total[6 * n_small : 6 * n_small + 2 * n_qv].reshape(heads_here, 2, HD)
    grad_qv = jnp.transpose(grad_qv, (1, 0, 2)).reshape(2, n_qv)
    grad_fc1_bias = total[6 * n_small + 2 * n_qv :]
    return (
        result,
        in_grad,
        six[1],
        six[2],
        grad_qkv,
        grad_qv,
        grad_out,
        six[0],
        six[3],
        six[4],
        grad_fc1,
        grad_fc1_bias,
        grad_fc2,
        six[5],
    )


def solution(mesh):
    placed = (
        P(("dp", "mp"), None),
        P("dp", None),
        P(),
        P(),
        P(None, None, "mp"),
        P(None, "mp"),
        P("mp", None),
        P(),
        P(),
        P(),
        P(None, "mp"),
        P("mp"),
        P("mp", None),
        P(),
        P(("dp", "mp"), None),
    )
    return jax.shard_map(
        body,
        mesh=mesh,
        in_specs=placed,
        out_specs=(
            P(("dp", "mp"), None),
            P(("dp", "mp"), None),
            P("mp"),
            P("mp"),
            P(None, None, "mp"),
            P(None, "mp"),
            P("mp", None),
            P("mp"),
            P("mp"),
            P("mp"),
            P(None, "mp"),
            P("mp"),
            P("mp", None),
            P("mp"),
        ),
        check_vma=False,
    )
```

```python
import functools

import jax
import jax.numpy as jnp
from jax import lax
from jax.experimental import pallas as pl
from jax.experimental.pallas import tpu as pltpu
from jax.sharding import PartitionSpec as P

HEADS = 16
HD = 64
DOC_MOST = 768
QB = 256
MASKED = -1e12
SMALL = pl.CostEstimate(flops=1, bytes_accessed=1, transcendentals=1)
eps = 1e-05
f32 = jnp.float32
bf16 = jnp.bfloat16


def dot(a, b, ca, cb):
    return lax.dot_general(a, b, (((ca,), (cb,)), ((), ())), preferred_element_type=f32)


def fill_mask(segq_ref, segk_ref, mask_ref, window, halo):
    for i in range(mask_ref.shape[0]):
        key_at = lax.broadcasted_iota(jnp.int32, (window, QB), 0) + i * QB
        query_at = lax.broadcasted_iota(jnp.int32, (window, QB), 1) + (i * QB + halo)
        same = segk_ref[i * QB : i * QB + window, :] == segq_ref[:, i * QB : (i + 1) * QB]
        allowed = same & (key_at <= query_at)
        mask_ref[i] = jnp.where(allowed, (key_at - query_at).astype(f32), MASKED)


def halves(rows):
    lane = lax.broadcasted_iota(jnp.int32, (rows, 2 * HD), 1)
    return [lane < HD, lane >= HD]


def attend_kernel(halo, start, slopes, segq, segk, q_ref, k_ref, v_ref, *refs):
    o_ref, lse_ref, mask_ref = refs[-3:]
    window = halo + QB
    pair = start + pl.program_id(0)

    @pl.when(pair == start)
    def _():
        fill_mask(segq, segk, mask_ref, window, halo)

    v_t = v_ref[...].T
    pick = halves(QB)
    for i in range(mask_ref.shape[0]):
        rows = slice(i * QB, (i + 1) * QB)
        keys = slice(i * QB, i * QB + window)
        query = q_ref[rows, :] * jnp.asarray(HD**-0.5, bf16)
        key_rows = k_ref[keys, :]
        out = []
        for h in range(2):
            q_h = jnp.where(pick[h], query, jnp.zeros_like(query))
            scores = dot(key_rows, q_h, 1, 1) + slopes[2 * pair + h] * mask_ref[i]
            top = jnp.max(scores, axis=0, keepdims=True)
            expo = jnp.exp(scores - top)
            total = jnp.sum(expo, axis=0, keepdims=True)
            o_t = dot(v_t[:, keys], expo.astype(bf16), 1, 0)
            out.append(o_t[h * HD : (h + 1) * HD, :] * (1.0 / total))
            lse_ref[0, h : h + 1, rows] = top + jnp.log(total)
        o_ref[rows, :] = jnp.concatenate(out, axis=0).T.astype(bf16)


def attend_back_kernel(halo, start, slopes, segq, segk, q_ref, k_ref, v_ref, g_ref, lse_ref, *refs):
    dq_ref, dk_ref, dv_ref, mask_ref, dk_acc, dv_acc = refs[-6:]
    window = halo + QB
    pair = start + pl.program_id(0)

    @pl.when(pair == start)
    def _():
        fill_mask(segq, segk, mask_ref, window, halo)

    k_t = k_ref[...].T
    pick = halves(QB)
    dk_acc[...] = jnp.zeros_like(dk_acc)
    dv_acc[...] = jnp.zeros_like(dv_acc)
    for i in range(mask_ref.shape[0]):
        rows = slice(i * QB, (i + 1) * QB)
        keys = slice(i * QB, i * QB + window)
        query = q_ref[rows, :] * jnp.asarray(HD**-0.5, bf16)
        grad = g_ref[rows, :]
        key_rows = k_ref[keys, :]
        value_rows = v_ref[keys, :]
        out = []
        for h in range(2):
            q_h = jnp.where(pick[h], query, jnp.zeros_like(query))
            g_h = jnp.where(pick[h], grad, jnp.zeros_like(grad))
            scores = dot(key_rows, q_h, 1, 1) + slopes[2 * pair + h] * mask_ref[i]
            probs = jnp.exp(scores - lse_ref[0, h : h + 1, rows])
            grad_probs = dot(value_rows, g_h, 1, 1)
            delta = jnp.sum(probs * grad_probs, axis=0, keepdims=True)
            grad_scores = (probs * (grad_probs - delta)).astype(bf16)
            dv_acc[keys, :] += dot(probs.astype(bf16), g_h, 1, 0)
            dk_acc[keys, :] += dot(grad_scores, q_h, 1, 0)
            dq_t = dot(k_t[:, keys], grad_scores, 1, 0)
            out.append(dq_t[h * HD : (h + 1) * HD, :])
        dq_ref[rows, :] = (jnp.concatenate(out, axis=0).T * HD**-0.5).astype(bf16)
    dk_ref[...] = dk_acc[...].astype(bf16)
    dv_ref[...] = dv_acc[...].astype(bf16)


def attend(part, slopes, segq, segk, q, k, v, before=()):
    rows, wide = q.shape
    ext = k.shape[0]
    halo = ext - rows
    pairs = wide // (2 * HD)
    blocks = rows // QB
    start = part * (pairs // 2)
    col = lambda n: pl.BlockSpec((n, 2 * HD), lambda p: (0, p + start))
    return pl.pallas_call(
        functools.partial(attend_kernel, halo, start),
        grid=(pairs // 2,),
        in_specs=[
            pl.BlockSpec(memory_space=pltpu.SMEM),
            pl.BlockSpec((1, rows), lambda p: (0, 0)),
            pl.BlockSpec((ext, 1), lambda p: (0, 0)),
            col(rows),
            col(ext),
            col(ext),
        ]
        + [pl.BlockSpec(memory_space=pl.ANY)] * len(before),
        out_specs=[col(rows), pl.BlockSpec((1, 2, rows), lambda p: (p + start, 0, 0))],
        out_shape=[
            jax.ShapeDtypeStruct((rows, wide), bf16),
            jax.ShapeDtypeStruct((pairs, 2, rows), f32),
        ],
        input_output_aliases={6 + i: i for i in range(len(before))},
        scratch_shapes=[pltpu.VMEM((blocks, halo + QB, QB), f32)],
        compiler_params=pltpu.CompilerParams(vmem_limit_bytes=40 << 20),
        cost_estimate=SMALL,
    )(slopes, segq, segk, q, k, v, *before)


def attend_back(part, slopes, segq, segk, q, k, v, grad, lse, before=()):
    rows, wide = q.shape
    ext = k.shape[0]
    halo = ext - rows
    pairs = wide // (2 * HD)
    blocks = rows // QB
    start, stop = [pairs * i // 8 for i in (0, 3, 6, 8)][part : part + 2]
    col = lambda n: pl.BlockSpec((n, 2 * HD), lambda p: (0, p + start))
    return pl.pallas_call(
        functools.partial(attend_back_kernel, halo, start),
        grid=(stop - start,),
        in_specs=[
            pl.BlockSpec(memory_space=pltpu.SMEM),
            pl.BlockSpec((1, rows), lambda p: (0, 0)),
            pl.BlockSpec((ext, 1), lambda p: (0, 0)),
            col(rows),
            col(ext),
            col(ext),
            col(rows),
            pl.BlockSpec((1, 2, rows), lambda p: (p + start, 0, 0)),
        ]
        + [pl.BlockSpec(memory_space=pl.ANY)] * len(before),
        out_specs=[col(rows), col(ext), col(ext)],
        out_shape=[
            jax.ShapeDtypeStruct((rows, wide), bf16),
            jax.ShapeDtypeStruct((ext, wide), bf16),
            jax.ShapeDtypeStruct((ext, wide), bf16),
        ],
        input_output_aliases={8 + i: i for i in range(len(before))},
        scratch_shapes=[
            pltpu.VMEM((blocks, halo + QB, QB), f32),
            pltpu.VMEM((ext, 2 * HD), f32),
            pltpu.VMEM((ext, 2 * HD), f32),
        ],
        compiler_params=pltpu.CompilerParams(vmem_limit_bytes=48 << 20),
        cost_estimate=SMALL,
    )(slopes, segq, segk, q, k, v, grad, lse, *before)


def own_att_kernel(at, qkv_ref, out_ref, *own_refs):
    for t, rows in enumerate((qkv_ref[0], out_ref[...], qkv_ref[1], qkv_ref[2])):
        half = rows.shape[1] // 2
        left, right = rows[:, :half], rows[:, half:]
        own_refs[0][t, 0] = jnp.where(at[0] == 0, left, right)
        if len(own_refs) == 2:
            own_refs[1][t, 0] = jnp.where(at[0] == 0, right, left)


def own_att(halves, at, qkv_t, out_weight):
    wide = out_weight.shape[1]
    places = 4 if halves == 2 else 1
    return pl.pallas_call(
        own_att_kernel,
        grid_spec=pltpu.PrefetchScalarGridSpec(
            num_scalar_prefetch=1,
            grid=(places,),
            in_specs=[
                pl.BlockSpec((3, HD, wide), lambda p, at: (0, at[1 + p], 0)),
                pl.BlockSpec((HD, wide), lambda p, at: (at[1 + p], 0)),
            ],
            out_specs=[pl.BlockSpec((4, 1, HD, wide // 2), lambda p, at: (0, p, 0, 0))] * halves,
        ),
        cost_estimate=SMALL,
        out_shape=[jax.ShapeDtypeStruct((4, places, HD, wide // 2), bf16)] * halves,
    )(at, qkv_t, out_weight)


def me_ff_kernel(at, fc1_ref, fc2_ref, me1_ref, me2_ref):
    me1_ref[...] = fc1_ref[...].T
    me2_ref[...] = fc2_ref[...]


def me_ff(at, fc1_weight, fc2_weight):
    hidden, wide = fc2_weight.shape
    piece = hidden // 8
    return pl.pallas_call(
        me_ff_kernel,
        grid_spec=pltpu.PrefetchScalarGridSpec(
            num_scalar_prefetch=1,
            grid=(1,),
            in_specs=[
                pl.BlockSpec((wide, piece), lambda i, at: (0, at[0])),
                pl.BlockSpec((piece, wide), lambda i, at: (at[0], 0)),
            ],
            out_specs=[pl.BlockSpec((piece, wide), lambda i, at: (0, 0))] * 2,
        ),
        cost_estimate=SMALL,
        out_shape=[jax.ShapeDtypeStruct((piece, wide), bf16)] * 2,
    )(at, fc1_weight, fc2_weight)


def own_ff_kernel(at, fc1_ref, fc2_ref, o1_ref, o2_ref):
    o1_ref[...] = fc1_ref[...]
    o2_ref[...] = fc2_ref[...]


def own_ff(at, fc1_weight, fc2_weight):
    hidden, wide = fc2_weight.shape
    piece = hidden // 8
    return pl.pallas_call(
        own_ff_kernel,
        grid_spec=pltpu.PrefetchScalarGridSpec(
            num_scalar_prefetch=1,
            grid=(8,),
            in_specs=[
                pl.BlockSpec((wide, piece), lambda i, at: (0, at[i])),
                pl.BlockSpec((piece, wide), lambda i, at: (at[i], 0)),
            ],
            out_specs=[
                pl.BlockSpec((wide, piece), lambda i, at: (0, i)),
                pl.BlockSpec((piece, wide), lambda i, at: (i, 0)),
            ],
        ),
        cost_estimate=SMALL,
        out_shape=[
            jax.ShapeDtypeStruct((wide, hidden), bf16),
            jax.ShapeDtypeStruct((hidden, wide), bf16),
        ],
    )(at, fc1_weight, fc2_weight)


def join_att_kernel(core, *refs):
    mine, other, out_refs = refs[:4], refs[4:8], refs[8:]
    left_mine = core[0] == 0

    def places(t, own_ref, x0_ref, x1_ref, y_ref, exchanged):
        hops = (y_ref[0, :, t], x1_ref[:, t]) if exchanged else (x1_ref[:, t], y_ref[0, :, t])
        return own_ref[t], (x0_ref[:, t], *hops, y_ref[1, :, t])

    for t, out_ref in enumerate(out_refs):
        own_a, rest_a = places(t, *mine, False)
        own_b, rest_b = places(t, *other, True)
        half = own_a.shape[-1]
        out_ref[:, 0, :, :half] = jnp.where(left_mine, own_a, own_b)
        out_ref[:, 0, :, half:] = jnp.where(left_mine, own_b, own_a)
        for place, (a, b) in enumerate(zip(rest_a, rest_b)):
            out_ref[place, 1:, :, :half] = jnp.where(left_mine, a, b)
            out_ref[place, 1:, :, half:] = jnp.where(left_mine, b, a)


def join_att(core, mine, other):
    rest, _, hd, half = mine[1].shape
    step = hd // 4
    one = pl.BlockSpec((rest, 4, step, half), lambda i: (0, 0, i, 0))
    side = [
        pl.BlockSpec((4, 4, step, half), lambda i: (0, 0, i, 0)),
        one,
        one,
        pl.BlockSpec((2, rest, 4, step, half), lambda i: (0, 0, 0, i, 0)),
    ]
    return pl.pallas_call(
        join_att_kernel,
        grid=(4,),
        in_specs=[pl.BlockSpec(memory_space=pltpu.SMEM)] + side + side,
        out_specs=[pl.BlockSpec((4, rest + 1, step, 2 * half), lambda i: (0, 0, i, 0))] * 4,
        cost_estimate=SMALL,
        out_shape=[jax.ShapeDtypeStruct((4, rest + 1, hd, 2 * half), bf16)] * 4,
    )(core, *mine, *other)


def add_att_kernel(*refs):
    mine, theirs, (hi_ref, lo_ref) = refs[:4], refs[4:8], refs[8:]
    i = pl.program_id(0)
    for t in range(4):
        total = (mine[t][...].astype(f32) + theirs[t][...].astype(f32)).astype(bf16)

        @pl.when(i < 2)
        def _():
            hi_ref[0, t] = total

        @pl.when(i >= 2)
        def _():
            lo_ref[0, t] = total


def add_att(mine, theirs):
    rows, half = mine[0].shape
    ours = pl.BlockSpec((rows // 4, half), lambda i: ((i + 2) % 4, 0))
    got = pl.BlockSpec((rows // 4, half), lambda i: ((2 * i + 1) % 4 - i // 2, 0))
    shape = jax.ShapeDtypeStruct((2, 4, rows // 4, half), bf16)
    return pl.pallas_call(
        add_att_kernel,
        grid=(4,),
        in_specs=[ours] * 4 + [got] * 4,
        out_specs=[
            pl.BlockSpec((1, 4, rows // 4, half), lambda i: (jnp.minimum(i, 1), 0, 0, 0)),
            pl.BlockSpec((1, 4, rows // 4, half), lambda i: (jnp.maximum(i - 2, 0), 0, 0, 0)),
        ],
        cost_estimate=SMALL,
        out_shape=[shape, shape],
    )(*mine, *theirs)


def last_att_kernel(at, mine_ref, other_ref, out_ref, qkv_ref):
    mine, other = mine_ref[0].astype(f32), other_ref[0].astype(f32)
    half = mine.shape[-1]
    left, right = jnp.where(at[0] == 0, mine, other), jnp.where(at[0] == 0, other, mine)
    out_ref[:, :half] = left[1]
    out_ref[:, half:] = right[1]
    for i, t in enumerate((0, 2, 3)):
        qkv_ref[i, :, :half] = left[t]
        qkv_ref[i, :, half:] = right[t]


def last_att(at, pieces, others):
    _, _, hd, half = pieces.shape
    block = lambda c: pl.BlockSpec((1, 4, hd, half), lambda p, at: (at[1 + 4 * c + p], 0, 0, 0))
    return pl.pallas_call(
        last_att_kernel,
        grid_spec=pltpu.PrefetchScalarGridSpec(
            num_scalar_prefetch=1,
            grid=(4,),
            in_specs=[block(0), block(1)],
            out_specs=[
                pl.BlockSpec((hd, 2 * half), lambda p, at: (p, 0)),
                pl.BlockSpec((3, hd, 2 * half), lambda p, at: (0, p, 0)),
            ],
        ),
        cost_estimate=SMALL,
        out_shape=[
            jax.ShapeDtypeStruct((4 * hd, 2 * half), f32),
            jax.ShapeDtypeStruct((3, 4 * hd, 2 * half), f32),
        ],
    )(at, pieces, others)


def swap(value, b):
    n = lax.axis_size("dp")
    return lax.ppermute(value, "dp", [(i, i ^ (1 << b)) for i in range(n)])


def hop(value, stage):
    n = lax.axis_size("dp")
    return lax.ppermute(
        value, "dp", [(i, i ^ (2 if (i & 1) == stage - 1 else 4)) for i in range(n)]
    )


def move(value, pairs):
    return lax.ppermute(value, "mp", pairs)


def shift(value, s):
    n = lax.axis_size("mp")
    return move(value, [(i, (i + s) % n) for i in range(n)])


def all_eight(value):
    n = lax.axis_size("dp")
    groups = None if n == 8 else [list(range(g, g + 8)) for g in range(0, n, 8)]
    return lax.all_gather(value, "dp", axis=0, axis_index_groups=groups)


def beyond(value):
    for b in range(3, lax.axis_size("dp").bit_length() - 1):
        value = value + swap(value, b)
    return value


def add(a, b):
    return (a.astype(f32) + b.astype(f32)).astype(bf16)


tie = lax.optimization_barrier


def norm_parts(rows):
    mean = jnp.mean(rows, axis=-1, keepdims=True)
    centred = rows - mean
    rstd = lax.rsqrt(jnp.mean(centred * centred, axis=-1, keepdims=True) + eps)
    return centred * rstd, rstd


def norm_back(grad, gain, xhat, rstd):
    scaled = grad * gain
    return rstd * (
        scaled
        - jnp.mean(scaled, axis=-1, keepdims=True)
        - xhat * jnp.mean(scaled * xhat, axis=-1, keepdims=True)
    )


def gelu_both(v):
    c, k = 0.7978845608028654, 0.044715
    t = jnp.tanh(c * (v + k * v * v * v))
    value = 0.5 * v * (1.0 + t)
    slope = 0.5 * (1.0 + t) + 0.5 * v * (1.0 - t * t) * (c * (1.0 + 3.0 * k * v * v))
    return value, slope


def body(
    tokens,
    segment_ids,
    norm1_gain,
    norm1_shift,
    qkv_weight,
    qv_bias,
    out_weight,
    out_bias,
    norm2_gain,
    norm2_shift,
    fc1_weight,
    fc1_bias,
    fc2_weight,
    fc2_bias,
    out_grad,
):
    rows, wide = tokens.shape
    half = wide // 2
    mp = lax.axis_size("mp")
    m = lax.axis_index("mp")
    d = lax.axis_index("dp") & 7
    core = d & 1
    ff_here = fc1_weight.shape[1]
    piece = ff_here // 8
    heads_here = qkv_weight.shape[2] // HD
    rest = mp - 1

    def slice_at(k):
        first = jnp.where((core ^ (k >> 2)) == 0, 2, 4)
        return d ^ ((k >> 2) + (k & 1) * first + ((k >> 1) & 1) * (6 - first))

    slices = slice_at(jnp.arange(8))
    place = slice_at(jnp.arange(4)) >> 1
    row = jnp.arange(mp * 8)
    other = jnp.maximum(row - 8, 0)
    shifts = jnp.where(row < 8, 0, other % rest + 1)
    lies_at = slice_at(jnp.where(row < 8, row, other // rest))
    ff_rows = (m + shifts) % mp * 8 + lies_at
    ff_from = (mp - shifts) % mp * 8 + lies_at
    head = jnp.arange(mp * heads_here)
    head_place = slice_at(head // mp) >> 1
    heads = (m + mp - head % mp) % mp * heads_here + head_place
    heads_from = head % mp * heads_here + head_place
    slopes = jnp.exp2(-8.0 * (heads + 1).astype(f32) / HEADS)

    def pick(table, at):
        n = table.shape[0]
        chosen = (at[:, None] == jnp.arange(n)[None, :]).astype(f32)
        return lax.dot(chosen, table, precision=lax.Precision.HIGHEST)

    near_rows = DOC_MOST - rows
    halo = DOC_MOST
    qv_own = jnp.transpose(qv_bias.reshape(2, heads_here, HD), (1, 0, 2))
    bias_own = jnp.concatenate([fc1_bias.reshape(8, piece), qv_own.reshape(heads_here, 2 * HD)])
    qkv_t = jnp.transpose(qkv_weight, (1, 2, 0))
    att_places = jnp.concatenate([core[None], place])
    (att_me,) = own_att(1, att_places, qkv_t, out_weight)
    att_me = att_me.reshape(4, HD, half)
    att_z = [shift(att_me, s) for s in range(1, mp)]
    bias_own, _ = tie((bias_own, att_me))
    bias_all = [bias_own] + [shift(bias_own, s) for s in range(1, mp)]
    me1, me2 = me_ff(slices, fc1_weight, fc2_weight)
    up = [(i, i + 1) for i in range(mp - 1)]
    tokens_late, _ = tie((tokens, att_me))
    halo1 = move(tokens_late[rows - near_rows :], up)
    fc1_b = pick(jnp.concatenate([v[:8] for v in bias_all]), ff_from).reshape(-1)
    qv_b = pick(jnp.concatenate([v[8:] for v in bias_all]), heads_from)
    q_bias, v_bias = qv_b[:, :HD].reshape(-1), qv_b[:, HD:].reshape(-1)
    seg_row = jnp.concatenate([jnp.full((1, halo), -1, jnp.int32), segment_ids], 1)
    segk = lax.dynamic_slice_in_dim(seg_row, m * rows, halo + rows, 1)
    segq = segk[:, halo:]
    segk = segk.reshape(halo + rows, 1)

    fc1_b, slices, att_places = tie((fc1_b, slices, att_places))
    own = own_att(2, att_places, qkv_t, out_weight)
    own1, own2 = own_ff(slices, fc1_weight, fc2_weight)
    small_ones = (fc1_b, q_bias, v_bias, segk, segq, slopes, own, own1, own2)
    att_z, small_ones = tie((att_z, small_ones))
    fc1_b, q_bias, v_bias, segk, segq, slopes, own, own1, own2 = small_ones
    att_x0 = jnp.stack(att_z)
    att_x1 = hop(att_x0, 1)
    att_x1, halo1 = tie((att_x1, halo1))
    halo2 = move(halo1, up)
    halo3 = move(tokens_late[: rows - near_rows], up)
    part0 = swap(att_x0, 0)
    att_y = hop(jnp.stack([att_x0, att_x1]), 2)
    part1 = swap(att_x1, 0)
    att_y, part0, part1, halo2, halo3, me1, me2 = tie(
        (att_y, part0, part1, halo2, halo3, me1, me2)
    )
    z1 = [shift(me1, mp - s) for s in range(1, mp)]
    ext = jnp.concatenate([halo2, halo3, halo1, tokens], 0).astype(f32)
    xhat_ext, rstd_ext = norm_parts(ext)
    norm1 = (xhat_ext * norm1_gain + norm1_shift).astype(bf16)
    col = [core * half, (1 - core) * half]

    def cols(value):
        return [lax.dynamic_slice_in_dim(value, at, half, 1) for at in col]

    n1 = cols(norm1)
    part_y = swap(att_y, 0)
    weights = join_att(
        core[None], (own[0], att_x0, att_x1, att_y), (own[1], part0, part1, part_y)
    )
    w_q, w_o, w_k, w_v = [w.reshape(HEADS * HD, wide) for w in weights]

    q = (dot(norm1[halo:], w_q, 1, 1) + q_bias).astype(bf16)
    k = dot(norm1, w_k, 1, 1).astype(bf16)
    v = (dot(norm1, w_v, 1, 1) + v_bias).astype(bf16)

    cut = rest * piece

    q, z1, me2 = tie((q, z1, me2))
    x0_1 = jnp.concatenate(z1)
    z2 = [shift(me2, mp - s) for s in range(1, mp)]
    x1_1 = hop(x0_1, 1)
    first = attend(0, slopes, segq, segk, q, k, v)
    first, x1_1, z2 = tie((first, x1_1, z2))
    x0_2 = jnp.concatenate(z2)
    z1 = jnp.concatenate([x0_1, x1_1])
    y1 = hop(z1, 2)
    x1_2 = hop(x0_2, 1)
    context, lse = attend(1, slopes, segq, segk, q, k, v, first)
    context, y1, x1_2 = tie((context, y1, x1_2))
    z2 = jnp.concatenate([x0_2, x1_2])
    y2 = hop(z2, 2)
    w1 = [z1, y1, swap(z1, 0), swap(y1, 0)]
    w2 = [z2, y2, swap(z2, 0), swap(y2, 0)]
    attention = dot(context, w_o, 1, 0)
    tokens_wide = tokens.astype(f32)
    resid = attention + out_bias + tokens_wide
    xhat2, rstd2 = norm_parts(resid)
    norm2 = (xhat2 * norm2_gain + norm2_shift).astype(bf16)

    pre, at = [dot(norm2, own1, 1, 0) + fc1_b[:ff_here]], ff_here
    for w in w1:
        pre.append(dot(norm2, w, 1, 1) + fc1_b[at : at + w.shape[0]])
        at += w.shape[0]
    hidden = [gelu_both(p)[0].astype(bf16) for p in pre]

    def partials(lhs, rhs):
        send = [lhs[3], lhs[4], lhs[0][:, 4 * piece :]]
        return [dot(v, rhs, 0, 0).astype(bf16) for v in send]

    def after_core(lhs, rhs, got):
        hi = jnp.concatenate(
            [
                (dot(lhs[2], rhs, 0, 0) + got[1].astype(f32)).astype(bf16),
                (dot(lhs[0][:, 2 * piece : 4 * piece], rhs, 0, 0) + got[2][2 * piece :].astype(f32)).astype(bf16),
            ]
        )
        lo = [
            (dot(lhs[1], rhs, 0, 0) + got[0].astype(f32)).astype(bf16),
            (dot(lhs[0][:, : 2 * piece], rhs, 0, 0) + got[2][: 2 * piece].astype(f32)).astype(bf16),
        ]
        return hi, lo

    def after_hop2(lo, got):
        send = jnp.concatenate([add(lo[0][cut:], got[cut : 2 * cut]), add(lo[1][piece:], got[2 * cut + piece :])])
        keep = [add(lo[0][:cut], got[:cut]), add(lo[1][:piece], got[2 * cut : 2 * cut + piece])]
        return send, keep

    def along_mp(keep, got):
        mine = add(keep[1], got[cut:])
        others = add(keep[0], got[:cut])
        blocks = jnp.concatenate([mine, others, mine, others])
        blocks = lax.dynamic_slice_in_dim(blocks, (mp - m) * piece, mp * piece, 0)
        return lax.psum_scatter(blocks, "mp", scatter_dimension=0, tiled=True)

    send2 = partials(hidden, out_grad)
    got2 = [swap(v, 0) for v in send2]
    mlp = sum(dot(h, w, 1, 0) for h, w in zip(hidden, [own2] + w2))
    result = (mlp + fc2_bias + resid).astype(bf16)
    grad_pre = [
        (dot(out_grad, w, 1, 1) * gelu_both(p)[1]).astype(bf16) for w, p in zip([own2] + w2, pre)
    ]
    send1 = partials(grad_pre, norm2)
    got1 = [swap(v, 0) for v in send1]
    hi2, lo2 = after_core(hidden, out_grad, got2)
    hop2_2 = hop(hi2, 2)

    grad_norm2 = dot(grad_pre[0], own1, 1, 1)
    grad_norm2 = grad_norm2 + sum(dot(g, w, 1, 0) for g, w in zip(grad_pre[1:], w1))
    out_grad_wide = out_grad.astype(f32)
    grad_resid = out_grad_wide + norm_back(grad_norm2, norm2_gain, xhat2, rstd2)
    hi1, lo1 = after_core(grad_pre, norm2, got1)
    grad_attention = grad_resid.astype(bf16)
    grad_att = cols(grad_attention)
    grad_context = dot(grad_attention, w_o, 1, 1).astype(bf16)

    grad_context, hi1, hi2 = tie((grad_context, hi1, hi2))
    hop2_1 = hop(hi1, 2)
    first = attend_back(0, slopes, segq, segk, q, k, v, grad_context, lse)
    first, hop2_2, result = tie((first, hop2_2, result))
    send2, keep2 = after_hop2(lo2, hop2_2)
    hop1_2 = hop(send2, 1)
    second = attend_back(1, slopes, segq, segk, q, k, v, grad_context, lse, first)
    second, hop2_1, hop1_2 = tie((second, hop2_1, hop1_2))
    send1, keep1 = after_hop2(lo1, hop2_1)
    hop1_1 = hop(send1, 1)
    sum2 = all_eight(beyond(along_mp(keep2, hop1_2)))
    grads = attend_back(2, slopes, segq, segk, q, k, v, grad_context, lse, second)
    (dq, dk, dv), hop1_1 = tie((grads, hop1_1))
    sum1 = along_mp(keep1, hop1_1)

    def weights_half(i):
        return [
            dot(dq, n1[i][halo:], 0, 0).astype(bf16),
            dot(context, grad_att[i], 0, 0).astype(bf16),
            dot(dk, n1[i], 0, 0).astype(bf16),
            dot(dv, n1[i], 0, 0).astype(bf16),
        ]

    grad_ext = dot(dk, w_k, 1, 0) + dot(dv, w_v, 1, 0)
    grad_halo = grad_ext[:halo].astype(bf16)
    grad_halo, dk, dv, dq = tie((grad_halo, dk, dv, dq))
    passed = move(grad_halo[:near_rows], [(i, i - 2) for i in range(2, mp)])
    theirs = weights_half(1)
    theirs, dk, dv, dq = tie((theirs, dk, dv, dq))
    theirs = [swap(v, 0) for v in theirs]
    mine = weights_half(0)
    att_hi, att_lo = add_att(mine, theirs)
    att_hi, passed, grad_halo, grad_ext, dq_late = tie((att_hi, passed, grad_halo, grad_ext, dq))
    att_got = hop(att_hi, 2)
    near = move(grad_halo[near_rows:], [(i, i - 1) for i in range(1, mp)])
    grad_norm1 = grad_ext[halo:] + dot(dq_late, w_q, 1, 0)
    att_got, grad_norm1, sum1 = tie((att_got, grad_norm1, sum1))
    sum1 = all_eight(beyond(sum1))
    att_hop1 = hop(add(att_lo[1], att_got[1]), 1)
    att_keep = add(att_lo[0], att_got[0])
    near = jnp.pad(passed.astype(f32), ((rows - near_rows, 0), (0, 0))) + near.astype(f32)
    grad_norm1 = grad_norm1 + near
    xhat1, rstd1 = xhat_ext[halo:], rstd_ext[halo:]
    in_grad = grad_resid + norm_back(grad_norm1, norm1_gain, xhat1, rstd1)
    att_keep = add(att_keep, att_hop1).reshape(4, mp, HD, half)
    att_z = [shift(att_keep[:, s], mp - s) for s in range(1, mp)]
    ff_bias = jnp.concatenate([jnp.sum(g.astype(f32), axis=0) for g in grad_pre])
    ff_bias = ff_bias.reshape(mp * 8, piece)
    qv_sums = jnp.concatenate(
        [jnp.sum(g.astype(f32), axis=0).reshape(mp * heads_here, HD) for g in (dq, dv[:, :])], 1
    )

    def in_order(table, at):
        n = table.shape[0]
        chosen = (at[None, :] == jnp.arange(n)[:, None]).astype(f32)
        return lax.dot(chosen, table, precision=lax.Precision.HIGHEST)

    small = jnp.stack(
        [
            jnp.sum(grad_resid, axis=0),
            jnp.sum(grad_norm1 * xhat1, axis=0),
            jnp.sum(grad_norm1, axis=0),
            jnp.sum(grad_norm2 * xhat2, axis=0),
            jnp.sum(grad_norm2, axis=0),
            jnp.sum(out_grad_wide, axis=0),
        ]
    )
    n_small = wide // mp
    vectors = jnp.concatenate(
        [
            jnp.transpose(small.reshape(6, mp, n_small), (1, 0, 2)).reshape(mp, -1),
            in_order(qv_sums, heads).reshape(mp, -1),
            in_order(ff_bias, ff_rows).reshape(mp, -1),
        ],
        1,
    )
    grad_fc1 = sum1.reshape(ff_here, wide).T.astype(f32)
    grad_fc2 = sum2.reshape(ff_here, wide).astype(f32)

    att_z, vectors, grad_fc2, in_grad = tie((att_z, vectors, grad_fc2, in_grad))
    for bit in range(lax.axis_size("dp").bit_length() - 1):
        vectors = vectors + swap(vectors, bit)
    att_sum = att_keep[:, 0].astype(f32)
    for got in att_z:
        att_sum = att_sum + got.astype(f32)
    att_sum = beyond(att_sum).astype(bf16)
    att_sum = jnp.stack([att_sum, hop(att_sum, 2)])
    att_sum, grad_fc1 = tie((jnp.stack([att_sum, hop(att_sum, 1)]), grad_fc1))
    att_sum = att_sum.reshape(4, 4, HD, half)
    number = row[:4]
    order = jnp.stack([number * 0, number * 0 + 1])
    lies = (slice_at(4 * order + ((number & 1) << 1) + (number >> 1))) >> 1
    at = jnp.sum(jnp.where(lies[:, None] == number[:, None], number[None, None], 0), axis=2)
    at = jnp.concatenate([core[None], at.reshape(-1)])
    grad_out, grad_qkv = last_att(at, att_sum, swap(att_sum, 0))
    grad_qkv = jnp.transpose(grad_qkv, (2, 0, 1))
    for bit in range(mp.bit_length() - 1):
        vectors = vectors + move(vectors, [(i, i ^ (1 << bit)) for i in range(mp)])
    total = lax.dynamic_index_in_dim(vectors, m, 0, False)
    six = total[: 6 * n_small].reshape(6, n_small)
    n_qv = heads_here * HD
    grad_qv = total[6 * n_small : 6 * n_small + 2 * n_qv].reshape(heads_here, 2, HD)
    grad_qv = jnp.transpose(grad_qv, (1, 0, 2)).reshape(2, n_qv)
    grad_fc1_bias = total[6 * n_small + 2 * n_qv :]
    return (
        result,
        in_grad,
        six[1],
        six[2],
        grad_qkv,
        grad_qv,
        grad_out,
        six[0],
        six[3],
        six[4],
        grad_fc1,
        grad_fc1_bias,
        grad_fc2,
        six[5],
    )


def solution(mesh):
    placed = (
        P(("dp", "mp"), None),
        P("dp", None),
        P(),
        P(),
        P(None, None, "mp"),
        P(None, "mp"),
        P("mp", None),
        P(),
        P(),
        P(),
        P(None, "mp"),
        P("mp"),
        P("mp", None),
        P(),
        P(("dp", "mp"), None),
    )
    return jax.shard_map(
        body,
        mesh=mesh,
        in_specs=placed,
        out_specs=(
            P(("dp", "mp"), None),
            P(("dp", "mp"), None),
            P("mp"),
            P("mp"),
            P(None, None, "mp"),
            P(None, "mp"),
            P("mp", None),
            P("mp"),
            P("mp"),
            P("mp"),
            P(None, "mp"),
            P("mp"),
            P("mp", None),
            P("mp"),
        ),
        check_vma=False,
    )
```

```python
import functools

import jax
import jax.numpy as jnp
from jax import lax
from jax.experimental import pallas as pl
from jax.experimental.pallas import tpu as pltpu
from jax.sharding import PartitionSpec as P

HEADS = 16
HD = 64
DOC_MOST = 768
QB = 256
MASKED = -1e12
SMALL = pl.CostEstimate(flops=1, bytes_accessed=1, transcendentals=1)
eps = 1e-05
f32 = jnp.float32
bf16 = jnp.bfloat16


def dot(a, b, ca, cb):
    return lax.dot_general(a, b, (((ca,), (cb,)), ((), ())), preferred_element_type=f32)


def fill_mask(segq_ref, segk_ref, mask_ref, window, halo):
    for i in range(mask_ref.shape[0]):
        key_at = lax.broadcasted_iota(jnp.int32, (window, QB), 0) + i * QB
        query_at = lax.broadcasted_iota(jnp.int32, (window, QB), 1) + (i * QB + halo)
        same = segk_ref[i * QB : i * QB + window, :] == segq_ref[:, i * QB : (i + 1) * QB]
        allowed = same & (key_at <= query_at)
        mask_ref[i] = jnp.where(allowed, (key_at - query_at).astype(f32), MASKED)


def halves(rows):
    lane = lax.broadcasted_iota(jnp.int32, (rows, 2 * HD), 1)
    return [lane < HD, lane >= HD]


def attend_kernel(halo, start, slopes, segq, segk, q_ref, k_ref, v_ref, *refs):
    o_ref, lse_ref, mask_ref = refs[-3:]
    window = halo + QB
    pair = start + pl.program_id(0)

    @pl.when(pair == start)
    def _():
        fill_mask(segq, segk, mask_ref, window, halo)

    v_t = v_ref[...].T
    pick = halves(QB)
    for i in range(mask_ref.shape[0]):
        rows = slice(i * QB, (i + 1) * QB)
        keys = slice(i * QB, i * QB + window)
        query = q_ref[rows, :] * jnp.asarray(HD**-0.5, bf16)
        key_rows = k_ref[keys, :]
        out = []
        for h in range(2):
            q_h = jnp.where(pick[h], query, jnp.zeros_like(query))
            scores = dot(key_rows, q_h, 1, 1) + slopes[2 * pair + h] * mask_ref[i]
            top = jnp.max(scores, axis=0, keepdims=True)
            expo = jnp.exp(scores - top)
            total = jnp.sum(expo, axis=0, keepdims=True)
            o_t = dot(v_t[:, keys], expo.astype(bf16), 1, 0)
            out.append(o_t[h * HD : (h + 1) * HD, :] * (1.0 / total))
            lse_ref[0, h : h + 1, rows] = top + jnp.log(total)
        o_ref[rows, :] = jnp.concatenate(out, axis=0).T.astype(bf16)


def attend_back_kernel(halo, start, slopes, segq, segk, q_ref, k_ref, v_ref, g_ref, lse_ref, *refs):
    dq_ref, dk_ref, dv_ref, mask_ref, dk_acc, dv_acc = refs[-6:]
    window = halo + QB
    pair = start + pl.program_id(0)

    @pl.when(pair == start)
    def _():
        fill_mask(segq, segk, mask_ref, window, halo)

    k_t = k_ref[...].T
    pick = halves(QB)
    dk_acc[...] = jnp.zeros_like(dk_acc)
    dv_acc[...] = jnp.zeros_like(dv_acc)
    for i in range(mask_ref.shape[0]):
        rows = slice(i * QB, (i + 1) * QB)
        keys = slice(i * QB, i * QB + window)
        query = q_ref[rows, :] * jnp.asarray(HD**-0.5, bf16)
        grad = g_ref[rows, :]
        key_rows = k_ref[keys, :]
        value_rows = v_ref[keys, :]
        out = []
        for h in range(2):
            q_h = jnp.where(pick[h], query, jnp.zeros_like(query))
            g_h = jnp.where(pick[h], grad, jnp.zeros_like(grad))
            scores = dot(key_rows, q_h, 1, 1) + slopes[2 * pair + h] * mask_ref[i]
            probs = jnp.exp(scores - lse_ref[0, h : h + 1, rows])
            grad_probs = dot(value_rows, g_h, 1, 1)
            delta = jnp.sum(probs * grad_probs, axis=0, keepdims=True)
            grad_scores = (probs * (grad_probs - delta)).astype(bf16)
            dv_acc[keys, :] += dot(probs.astype(bf16), g_h, 1, 0)
            dk_acc[keys, :] += dot(grad_scores, q_h, 1, 0)
            dq_t = dot(k_t[:, keys], grad_scores, 1, 0)
            out.append(dq_t[h * HD : (h + 1) * HD, :])
        dq_ref[rows, :] = (jnp.concatenate(out, axis=0).T * HD**-0.5).astype(bf16)
    dk_ref[...] = dk_acc[...].astype(bf16)
    dv_ref[...] = dv_acc[...].astype(bf16)


def attend(part, slopes, segq, segk, q, k, v, before=()):
    rows, wide = q.shape
    ext = k.shape[0]
    halo = ext - rows
    pairs = wide // (2 * HD)
    blocks = rows // QB
    start = part * (pairs // 2)
    col = lambda n: pl.BlockSpec((n, 2 * HD), lambda p: (0, p + start))
    return pl.pallas_call(
        functools.partial(attend_kernel, halo, start),
        grid=(pairs // 2,),
        in_specs=[
            pl.BlockSpec(memory_space=pltpu.SMEM),
            pl.BlockSpec((1, rows), lambda p: (0, 0)),
            pl.BlockSpec((ext, 1), lambda p: (0, 0)),
            col(rows),
            col(ext),
            col(ext),
        ]
        + [pl.BlockSpec(memory_space=pl.ANY)] * len(before),
        out_specs=[col(rows), pl.BlockSpec((1, 2, rows), lambda p: (p + start, 0, 0))],
        out_shape=[
            jax.ShapeDtypeStruct((rows, wide), bf16),
            jax.ShapeDtypeStruct((pairs, 2, rows), f32),
        ],
        input_output_aliases={6 + i: i for i in range(len(before))},
        scratch_shapes=[pltpu.VMEM((blocks, halo + QB, QB), f32)],
        compiler_params=pltpu.CompilerParams(vmem_limit_bytes=40 << 20),
        cost_estimate=SMALL,
    )(slopes, segq, segk, q, k, v, *before)


def attend_back(part, slopes, segq, segk, q, k, v, grad, lse, before=()):
    rows, wide = q.shape
    ext = k.shape[0]
    halo = ext - rows
    pairs = wide // (2 * HD)
    blocks = rows // QB
    start, stop = [pairs * i // 8 for i in (0, 3, 6, 8)][part : part + 2]
    col = lambda n: pl.BlockSpec((n, 2 * HD), lambda p: (0, p + start))
    return pl.pallas_call(
        functools.partial(attend_back_kernel, halo, start),
        grid=(stop - start,),
        in_specs=[
            pl.BlockSpec(memory_space=pltpu.SMEM),
            pl.BlockSpec((1, rows), lambda p: (0, 0)),
            pl.BlockSpec((ext, 1), lambda p: (0, 0)),
            col(rows),
            col(ext),
            col(ext),
            col(rows),
            pl.BlockSpec((1, 2, rows), lambda p: (p + start, 0, 0)),
        ]
        + [pl.BlockSpec(memory_space=pl.ANY)] * len(before),
        out_specs=[col(rows), col(ext), col(ext)],
        out_shape=[
            jax.ShapeDtypeStruct((rows, wide), bf16),
            jax.ShapeDtypeStruct((ext, wide), bf16),
            jax.ShapeDtypeStruct((ext, wide), bf16),
        ],
        input_output_aliases={8 + i: i for i in range(len(before))},
        scratch_shapes=[
            pltpu.VMEM((blocks, halo + QB, QB), f32),
            pltpu.VMEM((ext, 2 * HD), f32),
            pltpu.VMEM((ext, 2 * HD), f32),
        ],
        compiler_params=pltpu.CompilerParams(vmem_limit_bytes=48 << 20),
        cost_estimate=SMALL,
    )(slopes, segq, segk, q, k, v, grad, lse, *before)


def own_att_kernel(at, qkv_ref, out_ref, *own_refs):
    for t, rows in enumerate((qkv_ref[0], out_ref[...], qkv_ref[1], qkv_ref[2])):
        half = rows.shape[1] // 2
        left, right = rows[:, :half], rows[:, half:]
        own_refs[0][t, 0] = jnp.where(at[0] == 0, left, right)
        if len(own_refs) == 2:
            own_refs[1][t, 0] = jnp.where(at[0] == 0, right, left)


def own_att(halves, at, qkv_t, out_weight):
    wide = out_weight.shape[1]
    places = 4 if halves == 2 else 1
    return pl.pallas_call(
        own_att_kernel,
        grid_spec=pltpu.PrefetchScalarGridSpec(
            num_scalar_prefetch=1,
            grid=(places,),
            in_specs=[
                pl.BlockSpec((3, HD, wide), lambda p, at: (0, at[1 + p], 0)),
                pl.BlockSpec((HD, wide), lambda p, at: (at[1 + p], 0)),
            ],
            out_specs=[pl.BlockSpec((4, 1, HD, wide // 2), lambda p, at: (0, p, 0, 0))] * halves,
        ),
        cost_estimate=SMALL,
        out_shape=[jax.ShapeDtypeStruct((4, places, HD, wide // 2), bf16)] * halves,
    )(at, qkv_t, out_weight)


def me_ff_kernel(at, fc1_ref, fc2_ref, me1_ref, me2_ref):
    me1_ref[...] = fc1_ref[...].T
    me2_ref[...] = fc2_ref[...]


def me_ff(at, fc1_weight, fc2_weight):
    hidden, wide = fc2_weight.shape
    piece = hidden // 8
    return pl.pallas_call(
        me_ff_kernel,
        grid_spec=pltpu.PrefetchScalarGridSpec(
            num_scalar_prefetch=1,
            grid=(1,),
            in_specs=[
                pl.BlockSpec((wide, piece), lambda i, at: (0, at[0])),
                pl.BlockSpec((piece, wide), lambda i, at: (at[0], 0)),
            ],
            out_specs=[pl.BlockSpec((piece, wide), lambda i, at: (0, 0))] * 2,
        ),
        cost_estimate=SMALL,
        out_shape=[jax.ShapeDtypeStruct((piece, wide), bf16)] * 2,
    )(at, fc1_weight, fc2_weight)


def own_ff_kernel(at, fc1_ref, fc2_ref, o1_ref, o2_ref):
    o1_ref[...] = fc1_ref[...]
    o2_ref[...] = fc2_ref[...]


def own_ff(at, fc1_weight, fc2_weight):
    hidden, wide = fc2_weight.shape
    piece = hidden // 8
    return pl.pallas_call(
        own_ff_kernel,
        grid_spec=pltpu.PrefetchScalarGridSpec(
            num_scalar_prefetch=1,
            grid=(8,),
            in_specs=[
                pl.BlockSpec((wide, piece), lambda i, at: (0, at[i])),
                pl.BlockSpec((piece, wide), lambda i, at: (at[i], 0)),
            ],
            out_specs=[
                pl.BlockSpec((wide, piece), lambda i, at: (0, i)),
                pl.BlockSpec((piece, wide), lambda i, at: (i, 0)),
            ],
        ),
        cost_estimate=SMALL,
        out_shape=[
            jax.ShapeDtypeStruct((wide, hidden), bf16),
            jax.ShapeDtypeStruct((hidden, wide), bf16),
        ],
    )(at, fc1_weight, fc2_weight)


def join_att_kernel(core, *refs):
    mine, other, out_refs = refs[:4], refs[4:8], refs[8:]
    left_mine = core[0] == 0

    def places(t, own_ref, x0_ref, x1_ref, y_ref, exchanged):
        hops = (y_ref[0, :, t], x1_ref[:, t]) if exchanged else (x1_ref[:, t], y_ref[0, :, t])
        return own_ref[t], (x0_ref[:, t], *hops, y_ref[1, :, t])

    for t, out_ref in enumerate(out_refs):
        own_a, rest_a = places(t, *mine, False)
        own_b, rest_b = places(t, *other, True)
        half = own_a.shape[-1]
        out_ref[:, 0, :, :half] = jnp.where(left_mine, own_a, own_b)
        out_ref[:, 0, :, half:] = jnp.where(left_mine, own_b, own_a)
        for place, (a, b) in enumerate(zip(rest_a, rest_b)):
            out_ref[place, 1:, :, :half] = jnp.where(left_mine, a, b)
            out_ref[place, 1:, :, half:] = jnp.where(left_mine, b, a)


def join_att(core, mine, other):
    rest, _, hd, half = mine[1].shape
    step = hd // 4
    one = pl.BlockSpec((rest, 4, step, half), lambda i: (0, 0, i, 0))
    side = [
        pl.BlockSpec((4, 4, step, half), lambda i: (0, 0, i, 0)),
        one,
        one,
        pl.BlockSpec((2, rest, 4, step, half), lambda i: (0, 0, 0, i, 0)),
    ]
    return pl.pallas_call(
        join_att_kernel,
        grid=(4,),
        in_specs=[pl.BlockSpec(memory_space=pltpu.SMEM)] + side + side,
        out_specs=[pl.BlockSpec((4, rest + 1, step, 2 * half), lambda i: (0, 0, i, 0))] * 4,
        cost_estimate=SMALL,
        out_shape=[jax.ShapeDtypeStruct((4, rest + 1, hd, 2 * half), bf16)] * 4,
    )(core, *mine, *other)


def add_att_kernel(*refs):
    mine, theirs, (hi_ref, lo_ref) = refs[:4], refs[4:8], refs[8:]
    i = pl.program_id(0)
    for t in range(4):
        total = (mine[t][...].astype(f32) + theirs[t][...].astype(f32)).astype(bf16)

        @pl.when(i < 2)
        def _():
            hi_ref[0, t] = total

        @pl.when(i >= 2)
        def _():
            lo_ref[0, t] = total


def add_att(mine, theirs):
    rows, half = mine[0].shape
    ours = pl.BlockSpec((rows // 4, half), lambda i: ((i + 2) % 4, 0))
    got = pl.BlockSpec((rows // 4, half), lambda i: ((2 * i + 1) % 4 - i // 2, 0))
    shape = jax.ShapeDtypeStruct((2, 4, rows // 4, half), bf16)
    return pl.pallas_call(
        add_att_kernel,
        grid=(4,),
        in_specs=[ours] * 4 + [got] * 4,
        out_specs=[
            pl.BlockSpec((1, 4, rows // 4, half), lambda i: (jnp.minimum(i, 1), 0, 0, 0)),
            pl.BlockSpec((1, 4, rows // 4, half), lambda i: (jnp.maximum(i - 2, 0), 0, 0, 0)),
        ],
        cost_estimate=SMALL,
        out_shape=[shape, shape],
    )(*mine, *theirs)


def widen_t_kernel(in_ref, out_ref):
    out_ref[...] = in_ref[...].T.astype(f32)


def widen_t(value):
    rows, cols = value.shape
    step = 256
    return pl.pallas_call(
        widen_t_kernel,
        grid=(cols // step,),
        in_specs=[pl.BlockSpec((rows, step), lambda i: (0, i))],
        out_specs=pl.BlockSpec((step, rows), lambda i: (i, 0)),
        cost_estimate=SMALL,
        out_shape=jax.ShapeDtypeStruct((cols, rows), f32),
    )(value)


def last_att_kernel(at, mine_ref, other_ref, out_ref, qkv_ref):
    mine, other = mine_ref[0].astype(f32), other_ref[0].astype(f32)
    half = mine.shape[-1]
    left, right = jnp.where(at[0] == 0, mine, other), jnp.where(at[0] == 0, other, mine)
    out_ref[:, :half] = left[1]
    out_ref[:, half:] = right[1]
    for i, t in enumerate((0, 2, 3)):
        qkv_ref[i, :, :half] = left[t]
        qkv_ref[i, :, half:] = right[t]


def last_att(at, pieces, others):
    _, _, hd, half = pieces.shape
    block = lambda c: pl.BlockSpec((1, 4, hd, half), lambda p, at: (at[1 + 4 * c + p], 0, 0, 0))
    return pl.pallas_call(
        last_att_kernel,
        grid_spec=pltpu.PrefetchScalarGridSpec(
            num_scalar_prefetch=1,
            grid=(4,),
            in_specs=[block(0), block(1)],
            out_specs=[
                pl.BlockSpec((hd, 2 * half), lambda p, at: (p, 0)),
                pl.BlockSpec((3, hd, 2 * half), lambda p, at: (0, p, 0)),
            ],
        ),
        cost_estimate=SMALL,
        out_shape=[
            jax.ShapeDtypeStruct((4 * hd, 2 * half), f32),
            jax.ShapeDtypeStruct((3, 4 * hd, 2 * half), f32),
        ],
    )(at, pieces, others)


def swap(value, b):
    n = lax.axis_size("dp")
    return lax.ppermute(value, "dp", [(i, i ^ (1 << b)) for i in range(n)])


def hop(value, stage):
    n = lax.axis_size("dp")
    return lax.ppermute(
        value, "dp", [(i, i ^ (2 if (i & 1) == stage - 1 else 4)) for i in range(n)]
    )


def move(value, pairs):
    return lax.ppermute(value, "mp", pairs)


def shift(value, s):
    n = lax.axis_size("mp")
    return move(value, [(i, (i + s) % n) for i in range(n)])


def all_eight(value):
    n = lax.axis_size("dp")
    groups = None if n == 8 else [list(range(g, g + 8)) for g in range(0, n, 8)]
    return lax.all_gather(value, "dp", axis=0, axis_index_groups=groups)


def beyond(value):
    for b in range(3, lax.axis_size("dp").bit_length() - 1):
        value = value + swap(value, b)
    return value


def add(a, b):
    return (a.astype(f32) + b.astype(f32)).astype(bf16)


tie = lax.optimization_barrier


def norm_parts(rows):
    mean = jnp.mean(rows, axis=-1, keepdims=True)
    centred = rows - mean
    rstd = lax.rsqrt(jnp.mean(centred * centred, axis=-1, keepdims=True) + eps)
    return centred * rstd, rstd


def norm_back(grad, gain, xhat, rstd):
    scaled = grad * gain
    return rstd * (
        scaled
        - jnp.mean(scaled, axis=-1, keepdims=True)
        - xhat * jnp.mean(scaled * xhat, axis=-1, keepdims=True)
    )


def gelu_both(v):
    c, k = 0.7978845608028654, 0.044715
    t = jnp.tanh(c * (v + k * v * v * v))
    value = 0.5 * v * (1.0 + t)
    slope = 0.5 * (1.0 + t) + 0.5 * v * (1.0 - t * t) * (c * (1.0 + 3.0 * k * v * v))
    return value, slope


def body(
    tokens,
    segment_ids,
    norm1_gain,
    norm1_shift,
    qkv_weight,
    qv_bias,
    out_weight,
    out_bias,
    norm2_gain,
    norm2_shift,
    fc1_weight,
    fc1_bias,
    fc2_weight,
    fc2_bias,
    out_grad,
):
    rows, wide = tokens.shape
    half = wide // 2
    mp = lax.axis_size("mp")
    m = lax.axis_index("mp")
    d = lax.axis_index("dp") & 7
    core = d & 1
    ff_here = fc1_weight.shape[1]
    piece = ff_here // 8
    heads_here = qkv_weight.shape[2] // HD
    rest = mp - 1

    def slice_at(k):
        first = jnp.where((core ^ (k >> 2)) == 0, 2, 4)
        return d ^ ((k >> 2) + (k & 1) * first + ((k >> 1) & 1) * (6 - first))

    slices = slice_at(jnp.arange(8))
    place = slice_at(jnp.arange(4)) >> 1
    row = jnp.arange(mp * 8)
    other = jnp.maximum(row - 8, 0)
    shifts = jnp.where(row < 8, 0, other % rest + 1)
    lies_at = slice_at(jnp.where(row < 8, row, other // rest))
    ff_rows = (m + shifts) % mp * 8 + lies_at
    ff_from = (mp - shifts) % mp * 8 + lies_at
    head = jnp.arange(mp * heads_here)
    head_place = slice_at(head // mp) >> 1
    heads = (m + mp - head % mp) % mp * heads_here + head_place
    heads_from = head % mp * heads_here + head_place
    slopes = jnp.exp2(-8.0 * (heads + 1).astype(f32) / HEADS)

    def pick(table, at):
        n = table.shape[0]
        chosen = (at[:, None] == jnp.arange(n)[None, :]).astype(f32)
        return lax.dot(chosen, table, precision=lax.Precision.HIGHEST)

    near_rows = DOC_MOST - rows
    halo = DOC_MOST
    qv_own = jnp.transpose(qv_bias.reshape(2, heads_here, HD), (1, 0, 2))
    bias_own = jnp.concatenate([fc1_bias.reshape(8, piece), qv_own.reshape(heads_here, 2 * HD)])
    qkv_t = jnp.transpose(qkv_weight, (1, 2, 0))
    att_places = jnp.concatenate([core[None], place])
    (att_me,) = own_att(1, att_places, qkv_t, out_weight)
    att_me = att_me.reshape(4, HD, half)
    att_z = [shift(att_me, s) for s in range(1, mp)]
    bias_own, _ = tie((bias_own, att_me))
    bias_all = [bias_own] + [shift(bias_own, s) for s in range(1, mp)]
    me1, me2 = me_ff(slices, fc1_weight, fc2_weight)
    up = [(i, i + 1) for i in range(mp - 1)]
    tokens_late, _ = tie((tokens, att_me))
    halo1 = move(tokens_late[rows - near_rows :], up)
    fc1_b = pick(jnp.concatenate([v[:8] for v in bias_all]), ff_from).reshape(-1)
    qv_b = pick(jnp.concatenate([v[8:] for v in bias_all]), heads_from)
    q_bias, v_bias = qv_b[:, :HD].reshape(-1), qv_b[:, HD:].reshape(-1)
    seg_row = jnp.concatenate([jnp.full((1, halo), -1, jnp.int32), segment_ids], 1)
    segk = lax.dynamic_slice_in_dim(seg_row, m * rows, halo + rows, 1)
    segq = segk[:, halo:]
    segk = segk.reshape(halo + rows, 1)

    fc1_b, slices, att_places = tie((fc1_b, slices, att_places))
    own = own_att(2, att_places, qkv_t, out_weight)
    own1, own2 = own_ff(slices, fc1_weight, fc2_weight)
    small_ones = (fc1_b, q_bias, v_bias, segk, segq, slopes, own, own1, own2)
    att_z, small_ones = tie((att_z, small_ones))
    fc1_b, q_bias, v_bias, segk, segq, slopes, own, own1, own2 = small_ones
    att_x0 = jnp.stack(att_z)
    att_x1 = hop(att_x0, 1)
    att_x1, halo1 = tie((att_x1, halo1))
    halo2 = move(halo1, up)
    halo3 = move(tokens_late[: rows - near_rows], up)
    part0 = swap(att_x0, 0)
    att_y = hop(jnp.stack([att_x0, att_x1]), 2)
    part1 = swap(att_x1, 0)
    att_y, part0, part1, halo2, halo3, me1, me2 = tie(
        (att_y, part0, part1, halo2, halo3, me1, me2)
    )
    z1 = [shift(me1, mp - s) for s in range(1, mp)]
    ext = jnp.concatenate([halo2, halo3, halo1, tokens], 0).astype(f32)
    xhat_ext, rstd_ext = norm_parts(ext)
    norm1 = (xhat_ext * norm1_gain + norm1_shift).astype(bf16)
    col = [core * half, (1 - core) * half]

    def cols(value):
        return [lax.dynamic_slice_in_dim(value, at, half, 1) for at in col]

    n1 = cols(norm1)
    part_y = swap(att_y, 0)
    weights = join_att(
        core[None], (own[0], att_x0, att_x1, att_y), (own[1], part0, part1, part_y)
    )
    w_q, w_o, w_k, w_v = [w.reshape(HEADS * HD, wide) for w in weights]

    q = (dot(norm1[halo:], w_q, 1, 1) + q_bias).astype(bf16)
    k = dot(norm1, w_k, 1, 1).astype(bf16)
    v = (dot(norm1, w_v, 1, 1) + v_bias).astype(bf16)

    cut = rest * piece

    q, z1, me2 = tie((q, z1, me2))
    x0_1 = jnp.concatenate(z1)
    z2 = [shift(me2, mp - s) for s in range(1, mp)]
    x1_1 = hop(x0_1, 1)
    first = attend(0, slopes, segq, segk, q, k, v)
    first, x1_1, z2 = tie((first, x1_1, z2))
    x0_2 = jnp.concatenate(z2)
    z1 = jnp.concatenate([x0_1, x1_1])
    y1 = hop(z1, 2)
    x1_2 = hop(x0_2, 1)
    context, lse = attend(1, slopes, segq, segk, q, k, v, first)
    context, y1, x1_2 = tie((context, y1, x1_2))
    z2 = jnp.concatenate([x0_2, x1_2])
    y2 = hop(z2, 2)
    w1 = [z1, y1, swap(z1, 0), swap(y1, 0)]
    w2 = [z2, y2, swap(z2, 0), swap(y2, 0)]
    attention = dot(context, w_o, 1, 0)
    tokens_wide = tokens.astype(f32)
    resid = attention + out_bias + tokens_wide
    xhat2, rstd2 = norm_parts(resid)
    norm2 = (xhat2 * norm2_gain + norm2_shift).astype(bf16)

    pre, at = [dot(norm2, own1, 1, 0) + fc1_b[:ff_here]], ff_here
    for w in w1:
        pre.append(dot(norm2, w, 1, 1) + fc1_b[at : at + w.shape[0]])
        at += w.shape[0]
    hidden = [gelu_both(p)[0].astype(bf16) for p in pre]

    def partials(lhs, rhs):
        send = [lhs[3], lhs[4], lhs[0][:, 4 * piece :]]
        return [dot(v, rhs, 0, 0).astype(bf16) for v in send]

    def after_core(lhs, rhs, got):
        hi = jnp.concatenate(
            [
                (dot(lhs[2], rhs, 0, 0) + got[1].astype(f32)).astype(bf16),
                (dot(lhs[0][:, 2 * piece : 4 * piece], rhs, 0, 0) + got[2][2 * piece :].astype(f32)).astype(bf16),
            ]
        )
        lo = [
            (dot(lhs[1], rhs, 0, 0) + got[0].astype(f32)).astype(bf16),
            (dot(lhs[0][:, : 2 * piece], rhs, 0, 0) + got[2][: 2 * piece].astype(f32)).astype(bf16),
        ]
        return hi, lo

    def after_hop2(lo, got):
        send = jnp.concatenate([add(lo[0][cut:], got[cut : 2 * cut]), add(lo[1][piece:], got[2 * cut + piece :])])
        keep = [add(lo[0][:cut], got[:cut]), add(lo[1][:piece], got[2 * cut : 2 * cut + piece])]
        return send, keep

    def along_mp(keep, got):
        mine = add(keep[1], got[cut:])
        others = add(keep[0], got[:cut])
        blocks = jnp.concatenate([mine, others, mine, others])
        blocks = lax.dynamic_slice_in_dim(blocks, (mp - m) * piece, mp * piece, 0)
        return lax.psum_scatter(blocks, "mp", scatter_dimension=0, tiled=True)

    send2 = partials(hidden, out_grad)
    got2 = [swap(v, 0) for v in send2]
    mlp = sum(dot(h, w, 1, 0) for h, w in zip(hidden, [own2] + w2))
    result = (mlp + fc2_bias + resid).astype(bf16)
    grad_pre = [
        (dot(out_grad, w, 1, 1) * gelu_both(p)[1]).astype(bf16) for w, p in zip([own2] + w2, pre)
    ]
    send1 = partials(grad_pre, norm2)
    got1 = [swap(v, 0) for v in send1]
    hi2, lo2 = after_core(hidden, out_grad, got2)
    hop2_2 = hop(hi2, 2)

    grad_norm2 = dot(grad_pre[0], own1, 1, 1)
    grad_norm2 = grad_norm2 + sum(dot(g, w, 1, 0) for g, w in zip(grad_pre[1:], w1))
    out_grad_wide = out_grad.astype(f32)
    grad_resid = out_grad_wide + norm_back(grad_norm2, norm2_gain, xhat2, rstd2)
    hi1, lo1 = after_core(grad_pre, norm2, got1)
    grad_attention = grad_resid.astype(bf16)
    grad_att = cols(grad_attention)
    grad_context = dot(grad_attention, w_o, 1, 1).astype(bf16)

    grad_context, hi1, hi2 = tie((grad_context, hi1, hi2))
    hop2_1 = hop(hi1, 2)
    first = attend_back(0, slopes, segq, segk, q, k, v, grad_context, lse)
    first, hop2_2, result = tie((first, hop2_2, result))
    send2, keep2 = after_hop2(lo2, hop2_2)
    hop1_2 = hop(send2, 1)
    second = attend_back(1, slopes, segq, segk, q, k, v, grad_context, lse, first)
    second, hop2_1, hop1_2 = tie((second, hop2_1, hop1_2))
    send1, keep1 = after_hop2(lo1, hop2_1)
    hop1_1 = hop(send1, 1)
    sum2 = all_eight(beyond(along_mp(keep2, hop1_2)))
    grads = attend_back(2, slopes, segq, segk, q, k, v, grad_context, lse, second)
    (dq, dk, dv), hop1_1 = tie((grads, hop1_1))
    sum1 = along_mp(keep1, hop1_1)

    def weights_half(i):
        return [
            dot(dq, n1[i][halo:], 0, 0).astype(bf16),
            dot(context, grad_att[i], 0, 0).astype(bf16),
            dot(dk, n1[i], 0, 0).astype(bf16),
            dot(dv, n1[i], 0, 0).astype(bf16),
        ]

    grad_ext = dot(dk, w_k, 1, 0) + dot(dv, w_v, 1, 0)
    grad_halo = grad_ext[:halo].astype(bf16)
    grad_halo, dk, dv, dq = tie((grad_halo, dk, dv, dq))
    passed = move(grad_halo[:near_rows], [(i, i - 2) for i in range(2, mp)])
    theirs = weights_half(1)
    theirs, dk, dv, dq = tie((theirs, dk, dv, dq))
    theirs = [swap(v, 0) for v in theirs]
    mine = weights_half(0)
    att_hi, att_lo = add_att(mine, theirs)
    att_hi, grad_ext, dq_late = tie((att_hi, grad_ext, dq))
    att_got = hop(att_hi, 2)
    near = move(grad_halo[near_rows:], [(i, i - 1) for i in range(1, mp)])
    grad_norm1 = grad_ext[halo:] + dot(dq_late, w_q, 1, 0)
    att_got, grad_norm1, sum1 = tie((att_got, grad_norm1, sum1))
    sum1 = all_eight(beyond(sum1))
    att_hop1 = hop(add(att_lo[1], att_got[1]), 1)
    att_keep = add(att_lo[0], att_got[0])
    near = jnp.pad(passed.astype(f32), ((rows - near_rows, 0), (0, 0))) + near.astype(f32)
    grad_norm1 = grad_norm1 + near
    xhat1, rstd1 = xhat_ext[halo:], rstd_ext[halo:]
    in_grad = grad_resid + norm_back(grad_norm1, norm1_gain, xhat1, rstd1)
    ff_bias = jnp.concatenate([jnp.sum(g.astype(f32), axis=0) for g in grad_pre])
    ff_bias = ff_bias.reshape(mp * 8, piece)
    qv_sums = jnp.concatenate(
        [jnp.sum(g.astype(f32), axis=0).reshape(mp * heads_here, HD) for g in (dq, dv[:, :])], 1
    )

    def in_order(table, at):
        n = table.shape[0]
        chosen = (at[None, :] == jnp.arange(n)[:, None]).astype(f32)
        return lax.dot(chosen, table, precision=lax.Precision.HIGHEST)

    small = jnp.stack(
        [
            jnp.sum(grad_resid, axis=0),
            jnp.sum(grad_norm1 * xhat1, axis=0),
            jnp.sum(grad_norm1, axis=0),
            jnp.sum(grad_norm2 * xhat2, axis=0),
            jnp.sum(grad_norm2, axis=0),
            jnp.sum(out_grad_wide, axis=0),
        ]
    )
    n_small = wide // mp
    vectors = jnp.concatenate(
        [
            jnp.transpose(small.reshape(6, mp, n_small), (1, 0, 2)).reshape(mp, -1),
            in_order(qv_sums, heads).reshape(mp, -1),
            in_order(ff_bias, ff_rows).reshape(mp, -1),
        ],
        1,
    )
    grad_fc1 = widen_t(sum1.reshape(ff_here, wide))
    grad_fc2 = sum2.reshape(ff_here, wide).astype(f32)

    att_hop1, vectors = tie((att_hop1, vectors))
    att_keep = add(att_keep, att_hop1).reshape(4, mp, HD, half)
    att_z = [shift(att_keep[:, s], mp - s) for s in range(1, mp)]
    for bit in range(lax.axis_size("dp").bit_length() - 1):
        vectors = vectors + swap(vectors, bit)
    att_z, vectors, grad_fc2, in_grad = tie((att_z, vectors, grad_fc2, in_grad))
    att_sum = att_keep[:, 0].astype(f32)
    for got in att_z:
        att_sum = att_sum + got.astype(f32)
    att_sum = beyond(att_sum).astype(bf16)
    att_sum = jnp.stack([att_sum, hop(att_sum, 2)])
    att_sum, grad_fc1 = tie((jnp.stack([att_sum, hop(att_sum, 1)]), grad_fc1))
    att_sum = att_sum.reshape(4, 4, HD, half)
    number = row[:4]
    order = jnp.stack([number * 0, number * 0 + 1])
    lies = (slice_at(4 * order + ((number & 1) << 1) + (number >> 1))) >> 1
    at = jnp.sum(jnp.where(lies[:, None] == number[:, None], number[None, None], 0), axis=2)
    at = jnp.concatenate([core[None], at.reshape(-1)])
    grad_out, grad_qkv = last_att(at, att_sum, swap(att_sum, 0))
    grad_qkv = jnp.transpose(grad_qkv, (2, 0, 1))
    for bit in range(mp.bit_length() - 1):
        vectors = vectors + move(vectors, [(i, i ^ (1 << bit)) for i in range(mp)])
    total = lax.dynamic_index_in_dim(vectors, m, 0, False)
    six = total[: 6 * n_small].reshape(6, n_small)
    n_qv = heads_here * HD
    grad_qv = total[6 * n_small : 6 * n_small + 2 * n_qv].reshape(heads_here, 2, HD)
    grad_qv = jnp.transpose(grad_qv, (1, 0, 2)).reshape(2, n_qv)
    grad_fc1_bias = total[6 * n_small + 2 * n_qv :]
    return (
        result,
        in_grad,
        six[1],
        six[2],
        grad_qkv,
        grad_qv,
        grad_out,
        six[0],
        six[3],
        six[4],
        grad_fc1,
        grad_fc1_bias,
        grad_fc2,
        six[5],
    )


def solution(mesh):
    placed = (
        P(("dp", "mp"), None),
        P("dp", None),
        P(),
        P(),
        P(None, None, "mp"),
        P(None, "mp"),
        P("mp", None),
        P(),
        P(),
        P(),
        P(None, "mp"),
        P("mp"),
        P("mp", None),
        P(),
        P(("dp", "mp"), None),
    )
    return jax.shard_map(
        body,
        mesh=mesh,
        in_specs=placed,
        out_specs=(
            P(("dp", "mp"), None),
            P(("dp", "mp"), None),
            P("mp"),
            P("mp"),
            P(None, None, "mp"),
            P(None, "mp"),
            P("mp", None),
            P("mp"),
            P("mp"),
            P("mp"),
            P(None, "mp"),
            P("mp"),
            P("mp", None),
            P("mp"),
        ),
        check_vma=False,
    )
```

```python
import functools

import jax
import jax.numpy as jnp
from jax import lax
from jax.experimental import pallas as pl
from jax.experimental.pallas import tpu as pltpu
from jax.sharding import PartitionSpec as P

HEADS = 16
HD = 64
DOC_MOST = 768
QB = 256
MASKED = -1e12
SMALL = pl.CostEstimate(flops=1, bytes_accessed=1, transcendentals=1)
eps = 1e-05
f32 = jnp.float32
bf16 = jnp.bfloat16


def dot(a, b, ca, cb):
    return lax.dot_general(a, b, (((ca,), (cb,)), ((), ())), preferred_element_type=f32)


def fill_mask(segq_ref, segk_ref, mask_ref, window, halo):
    for i in range(mask_ref.shape[0]):
        key_at = lax.broadcasted_iota(jnp.int32, (window, QB), 0) + i * QB
        query_at = lax.broadcasted_iota(jnp.int32, (window, QB), 1) + (i * QB + halo)
        same = segk_ref[i * QB : i * QB + window, :] == segq_ref[:, i * QB : (i + 1) * QB]
        allowed = same & (key_at <= query_at)
        mask_ref[i] = jnp.where(allowed, (key_at - query_at).astype(f32), MASKED)


def halves(rows):
    lane = lax.broadcasted_iota(jnp.int32, (rows, 2 * HD), 1)
    return [lane < HD, lane >= HD]


def attend_kernel(halo, start, slopes, segq, segk, q_ref, k_ref, v_ref, *refs):
    o_ref, lse_ref, mask_ref = refs[-3:]
    window = halo + QB
    pair = start + pl.program_id(0)

    @pl.when(pair == start)
    def _():
        fill_mask(segq, segk, mask_ref, window, halo)

    v_t = v_ref[...].T
    pick = halves(QB)
    for i in range(mask_ref.shape[0]):
        rows = slice(i * QB, (i + 1) * QB)
        keys = slice(i * QB, i * QB + window)
        query = q_ref[rows, :] * jnp.asarray(HD**-0.5, bf16)
        key_rows = k_ref[keys, :]
        out = []
        for h in range(2):
            q_h = jnp.where(pick[h], query, jnp.zeros_like(query))
            scores = dot(key_rows, q_h, 1, 1) + slopes[2 * pair + h] * mask_ref[i]
            top = jnp.max(scores, axis=0, keepdims=True)
            expo = jnp.exp(scores - top)
            total = jnp.sum(expo, axis=0, keepdims=True)
            o_t = dot(v_t[:, keys], expo.astype(bf16), 1, 0)
            out.append(o_t[h * HD : (h + 1) * HD, :] * (1.0 / total))
            lse_ref[0, h : h + 1, rows] = top + jnp.log(total)
        o_ref[rows, :] = jnp.concatenate(out, axis=0).T.astype(bf16)


def attend_back_kernel(halo, start, slopes, segq, segk, q_ref, k_ref, v_ref, g_ref, lse_ref, *refs):
    dq_ref, dk_ref, dv_ref, mask_ref, dk_acc, dv_acc = refs[-6:]
    window = halo + QB
    pair = start + pl.program_id(0)

    @pl.when(pair == start)
    def _():
        fill_mask(segq, segk, mask_ref, window, halo)

    k_t = k_ref[...].T
    pick = halves(QB)
    dk_acc[...] = jnp.zeros_like(dk_acc)
    dv_acc[...] = jnp.zeros_like(dv_acc)
    for i in range(mask_ref.shape[0]):
        rows = slice(i * QB, (i + 1) * QB)
        keys = slice(i * QB, i * QB + window)
        query = q_ref[rows, :] * jnp.asarray(HD**-0.5, bf16)
        grad = g_ref[rows, :]
        key_rows = k_ref[keys, :]
        value_rows = v_ref[keys, :]
        out = []
        for h in range(2):
            q_h = jnp.where(pick[h], query, jnp.zeros_like(query))
            g_h = jnp.where(pick[h], grad, jnp.zeros_like(grad))
            scores = dot(key_rows, q_h, 1, 1) + slopes[2 * pair + h] * mask_ref[i]
            probs = jnp.exp(scores - lse_ref[0, h : h + 1, rows])
            grad_probs = dot(value_rows, g_h, 1, 1)
            delta = jnp.sum(probs * grad_probs, axis=0, keepdims=True)
            grad_scores = (probs * (grad_probs - delta)).astype(bf16)
            dv_acc[keys, :] += dot(probs.astype(bf16), g_h, 1, 0)
            dk_acc[keys, :] += dot(grad_scores, q_h, 1, 0)
            dq_t = dot(k_t[:, keys], grad_scores, 1, 0)
            out.append(dq_t[h * HD : (h + 1) * HD, :])
        dq_ref[rows, :] = (jnp.concatenate(out, axis=0).T * HD**-0.5).astype(bf16)
    dk_ref[...] = dk_acc[...].astype(bf16)
    dv_ref[...] = dv_acc[...].astype(bf16)


def attend(part, slopes, segq, segk, q, k, v, before=()):
    rows, wide = q.shape
    ext = k.shape[0]
    halo = ext - rows
    pairs = wide // (2 * HD)
    blocks = rows // QB
    start = part * (pairs // 2)
    col = lambda n: pl.BlockSpec((n, 2 * HD), lambda p: (0, p + start))
    return pl.pallas_call(
        functools.partial(attend_kernel, halo, start),
        grid=(pairs // 2,),
        in_specs=[
            pl.BlockSpec(memory_space=pltpu.SMEM),
            pl.BlockSpec((1, rows), lambda p: (0, 0)),
            pl.BlockSpec((ext, 1), lambda p: (0, 0)),
            col(rows),
            col(ext),
            col(ext),
        ]
        + [pl.BlockSpec(memory_space=pl.ANY)] * len(before),
        out_specs=[col(rows), pl.BlockSpec((1, 2, rows), lambda p: (p + start, 0, 0))],
        out_shape=[
            jax.ShapeDtypeStruct((rows, wide), bf16),
            jax.ShapeDtypeStruct((pairs, 2, rows), f32),
        ],
        input_output_aliases={6 + i: i for i in range(len(before))},
        scratch_shapes=[pltpu.VMEM((blocks, halo + QB, QB), f32)],
        compiler_params=pltpu.CompilerParams(vmem_limit_bytes=40 << 20),
        cost_estimate=SMALL,
    )(slopes, segq, segk, q, k, v, *before)


def attend_back(part, slopes, segq, segk, q, k, v, grad, lse, before=()):
    rows, wide = q.shape
    ext = k.shape[0]
    halo = ext - rows
    pairs = wide // (2 * HD)
    blocks = rows // QB
    start, stop = [pairs * i // 8 for i in (0, 3, 6, 8)][part : part + 2]
    col = lambda n: pl.BlockSpec((n, 2 * HD), lambda p: (0, p + start))
    return pl.pallas_call(
        functools.partial(attend_back_kernel, halo, start),
        grid=(stop - start,),
        in_specs=[
            pl.BlockSpec(memory_space=pltpu.SMEM),
            pl.BlockSpec((1, rows), lambda p: (0, 0)),
            pl.BlockSpec((ext, 1), lambda p: (0, 0)),
            col(rows),
            col(ext),
            col(ext),
            col(rows),
            pl.BlockSpec((1, 2, rows), lambda p: (p + start, 0, 0)),
        ]
        + [pl.BlockSpec(memory_space=pl.ANY)] * len(before),
        out_specs=[col(rows), col(ext), col(ext)],
        out_shape=[
            jax.ShapeDtypeStruct((rows, wide), bf16),
            jax.ShapeDtypeStruct((ext, wide), bf16),
            jax.ShapeDtypeStruct((ext, wide), bf16),
        ],
        input_output_aliases={8 + i: i for i in range(len(before))},
        scratch_shapes=[
            pltpu.VMEM((blocks, halo + QB, QB), f32),
            pltpu.VMEM((ext, 2 * HD), f32),
            pltpu.VMEM((ext, 2 * HD), f32),
        ],
        compiler_params=pltpu.CompilerParams(vmem_limit_bytes=48 << 20),
        cost_estimate=SMALL,
    )(slopes, segq, segk, q, k, v, grad, lse, *before)


def own_att_kernel(at, qkv_ref, out_ref, *own_refs):
    for t, rows in enumerate((qkv_ref[0], out_ref[...], qkv_ref[1], qkv_ref[2])):
        half = rows.shape[1] // 2
        left, right = rows[:, :half], rows[:, half:]
        own_refs[0][t, 0] = jnp.where(at[0] == 0, left, right)
        if len(own_refs) == 2:
            own_refs[1][t, 0] = jnp.where(at[0] == 0, right, left)


def own_att(halves, at, qkv_t, out_weight):
    wide = out_weight.shape[1]
    places = 4 if halves == 2 else 1
    return pl.pallas_call(
        own_att_kernel,
        grid_spec=pltpu.PrefetchScalarGridSpec(
            num_scalar_prefetch=1,
            grid=(places,),
            in_specs=[
                pl.BlockSpec((3, HD, wide), lambda p, at: (0, at[1 + p], 0)),
                pl.BlockSpec((HD, wide), lambda p, at: (at[1 + p], 0)),
            ],
            out_specs=[pl.BlockSpec((4, 1, HD, wide // 2), lambda p, at: (0, p, 0, 0))] * halves,
        ),
        cost_estimate=SMALL,
        out_shape=[jax.ShapeDtypeStruct((4, places, HD, wide // 2), bf16)] * halves,
    )(at, qkv_t, out_weight)


def me_ff_kernel(at, fc1_ref, fc2_ref, me1_ref, me2_ref):
    me1_ref[...] = fc1_ref[...].T
    me2_ref[...] = fc2_ref[...]


def me_ff(at, fc1_weight, fc2_weight):
    hidden, wide = fc2_weight.shape
    piece = hidden // 8
    return pl.pallas_call(
        me_ff_kernel,
        grid_spec=pltpu.PrefetchScalarGridSpec(
            num_scalar_prefetch=1,
            grid=(1,),
            in_specs=[
                pl.BlockSpec((wide, piece), lambda i, at: (0, at[0])),
                pl.BlockSpec((piece, wide), lambda i, at: (at[0], 0)),
            ],
            out_specs=[pl.BlockSpec((piece, wide), lambda i, at: (0, 0))] * 2,
        ),
        cost_estimate=SMALL,
        out_shape=[jax.ShapeDtypeStruct((piece, wide), bf16)] * 2,
    )(at, fc1_weight, fc2_weight)


def own_ff_kernel(at, fc1_ref, fc2_ref, o1_ref, o2_ref):
    o1_ref[...] = fc1_ref[...]
    o2_ref[...] = fc2_ref[...]


def own_ff(at, fc1_weight, fc2_weight):
    hidden, wide = fc2_weight.shape
    piece = hidden // 8
    return pl.pallas_call(
        own_ff_kernel,
        grid_spec=pltpu.PrefetchScalarGridSpec(
            num_scalar_prefetch=1,
            grid=(8,),
            in_specs=[
                pl.BlockSpec((wide, piece), lambda i, at: (0, at[i])),
                pl.BlockSpec((piece, wide), lambda i, at: (at[i], 0)),
            ],
            out_specs=[
                pl.BlockSpec((wide, piece), lambda i, at: (0, i)),
                pl.BlockSpec((piece, wide), lambda i, at: (i, 0)),
            ],
        ),
        cost_estimate=SMALL,
        out_shape=[
            jax.ShapeDtypeStruct((wide, hidden), bf16),
            jax.ShapeDtypeStruct((hidden, wide), bf16),
        ],
    )(at, fc1_weight, fc2_weight)


def join_att_kernel(core, *refs):
    mine, other, out_refs = refs[:4], refs[4:8], refs[8:]
    left_mine = core[0] == 0

    def places(t, own_ref, x0_ref, x1_ref, y_ref, exchanged):
        hops = (y_ref[0, :, t], x1_ref[:, t]) if exchanged else (x1_ref[:, t], y_ref[0, :, t])
        return own_ref[t], (x0_ref[:, t], *hops, y_ref[1, :, t])

    for t, out_ref in enumerate(out_refs):
        own_a, rest_a = places(t, *mine, False)
        own_b, rest_b = places(t, *other, True)
        half = own_a.shape[-1]
        out_ref[:, 0, :, :half] = jnp.where(left_mine, own_a, own_b)
        out_ref[:, 0, :, half:] = jnp.where(left_mine, own_b, own_a)
        for place, (a, b) in enumerate(zip(rest_a, rest_b)):
            out_ref[place, 1:, :, :half] = jnp.where(left_mine, a, b)
            out_ref[place, 1:, :, half:] = jnp.where(left_mine, b, a)


def join_att(core, mine, other):
    rest, _, hd, half = mine[1].shape
    step = hd // 4
    one = pl.BlockSpec((rest, 4, step, half), lambda i: (0, 0, i, 0))
    side = [
        pl.BlockSpec((4, 4, step, half), lambda i: (0, 0, i, 0)),
        one,
        one,
        pl.BlockSpec((2, rest, 4, step, half), lambda i: (0, 0, 0, i, 0)),
    ]
    return pl.pallas_call(
        join_att_kernel,
        grid=(4,),
        in_specs=[pl.BlockSpec(memory_space=pltpu.SMEM)] + side + side,
        out_specs=[pl.BlockSpec((4, rest + 1, step, 2 * half), lambda i: (0, 0, i, 0))] * 4,
        cost_estimate=SMALL,
        out_shape=[jax.ShapeDtypeStruct((4, rest + 1, hd, 2 * half), bf16)] * 4,
    )(core, *mine, *other)


def add_att_kernel(*refs):
    mine, theirs, (hi_ref, lo_ref) = refs[:4], refs[4:8], refs[8:]
    i = pl.program_id(0)
    for t in range(4):
        total = (mine[t][...].astype(f32) + theirs[t][...].astype(f32)).astype(bf16)

        @pl.when(i < 2)
        def _():
            hi_ref[0, t] = total

        @pl.when(i >= 2)
        def _():
            lo_ref[0, t] = total


def add_att(mine, theirs):
    rows, half = mine[0].shape
    ours = pl.BlockSpec((rows // 4, half), lambda i: ((i + 2) % 4, 0))
    got = pl.BlockSpec((rows // 4, half), lambda i: ((2 * i + 1) % 4 - i // 2, 0))
    shape = jax.ShapeDtypeStruct((2, 4, rows // 4, half), bf16)
    return pl.pallas_call(
        add_att_kernel,
        grid=(4,),
        in_specs=[ours] * 4 + [got] * 4,
        out_specs=[
            pl.BlockSpec((1, 4, rows // 4, half), lambda i: (jnp.minimum(i, 1), 0, 0, 0)),
            pl.BlockSpec((1, 4, rows // 4, half), lambda i: (jnp.maximum(i - 2, 0), 0, 0, 0)),
        ],
        cost_estimate=SMALL,
        out_shape=[shape, shape],
    )(*mine, *theirs)


def widen_t_kernel(in_ref, out_ref):
    out_ref[...] = in_ref[...].T.astype(f32)


def widen_t(value):
    rows, cols = value.shape
    step = 256
    return pl.pallas_call(
        widen_t_kernel,
        grid=(cols // step,),
        in_specs=[pl.BlockSpec((rows, step), lambda i: (0, i))],
        out_specs=pl.BlockSpec((step, rows), lambda i: (i, 0)),
        cost_estimate=SMALL,
        out_shape=jax.ShapeDtypeStruct((cols, rows), f32),
    )(value)


def last_att_kernel(at, mine_ref, other_ref, out_ref, qkv_ref):
    mine, other = mine_ref[0].astype(f32), other_ref[0].astype(f32)
    half = mine.shape[-1]
    left, right = jnp.where(at[0] == 0, mine, other), jnp.where(at[0] == 0, other, mine)
    out_ref[:, :half] = left[1]
    out_ref[:, half:] = right[1]
    for i, t in enumerate((0, 2, 3)):
        qkv_ref[i, :, :half] = left[t]
        qkv_ref[i, :, half:] = right[t]


def last_att(at, pieces, others):
    _, _, hd, half = pieces.shape
    block = lambda c: pl.BlockSpec((1, 4, hd, half), lambda p, at: (at[1 + 4 * c + p], 0, 0, 0))
    return pl.pallas_call(
        last_att_kernel,
        grid_spec=pltpu.PrefetchScalarGridSpec(
            num_scalar_prefetch=1,
            grid=(4,),
            in_specs=[block(0), block(1)],
            out_specs=[
                pl.BlockSpec((hd, 2 * half), lambda p, at: (p, 0)),
                pl.BlockSpec((3, hd, 2 * half), lambda p, at: (0, p, 0)),
            ],
        ),
        cost_estimate=SMALL,
        out_shape=[
            jax.ShapeDtypeStruct((4 * hd, 2 * half), f32),
            jax.ShapeDtypeStruct((3, 4 * hd, 2 * half), f32),
        ],
    )(at, pieces, others)


def swap(value, b):
    n = lax.axis_size("dp")
    return lax.ppermute(value, "dp", [(i, i ^ (1 << b)) for i in range(n)])


def hop(value, stage):
    n = lax.axis_size("dp")
    return lax.ppermute(
        value, "dp", [(i, i ^ (2 if (i & 1) == stage - 1 else 4)) for i in range(n)]
    )


def move(value, pairs):
    return lax.ppermute(value, "mp", pairs)


def shift(value, s):
    n = lax.axis_size("mp")
    return move(value, [(i, (i + s) % n) for i in range(n)])


def all_eight(value):
    n = lax.axis_size("dp")
    groups = None if n == 8 else [list(range(g, g + 8)) for g in range(0, n, 8)]
    return lax.all_gather(value, "dp", axis=0, axis_index_groups=groups)


def beyond(value):
    for b in range(3, lax.axis_size("dp").bit_length() - 1):
        value = value + swap(value, b)
    return value


def add(a, b):
    return (a.astype(f32) + b.astype(f32)).astype(bf16)


tie = lax.optimization_barrier


def norm_parts(rows):
    mean = jnp.mean(rows, axis=-1, keepdims=True)
    centred = rows - mean
    rstd = lax.rsqrt(jnp.mean(centred * centred, axis=-1, keepdims=True) + eps)
    return centred * rstd, rstd


def norm_back(grad, gain, xhat, rstd):
    scaled = grad * gain
    return rstd * (
        scaled
        - jnp.mean(scaled, axis=-1, keepdims=True)
        - xhat * jnp.mean(scaled * xhat, axis=-1, keepdims=True)
    )


def gelu_both(v):
    c, k = 0.7978845608028654, 0.044715
    t = jnp.tanh(c * (v + k * v * v * v))
    value = 0.5 * v * (1.0 + t)
    slope = 0.5 * (1.0 + t) + 0.5 * v * (1.0 - t * t) * (c * (1.0 + 3.0 * k * v * v))
    return value, slope


def body(
    tokens,
    segment_ids,
    norm1_gain,
    norm1_shift,
    qkv_weight,
    qv_bias,
    out_weight,
    out_bias,
    norm2_gain,
    norm2_shift,
    fc1_weight,
    fc1_bias,
    fc2_weight,
    fc2_bias,
    out_grad,
):
    rows, wide = tokens.shape
    half = wide // 2
    mp = lax.axis_size("mp")
    m = lax.axis_index("mp")
    d = lax.axis_index("dp") & 7
    core = d & 1
    ff_here = fc1_weight.shape[1]
    piece = ff_here // 8
    heads_here = qkv_weight.shape[2] // HD
    rest = mp - 1

    def slice_at(k):
        first = jnp.where((core ^ (k >> 2)) == 0, 2, 4)
        return d ^ ((k >> 2) + (k & 1) * first + ((k >> 1) & 1) * (6 - first))

    slices = slice_at(jnp.arange(8))
    place = slice_at(jnp.arange(4)) >> 1
    row = jnp.arange(mp * 8)
    other = jnp.maximum(row - 8, 0)
    shifts = jnp.where(row < 8, 0, other % rest + 1)
    lies_at = slice_at(jnp.where(row < 8, row, other // rest))
    ff_rows = (m + shifts) % mp * 8 + lies_at
    ff_from = (mp - shifts) % mp * 8 + lies_at
    head = jnp.arange(mp * heads_here)
    head_place = slice_at(head // mp) >> 1
    heads = (m + mp - head % mp) % mp * heads_here + head_place
    heads_from = head % mp * heads_here + head_place
    slopes = jnp.exp2(-8.0 * (heads + 1).astype(f32) / HEADS)

    def pick(table, at):
        n = table.shape[0]
        chosen = (at[:, None] == jnp.arange(n)[None, :]).astype(f32)
        return lax.dot(chosen, table, precision=lax.Precision.HIGHEST)

    near_rows = DOC_MOST - rows
    halo = DOC_MOST
    qv_own = jnp.transpose(qv_bias.reshape(2, heads_here, HD), (1, 0, 2))
    bias_own = jnp.concatenate([fc1_bias.reshape(8, piece), qv_own.reshape(heads_here, 2 * HD)])
    qkv_t = jnp.transpose(qkv_weight, (1, 2, 0))
    att_places = jnp.concatenate([core[None], place])
    (att_me,) = own_att(1, att_places, qkv_t, out_weight)
    att_me = att_me.reshape(4, HD, half)
    att_z = [shift(att_me, s) for s in range(1, mp)]
    bias_own, _ = tie((bias_own, att_me))
    bias_all = [bias_own] + [shift(bias_own, s) for s in range(1, mp)]
    me1, me2 = me_ff(slices, fc1_weight, fc2_weight)
    up = [(i, i + 1) for i in range(mp - 1)]
    tokens_late, _ = tie((tokens, att_me))
    halo1 = move(tokens_late, up)
    fc1_b = pick(jnp.concatenate([v[:8] for v in bias_all]), ff_from).reshape(-1)
    qv_b = pick(jnp.concatenate([v[8:] for v in bias_all]), heads_from)
    q_bias, v_bias = qv_b[:, :HD].reshape(-1), qv_b[:, HD:].reshape(-1)
    seg_row = jnp.concatenate([jnp.full((1, halo), -1, jnp.int32), segment_ids], 1)
    segk = lax.dynamic_slice_in_dim(seg_row, m * rows, halo + rows, 1)
    segq = segk[:, halo:]
    segk = segk.reshape(halo + rows, 1)

    fc1_b, slices, att_places = tie((fc1_b, slices, att_places))
    own = own_att(2, att_places, qkv_t, out_weight)
    own1, own2 = own_ff(slices, fc1_weight, fc2_weight)
    small_ones = (fc1_b, q_bias, v_bias, segk, segq, slopes, own, own1, own2)
    att_z, small_ones = tie((att_z, small_ones))
    fc1_b, q_bias, v_bias, segk, segq, slopes, own, own1, own2 = small_ones
    att_x0 = jnp.stack(att_z)
    att_x1 = hop(att_x0, 1)
    att_x1, halo1 = tie((att_x1, halo1))
    halo2 = move(halo1[rows - near_rows :], up)
    part0 = swap(att_x0, 0)
    att_y = hop(jnp.stack([att_x0, att_x1]), 2)
    part1 = swap(att_x1, 0)
    att_y, part0, part1, halo2, me1, me2 = tie((att_y, part0, part1, halo2, me1, me2))
    z1 = [shift(me1, mp - s) for s in range(1, mp)]
    ext = jnp.concatenate([halo2, halo1, tokens], 0).astype(f32)
    xhat_ext, rstd_ext = norm_parts(ext)
    norm1 = (xhat_ext * norm1_gain + norm1_shift).astype(bf16)
    col = [core * half, (1 - core) * half]

    def cols(value):
        return [lax.dynamic_slice_in_dim(value, at, half, 1) for at in col]

    n1 = cols(norm1)
    part_y = swap(att_y, 0)
    weights = join_att(
        core[None], (own[0], att_x0, att_x1, att_y), (own[1], part0, part1, part_y)
    )
    w_q, w_o, w_k, w_v = [w.reshape(HEADS * HD, wide) for w in weights]

    q = (dot(norm1[halo:], w_q, 1, 1) + q_bias).astype(bf16)
    k = dot(norm1, w_k, 1, 1).astype(bf16)
    v = (dot(norm1, w_v, 1, 1) + v_bias).astype(bf16)

    cut = rest * piece

    q, z1, me2 = tie((q, z1, me2))
    x0_1 = jnp.concatenate(z1)
    z2 = [shift(me2, mp - s) for s in range(1, mp)]
    x1_1 = hop(x0_1, 1)
    first = attend(0, slopes, segq, segk, q, k, v)
    first, x1_1, z2 = tie((first, x1_1, z2))
    x0_2 = jnp.concatenate(z2)
    z1 = jnp.concatenate([x0_1, x1_1])
    y1 = hop(z1, 2)
    x1_2 = hop(x0_2, 1)
    context, lse = attend(1, slopes, segq, segk, q, k, v, first)
    context, y1, x1_2 = tie((context, y1, x1_2))
    z2 = jnp.concatenate([x0_2, x1_2])
    y2 = hop(z2, 2)
    w1 = [z1, y1, swap(z1, 0), swap(y1, 0)]
    w2 = [z2, y2, swap(z2, 0), swap(y2, 0)]
    attention = dot(context, w_o, 1, 0)
    tokens_wide = tokens.astype(f32)
    resid = attention + out_bias + tokens_wide
    xhat2, rstd2 = norm_parts(resid)
    norm2 = (xhat2 * norm2_gain + norm2_shift).astype(bf16)

    pre, at = [dot(norm2, own1, 1, 0) + fc1_b[:ff_here]], ff_here
    for w in w1:
        pre.append(dot(norm2, w, 1, 1) + fc1_b[at : at + w.shape[0]])
        at += w.shape[0]
    hidden = [gelu_both(p)[0].astype(bf16) for p in pre]

    def partials(lhs, rhs):
        send = [lhs[3], lhs[4], lhs[0][:, 4 * piece :]]
        return [dot(v, rhs, 0, 0).astype(bf16) for v in send]

    def after_core(lhs, rhs, got):
        hi = jnp.concatenate(
            [
                (dot(lhs[2], rhs, 0, 0) + got[1].astype(f32)).astype(bf16),
                (dot(lhs[0][:, 2 * piece : 4 * piece], rhs, 0, 0) + got[2][2 * piece :].astype(f32)).astype(bf16),
            ]
        )
        lo = [
            (dot(lhs[1], rhs, 0, 0) + got[0].astype(f32)).astype(bf16),
            (dot(lhs[0][:, : 2 * piece], rhs, 0, 0) + got[2][: 2 * piece].astype(f32)).astype(bf16),
        ]
        return hi, lo

    def after_hop2(lo, got):
        send = jnp.concatenate([add(lo[0][cut:], got[cut : 2 * cut]), add(lo[1][piece:], got[2 * cut + piece :])])
        keep = [add(lo[0][:cut], got[:cut]), add(lo[1][:piece], got[2 * cut : 2 * cut + piece])]
        return send, keep

    def along_mp(keep, got):
        mine = add(keep[1], got[cut:])
        others = add(keep[0], got[:cut])
        blocks = jnp.concatenate([mine, others, mine, others])
        blocks = lax.dynamic_slice_in_dim(blocks, (mp - m) * piece, mp * piece, 0)
        return lax.psum_scatter(blocks, "mp", scatter_dimension=0, tiled=True)

    send2 = partials(hidden, out_grad)
    got2 = [swap(v, 0) for v in send2]
    mlp = sum(dot(h, w, 1, 0) for h, w in zip(hidden, [own2] + w2))
    result = (mlp + fc2_bias + resid).astype(bf16)
    grad_pre = [
        (dot(out_grad, w, 1, 1) * gelu_both(p)[1]).astype(bf16) for w, p in zip([own2] + w2, pre)
    ]
    send1 = partials(grad_pre, norm2)
    got1 = [swap(v, 0) for v in send1]
    hi2, lo2 = after_core(hidden, out_grad, got2)
    hop2_2 = hop(hi2, 2)

    grad_norm2 = dot(grad_pre[0], own1, 1, 1)
    grad_norm2 = grad_norm2 + sum(dot(g, w, 1, 0) for g, w in zip(grad_pre[1:], w1))
    out_grad_wide = out_grad.astype(f32)
    grad_resid = out_grad_wide + norm_back(grad_norm2, norm2_gain, xhat2, rstd2)
    hi1, lo1 = after_core(grad_pre, norm2, got1)
    grad_attention = grad_resid.astype(bf16)
    grad_att = cols(grad_attention)
    grad_context = dot(grad_attention, w_o, 1, 1).astype(bf16)

    grad_context, hi1, hi2 = tie((grad_context, hi1, hi2))
    hop2_1 = hop(hi1, 2)
    first = attend_back(0, slopes, segq, segk, q, k, v, grad_context, lse)
    first, hop2_2, result = tie((first, hop2_2, result))
    send2, keep2 = after_hop2(lo2, hop2_2)
    hop1_2 = hop(send2, 1)
    second = attend_back(1, slopes, segq, segk, q, k, v, grad_context, lse, first)
    second, hop2_1, hop1_2 = tie((second, hop2_1, hop1_2))
    send1, keep1 = after_hop2(lo1, hop2_1)
    hop1_1 = hop(send1, 1)
    sum2 = all_eight(beyond(along_mp(keep2, hop1_2)))
    grads = attend_back(2, slopes, segq, segk, q, k, v, grad_context, lse, second)
    (dq, dk, dv), hop1_1 = tie((grads, hop1_1))
    sum1 = along_mp(keep1, hop1_1)

    def weights_half(i):
        return [
            dot(dq, n1[i][halo:], 0, 0).astype(bf16),
            dot(context, grad_att[i], 0, 0).astype(bf16),
            dot(dk, n1[i], 0, 0).astype(bf16),
            dot(dv, n1[i], 0, 0).astype(bf16),
        ]

    grad_ext = dot(dk, w_k, 1, 0) + dot(dv, w_v, 1, 0)
    grad_halo = grad_ext[:halo].astype(bf16)
    grad_halo, dk, dv, dq = tie((grad_halo, dk, dv, dq))
    passed = move(grad_halo[:near_rows], [(i, i - 2) for i in range(2, mp)])
    theirs = weights_half(1)
    theirs, dk, dv, dq = tie((theirs, dk, dv, dq))
    theirs = [swap(v, 0) for v in theirs]
    mine = weights_half(0)
    att_hi, att_lo = add_att(mine, theirs)
    att_hi, grad_ext, dq_late = tie((att_hi, grad_ext, dq))
    att_got = hop(att_hi, 2)
    near = move(grad_halo[near_rows:], [(i, i - 1) for i in range(1, mp)])
    grad_norm1 = grad_ext[halo:] + dot(dq_late, w_q, 1, 0)
    att_got, grad_norm1, sum1 = tie((att_got, grad_norm1, sum1))
    sum1 = all_eight(beyond(sum1))
    att_hop1 = hop(add(att_lo[1], att_got[1]), 1)
    att_keep = add(att_lo[0], att_got[0])
    near = jnp.pad(passed.astype(f32), ((rows - near_rows, 0), (0, 0))) + near.astype(f32)
    grad_norm1 = grad_norm1 + near
    xhat1, rstd1 = xhat_ext[halo:], rstd_ext[halo:]
    in_grad = grad_resid + norm_back(grad_norm1, norm1_gain, xhat1, rstd1)
    ff_bias = jnp.concatenate([jnp.sum(g.astype(f32), axis=0) for g in grad_pre])
    ff_bias = ff_bias.reshape(mp * 8, piece)
    qv_sums = jnp.concatenate(
        [jnp.sum(g.astype(f32), axis=0).reshape(mp * heads_here, HD) for g in (dq, dv[:, :])], 1
    )

    def in_order(table, at):
        n = table.shape[0]
        chosen = (at[None, :] == jnp.arange(n)[:, None]).astype(f32)
        return lax.dot(chosen, table, precision=lax.Precision.HIGHEST)

    small = jnp.stack(
        [
            jnp.sum(grad_resid, axis=0),
            jnp.sum(grad_norm1 * xhat1, axis=0),
            jnp.sum(grad_norm1, axis=0),
            jnp.sum(grad_norm2 * xhat2, axis=0),
            jnp.sum(grad_norm2, axis=0),
            jnp.sum(out_grad_wide, axis=0),
        ]
    )
    n_small = wide // mp
    vectors = jnp.concatenate(
        [
            jnp.transpose(small.reshape(6, mp, n_small), (1, 0, 2)).reshape(mp, -1),
            in_order(qv_sums, heads).reshape(mp, -1),
            in_order(ff_bias, ff_rows).reshape(mp, -1),
        ],
        1,
    )
    grad_fc1 = widen_t(sum1.reshape(ff_here, wide))
    grad_fc2 = sum2.reshape(ff_here, wide).astype(f32)

    att_hop1, vectors = tie((att_hop1, vectors))
    att_keep = add(att_keep, att_hop1).reshape(4, mp, HD, half)
    att_z = [shift(att_keep[:, s], mp - s) for s in range(1, mp)]
    for bit in range(lax.axis_size("dp").bit_length() - 1):
        vectors = vectors + swap(vectors, bit)
    att_z, vectors, grad_fc2, in_grad = tie((att_z, vectors, grad_fc2, in_grad))
    att_sum = att_keep[:, 0].astype(f32)
    for got in att_z:
        att_sum = att_sum + got.astype(f32)
    att_sum = beyond(att_sum).astype(bf16)
    att_sum = jnp.stack([att_sum, hop(att_sum, 2)])
    att_sum, grad_fc1 = tie((jnp.stack([att_sum, hop(att_sum, 1)]), grad_fc1))
    att_sum = att_sum.reshape(4, 4, HD, half)
    number = row[:4]
    order = jnp.stack([number * 0, number * 0 + 1])
    lies = (slice_at(4 * order + ((number & 1) << 1) + (number >> 1))) >> 1
    at = jnp.sum(jnp.where(lies[:, None] == number[:, None], number[None, None], 0), axis=2)
    at = jnp.concatenate([core[None], at.reshape(-1)])
    grad_out, grad_qkv = last_att(at, att_sum, swap(att_sum, 0))
    grad_qkv = jnp.transpose(grad_qkv, (2, 0, 1))
    for bit in range(mp.bit_length() - 1):
        vectors = vectors + move(vectors, [(i, i ^ (1 << bit)) for i in range(mp)])
    total = lax.dynamic_index_in_dim(vectors, m, 0, False)
    six = total[: 6 * n_small].reshape(6, n_small)
    n_qv = heads_here * HD
    grad_qv = total[6 * n_small : 6 * n_small + 2 * n_qv].reshape(heads_here, 2, HD)
    grad_qv = jnp.transpose(grad_qv, (1, 0, 2)).reshape(2, n_qv)
    grad_fc1_bias = total[6 * n_small + 2 * n_qv :]
    return (
        result,
        in_grad,
        six[1],
        six[2],
        grad_qkv,
        grad_qv,
        grad_out,
        six[0],
        six[3],
        six[4],
        grad_fc1,
        grad_fc1_bias,
        grad_fc2,
        six[5],
    )


def solution(mesh):
    placed = (
        P(("dp", "mp"), None),
        P("dp", None),
        P(),
        P(),
        P(None, None, "mp"),
        P(None, "mp"),
        P("mp", None),
        P(),
        P(),
        P(),
        P(None, "mp"),
        P("mp"),
        P("mp", None),
        P(),
        P(("dp", "mp"), None),
    )
    return jax.shard_map(
        body,
        mesh=mesh,
        in_specs=placed,
        out_specs=(
            P(("dp", "mp"), None),
            P(("dp", "mp"), None),
            P("mp"),
            P("mp"),
            P(None, None, "mp"),
            P(None, "mp"),
            P("mp", None),
            P("mp"),
            P("mp"),
            P("mp"),
            P(None, "mp"),
            P("mp"),
            P("mp", None),
            P("mp"),
        ),
        check_vma=False,
    )
```
